256 devices in a mesh: gy: 16 (over z, core), gz: 16 (over y, x).
Axes of the slice: x: 4, y: 4, z: 8, core: 2. Of those that a mesh axis runs over, the one named last changes fastest.
Arguments:
- displacement: float32 [3, 128, 128, 256], P(None, 'gy', 'gz'), may hold values from -0.08 to 0.08
- load: float32 [3, 128, 128, 256], P(None, 'gy', 'gz'), may hold values from -6 to 6
- occupancy: int32 [128, 128, 256], P('gy', 'gz'), may hold values 0 or 1
- voxel_muscle_group: int32 [128, 128, 256], P('gy', 'gz'), may hold values from 0 to 31
- activation: float32 [32], replicated, may hold values from 0.2 to 2
Outputs:
- adjoint: float32 [3, 128, 128, 256], P(None, 'gy', 'gz')
- muscle_grad: float32 [32], replicated
The draws below stay inside these ranges and needn't reach their ends.
All inputs are finite; a program needn't handle non-finite values. No bound on the sum of `occupancy` on one device may be relied on, other than what follows from the above.
Results may differ from the reference program's by a relative error of at most 0.0003.
Values sent between devices are 32-bit elements; how exact they have to be, the bound alone decides.
No kernel may reach another device: no remote copies, remote signals or barrier semaphores. Data moves between devices by JAX's collectives and lax.ppermute only.
A program may use at most 64 MiB of HBM per device.

```python
import math
from functools import reduce
import jax
import jax.numpy as jnp
from jax import lax

CY = 8
NX = 256
MUSCLES = 32
ITERS = 4
NY = 128
NZ = 128
N_GY = 16


def place_ends(values, rng, smallest, largest):
    shape = values.shape
    spot = [jax.random.randint(jax.random.fold_in(rng, axis), (), 0, shape[axis]) for axis in range(len(shape))]
    values = values.at[tuple(spot)].set(smallest)
    longest = shape.index(max(shape))
    spot[longest] = (spot[longest] + 1) % shape[longest]
    return values.at[tuple(spot)].set(largest)


def block_levels(key, extent, pieces, low, largest):
    factor_of = 1.0
    for axis_at, blocks in pieces:
        heights = jax.random.uniform(jax.random.fold_in(jax.random.fold_in(key, 6), axis_at), (blocks,), jnp.float32, low / len(pieces), largest / len(pieces))
        factor_of = factor_of * jnp.repeat(jnp.exp(heights), extent[axis_at] // blocks).reshape((-1,) + (1,) * (len(extent) - 1 - axis_at))
    return factor_of


def scatter_about(key, shape, spread, bound, split=(), kind=jnp.bfloat16):
    factor_of = block_levels(key, shape, split, -0.22, 0.18) if split else 1.0
    drawn = jax.random.normal(key, shape, jnp.float32) * spread * factor_of
    return jnp.minimum(jnp.maximum(drawn, -bound), bound).astype(kind)


def setup_inputs(seed: int = 0) -> dict:
    streams_of = jax.random.split(jax.random.key(seed), 6)
    return {
        "displacement": jnp.clip(jax.random.uniform(streams_of[0], (3, NY, NZ, NX), jnp.float32, -0.08, 0.08) * block_levels(streams_of[0], (3, NY, NZ, NX), ((1, 16), (2, 16)), -0.4, 0.0), -0.08, 0.08),
        "load": scatter_about(streams_of[1], (3, NY, NZ, NX), 1.0, 6.0, ((1, 16), (2, 16)), jnp.float32),
        "occupancy": place_ends((jax.random.randint(streams_of[2], (NY, NZ, NX), 0, 4) < 3).astype(jnp.int32), jax.random.fold_in(streams_of[2], 1), 0, 1),
        "voxel_muscle_group": place_ends(jax.random.randint(streams_of[3], (NY, NZ, NX), 0, MUSCLES), jax.random.fold_in(streams_of[3], 1), 0, MUSCLES - 1).astype(jnp.int32),
        "activation": jnp.clip(jnp.exp(jax.random.uniform(streams_of[4], (MUSCLES,), jnp.float32, math.log(0.2), math.log(2.0))), 0.2, 2.0),
    }


shear_modulus = 1.0
lame_first = 4.0
mass_scale = 0.05

def accumulate_every(summand_terms):
    return reduce(lambda earlier_part, later_part: earlier_part + later_part, summand_terms)

def forward_x(values):
    return jnp.concatenate([values[..., 1:], jnp.zeros_like(values[..., :1])], axis=-1)

def backward_x(values):
    return jnp.concatenate([jnp.zeros_like(values[..., :1]), values[..., :-1]], axis=-1)

def element_gradient(extended):
    leading = forward_x(extended)
    paired = extended + leading
    slopes = leading - extended
    summed_z = paired[:, :, :-1] + paired[:, :, 1:]
    differ_z = paired[:, :, 1:] - paired[:, :, :-1]
    slopes_z = slopes[:, :, :-1] + slopes[:, :, 1:]
    grad_x = 0.25 * (slopes_z[:, :-1] + slopes_z[:, 1:])
    grad_y = 0.25 * (summed_z[:, 1:] - summed_z[:, :-1])
    grad_z = 0.25 * (differ_z[:, :-1] + differ_z[:, 1:])
    return [[grad_x[comp_idx], grad_y[comp_idx], grad_z[comp_idx]] for comp_idx in range(extended.shape[0])]

def element_terms(state_ext):
    deform = element_gradient(state_ext[:3])
    deform = [[deform[row_index][col_idx] + (1.0 if row_index == col_idx else 0.0) for col_idx in range(3)] for row_index in range(3)]
    cofactor = [[deform[(row_index + 1) % 3][(col_idx + 1) % 3] * deform[(row_index + 2) % 3][(col_idx + 2) % 3] - deform[(row_index + 1) % 3][(col_idx + 2) % 3] * deform[(row_index + 2) % 3][(col_idx + 1) % 3] for col_idx in range(3)] for row_index in range(3)]
    volume_ratio = accumulate_every([deform[0][col_idx] * cofactor[0][col_idx] for col_idx in range(3)])
    inverse_t = [[cofactor[row_index][col_idx] / volume_ratio for col_idx in range(3)] for row_index in range(3)]
    shear_term = shear_modulus - lame_first * jnp.log(volume_ratio)
    occupied = state_ext[3, :-1, :-1]
    muscle_act = state_ext[4, :-1, :-1]
    fiber = [deform[row_index][0] for row_index in range(3)]
    return (inverse_t, shear_term, occupied, muscle_act, fiber)

def stress_rate(grad_field, terms):
    inverse_t, shear_term, occupied, muscle_act, fiber = terms
    trace_term = accumulate_every([inverse_t[row_index][col_idx] * grad_field[row_index][col_idx] for row_index in range(3) for col_idx in range(3)])
    mixed = [[accumulate_every([grad_field[inner_idx][mid_idx] * inverse_t[inner_idx][col_idx] for inner_idx in range(3)]) for col_idx in range(3)] for mid_idx in range(3)]
    rotated = [[accumulate_every([inverse_t[row_index][mid_idx] * mixed[mid_idx][col_idx] for mid_idx in range(3)]) for col_idx in range(3)] for row_index in range(3)]
    scaled = 0.25 * occupied
    result = []
    for row_index in range(3):
        line = []
        for col_idx in range(3):
            value = shear_modulus * grad_field[row_index][col_idx] + shear_term * rotated[row_index][col_idx] + lame_first * trace_term * inverse_t[row_index][col_idx]
            if col_idx == 0:
                value = value + muscle_act * grad_field[row_index][0]
            line.append(scaled * value)
        result.append(line)
    return result

def node_forces(rate):
    forces = []
    for row_index in range(3):
        along_x = backward_x(rate[row_index][0]) - rate[row_index][0]
        across_y = rate[row_index][1] + backward_x(rate[row_index][1])
        across_z = rate[row_index][2] + backward_x(rate[row_index][2])
        combined = along_x[:, :-1] + along_x[:, 1:] + (across_z[:, :-1] - across_z[:, 1:])
        stacked_y = across_y[:, :-1] + across_y[:, 1:]
        forces.append(combined[:-1] + combined[1:] + (stacked_y[:-1] - stacked_y[1:]))
    return jnp.stack(forces)

def apply_operator(extended, terms):
    return node_forces(stress_rate(element_gradient(extended), terms))

def muscle_sums(extended, terms, muscle_ids, levels):
    grad_field = element_gradient(extended)
    fiber = terms[4]
    occupied = terms[2]
    work = accumulate_every([fiber[row_index][1:, 1:] * grad_field[row_index][0][1:, 1:] for row_index in range(3)]) * occupied[1:, 1:]
    return lax.optimization_barrier(jnp.sum(jnp.where(muscle_ids[None] == levels[:, None, None, None], work[None], jnp.zeros((), work.dtype)), axis=(1, 2, 3)))

def pad_field(field):
    return jnp.pad(field, ((0, 0), (1, 1), (1, 1), (0, 0)))

def reference(displacement, load, occupancy, voxel_muscle_group, activation):

    def add_level(level, total):
        return total + jnp.where(voxel_muscle_group == level, activation[level], jnp.zeros((), activation.dtype))
    muscle_act = lax.fori_loop(0, MUSCLES, add_level, jnp.zeros(occupancy.shape, activation.dtype))
    state = jnp.concatenate([displacement, occupancy.astype(displacement.dtype)[None], muscle_act.astype(displacement.dtype)[None]], axis=0)
    state_pad = pad_field(state)
    blocks = jnp.arange(N_GY, dtype=jnp.int32)

    def operate(field):
        padded = pad_field(field)

        def one_block(block):
            start = (block * CY).astype(jnp.int32)
            extended = lax.dynamic_slice_in_dim(padded, start, CY + 2, 1)
            terms = element_terms(lax.dynamic_slice_in_dim(state_pad, start, CY + 2, 1))
            return apply_operator(extended, terms)
        forces = lax.map(one_block, blocks)
        forces = jnp.transpose(forces, (1, 0, 2, 3, 4)).reshape(field.shape)
        return mass_scale * field + forces
    solution = jnp.zeros_like(load)
    residual, direction = (load, load)
    norm_now = jnp.sum(residual * residual)
    for step in range(ITERS):
        image = operate(direction)
        alpha = norm_now / jnp.sum(direction * image)
        solution = solution + alpha * direction
        residual = residual - alpha * image
        norm_next = jnp.sum(residual * residual)
        direction = residual + norm_next / norm_now * direction
        norm_now = norm_next
    adjoint_padded = pad_field(solution)
    levels = jnp.arange(MUSCLES, dtype=jnp.int32)

    def block_sums(block):
        start = (block * CY).astype(jnp.int32)
        extended = lax.dynamic_slice_in_dim(adjoint_padded, start, CY + 2, 1)
        terms = element_terms(lax.dynamic_slice_in_dim(state_pad, start, CY + 2, 1))
        return muscle_sums(extended, terms, lax.dynamic_slice_in_dim(voxel_muscle_group, start, CY, 0), levels)
    total = lax.optimization_barrier(jnp.sum(lax.map(block_sums, blocks), axis=0))
    muscle_grad = -(1.0 / math.sqrt(NX * NY * NZ / MUSCLES)) * total
    return (solution, muscle_grad)
```

```python
import functools
import math

import jax
import jax.numpy as jnp
from jax import lax
from jax.experimental import pallas as pl
from jax.experimental.pallas import tpu as pltpu
from jax.sharding import PartitionSpec as P

SHEAR = 1.0
LAME = 4.0
MASS = 0.05

LOW, HIGH = 3, 4
SIGMA = 16.0
SHIFTS = (0.0, 9.95, 1.95)
NB = 4
LANES = 128
SUB = 8
TERMS = 15
QUADS = tuple((zt, h) for zt in range(2) for h in range(2))


class Tile:
    def __init__(self):
        self.lane = lax.broadcasted_iota(jnp.int32, (SUB, LANES), 1)
        self.sub = lax.broadcasted_iota(jnp.int32, (SUB, LANES), 0)
        self.last_lane = self.lane == LANES - 1
        self.first_lane = self.lane == 0
        self.last_sub = self.sub == SUB - 1
        self.first_sub = self.sub == 0

    def xup(self, v):
        out = {}
        for zt in range(2):
            r0 = pltpu.roll(v[zt, 0], LANES - 1, 1)
            r1 = pltpu.roll(v[zt, 1], LANES - 1, 1)
            out[zt, 0] = jnp.where(self.last_lane, r1, r0)
            out[zt, 1] = jnp.where(self.last_lane, 0.0, r1)
        return out

    def xdown(self, v):
        out = {}
        for zt in range(2):
            r0 = pltpu.roll(v[zt, 0], 1, 1)
            r1 = pltpu.roll(v[zt, 1], 1, 1)
            out[zt, 0] = jnp.where(self.first_lane, 0.0, r0)
            out[zt, 1] = jnp.where(self.first_lane, r0, r1)
        return out

    def zup(self, v):
        out = {}
        for h in range(2):
            r0 = pltpu.roll(v[0, h], SUB - 1, 0)
            r1 = pltpu.roll(v[1, h], SUB - 1, 0)
            out[0, h] = jnp.where(self.last_sub, r1, r0)
            out[1, h] = r1
        return out

    def zdown(self, v):
        out = {}
        for h in range(2):
            r0 = pltpu.roll(v[0, h], 1, 0)
            r1 = pltpu.roll(v[1, h], 1, 0)
            out[0, h] = r0
            out[1, h] = jnp.where(self.first_sub, r0, r1)
        return out

    def own(self, v):
        out = []
        for h in range(2):
            r0 = pltpu.roll(v[0, h], SUB - LOW, 0)
            r1 = pltpu.roll(v[1, h], SUB - LOW, 0)
            out.append(jnp.where(self.sub < SUB - LOW, r0, r1))
        return out


def get(ref, *index):
    return {
        (zt, h): ref[(*index, pl.ds(SUB * zt, SUB), pl.ds(LANES * h, LANES))] for zt, h in QUADS
    }


def put(ref, value, *index):
    for zt, h in QUADS:
        ref[(*index, pl.ds(SUB * zt, SUB), pl.ds(LANES * h, LANES))] = value[zt, h]


def add(a, b):
    return {k: a[k] + b[k] for k in QUADS}


def sub(a, b):
    return {k: a[k] - b[k] for k in QUADS}


def raw_gradient(tile, ref, lead, q):
    result = []
    for comp in range(3):
        here = get(ref, *lead, comp, q)
        above = get(ref, *lead, comp, q + 1)
        both, step = add(here, above), sub(above, here)
        both_x, step_x = tile.xup(both), tile.xup(step)
        wide, slope, rise = add(both, both_x), sub(both_x, both), add(step, step_x)
        result.append(
            (
                add(slope, tile.zup(slope)),
                add(rise, tile.zup(rise)),
                sub(tile.zup(wide), wide),
            )
        )
    return result


def row_terms(tile, ext, terms, q):
    grad = raw_gradient(tile, ext, (), q)
    occ, level = get(ext, 6, q), get(ext, 7, q)
    for k in QUADS:
        deform = [
            [0.25 * grad[r][c][k] + (1.0 if r == c else 0.0) for c in range(3)] for r in range(3)
        ]
        cof = [
            [
                deform[(r + 1) % 3][(c + 1) % 3] * deform[(r + 2) % 3][(c + 2) % 3]
                - deform[(r + 1) % 3][(c + 2) % 3] * deform[(r + 2) % 3][(c + 1) % 3]
                for c in range(3)
            ]
            for r in range(3)
        ]
        volume = deform[0][0] * cof[0][0] + deform[0][1] * cof[0][1] + deform[0][2] * cof[0][2]
        inverse = 1.0 / volume
        scaled = occ[k] * (1.0 / (16.0 * SIGMA))
        values = [cof[r][c] * inverse for r in range(3) for c in range(3)]
        values.append(scaled * (SHEAR - LAME * jnp.log(volume)))
        values.append(scaled)
        values.append(scaled * (SHEAR + level[k]))
        quarter = 0.25 * occ[k]
        values += [quarter * deform[r][0] for r in range(3)]
        zt, h = k
        for i, value in enumerate(values):
            terms[i, q, pl.ds(SUB * zt, SUB), pl.ds(LANES * h, LANES)] = value


def row_rate(grad, terms, works, step, q, need_work=True):
    rate = [[{} for _ in range(3)] for _ in range(3)]
    for k in QUADS:
        zt, h = k

        def term(i):
            return terms[i, q, pl.ds(SUB * zt, SUB), pl.ds(LANES * h, LANES)]

        g = [[grad[r][c][k] for c in range(3)] for r in range(3)]
        inv_t = [[term(3 * r + c) for c in range(3)] for r in range(3)]
        shear, occ, fibre = term(9), term(10), term(11)
        pulled = [
            [
                inv_t[0][a] * g[0][b] + inv_t[1][a] * g[1][b] + inv_t[2][a] * g[2][b]
                for b in range(3)
            ]
            for a in range(3)
        ]
        spread = (LAME * occ) * (pulled[0][0] + pulled[1][1] + pulled[2][2])
        z = [
            [shear * pulled[c][m] + (spread if c == m else 0.0) for c in range(3)]
            for m in range(3)
        ]
        for r in range(3):
            for c in range(3):
                rate[r][c][k] = (
                    (fibre if c == 0 else occ) * g[r][c]
                    + inv_t[r][0] * z[0][c]
                    + inv_t[r][1] * z[1][c]
                    + inv_t[r][2] * z[2][c]
                )
        if need_work:
            works[step, q, pl.ds(SUB * zt, SUB), pl.ds(LANES * h, LANES)] = (
                term(12) * g[0][0] + term(13) * g[1][0] + term(14) * g[2][0]
            )
    return rate


def row_force(tile, before, rate, comp):
    p = {k: before[comp, 0][k] + rate[comp][0][k] for k in QUADS}
    a = {k: before[comp, 1][k] - rate[comp][1][k] for k in QUADS}
    b = {k: before[comp, 2][k] + rate[comp][2][k] for k in QUADS}
    along = add(p, tile.zdown(p))
    across = add(tile.zdown(add(a, b)), sub(a, b))
    return add(tile.xdown(add(along, across)), sub(across, along))


def krylov_kernel(
    axes, e_ref, ylo_ref, yhi_ref, load_ref, group_ref, sums_ref, basis_ref, ext, fields, terms, last, works, table
):
    rows = load_ref.shape[1]
    tile = Tile()
    top_y = jnp.where(lax.axis_index(axes[0]) == lax.axis_size(axes[0]) - 1, LOW + rows, -1)
    top_z = jnp.where(lax.axis_index(axes[1]) == lax.axis_size(axes[1]) - 1, LOW + rows, -1)
    keep_z = {
        (zt, h): jnp.where(tile.sub + SUB * zt == top_z, 0.0, 1.0) for zt, h in QUADS
    }
    count = LOW + rows + HIGH
    blank = jnp.zeros((SUB, ext.shape[-1]), jnp.float32)

    def assemble(c, carry):
        for q in range(count):
            ext[c, q, pl.ds(SUB, SUB), :] = blank
            if q < LOW:
                ext[c, q, pl.ds(0, count), :] = ylo_ref[c, q]
            elif q < LOW + rows:
                ext[c, q, pl.ds(0, count), :] = e_ref[c, q - LOW]
            else:
                ext[c, q, pl.ds(0, count), :] = yhi_ref[c, q - LOW - rows]
        return carry

    lax.fori_loop(0, ext.shape[0], assemble, 0)

    def remember(rate):
        for r in range(3):
            for c in range(3):
                put(last, rate[r][c], 3 * r + c)

    for step in range(3):
        source, lead = (ext, ()) if step == 0 else (fields, (step - 1,))
        base = 3 if step == 0 else 0

        class View:
            pass

        def grad_of(q, source=source, lead=lead, base=base):
            result = []
            for comp in range(3):
                here = get(source, *lead, base + comp, q)
                above = get(source, *lead, base + comp, q + 1)
                both, rise0 = add(here, above), sub(above, here)
                both_x, rise_x = tile.xup(both), tile.xup(rise0)
                wide, slope, rise = add(both, both_x), sub(both_x, both), add(rise0, rise_x)
                result.append(
                    (
                        add(slope, tile.zup(slope)),
                        add(rise, tile.zup(rise)),
                        sub(tile.zup(wide), wide),
                    )
                )
            return result

        def rate_of(q, step=step, grad_of=grad_of):
            if step == 0:
                row_terms(tile, ext, terms, q)
            return row_rate(grad_of(q), terms, works, step, q)

        def body(q, carry, step=step, rate_of=rate_of, source=source, lead=lead, base=base):
            rate = rate_of(q)
            before = {(r, c): get(last, 3 * r + c) for r in range(3) for c in range(3)}
            keep_y = jnp.where(q == top_y, 0.0, 1.0)
            for comp in range(3):
                force = row_force(tile, before, rate, comp)
                if SHIFTS[step] != 0.0:
                    here = get(source, *lead, base + comp, q)
                    force = {k: force[k] - (SHIFTS[step] / SIGMA) * here[k] for k in QUADS}
                force = {k: force[k] * (keep_z[k] * keep_y) for k in QUADS}
                put(fields, force, step, comp, q)
            remember(rate)
            return carry

        remember(rate_of(step))
        lax.fori_loop(step + 1, count - 1 - step, body, 0)

    inside = {
        (zt, h): (tile.sub + SUB * zt >= LOW) & (tile.sub + SUB * zt < LOW + rows)
        for zt, h in QUADS
    }
    zero = jnp.zeros((SUB, LANES), jnp.float32)
    pairs = [(i, j) for i in range(NB) for j in range(i, NB)]

    def finish(y, acc):
        acc = list(acc)
        q = y + LOW
        grad = []
        for comp in range(3):
            here = get(fields, 2, comp, q)
            above = get(fields, 2, comp, q + 1)
            both, rise0 = add(here, above), sub(above, here)
            both_x, rise_x = tile.xup(both), tile.xup(rise0)
            wide, slope, rise = add(both, both_x), sub(both_x, both), add(rise0, rise_x)
            grad.append(
                (
                    add(slope, tile.zup(slope)),
                    add(rise, tile.zup(rise)),
                    sub(tile.zup(wide), wide),
                )
            )
        rate = row_rate(grad, terms, works, 3, q)
        for k in QUADS:
            energy = zero
            for r in range(3):
                for c in range(3):
                    energy = energy + rate[r][c][k] * grad[r][c][k]
            acc[-1] = acc[-1] + jnp.where(inside[k], energy, 0.0)
        for comp in range(3):
            vectors = [[load_ref[comp, y, :, pl.ds(LANES * h, LANES)] for h in range(2)]]
            for step in range(3):
                value = tile.own(get(fields, step, comp, q))
                for h in range(2):
                    basis_ref[step, comp, y, :, pl.ds(LANES * h, LANES)] = value[h]
                vectors.append(value)
            for n, (i, j) in enumerate(pairs):
                acc[n] = acc[n] + (
                    vectors[i][0] * vectors[j][0] + vectors[i][1] * vectors[j][1]
                )
        return tuple(acc)

    acc = lax.fori_loop(0, rows, finish, tuple(zero for _ in range(len(pairs) + 1)))
    table[...] = jnp.zeros_like(table)
    muscles = (table.shape[0] // 2) // NB
    for n, value in enumerate(acc):
        table[pl.ds(NB * muscles + n, 1), :] = jnp.sum(value, axis=0, keepdims=True)

    def compact(y, carry):
        for step in range(NB):
            value = tile.own(get(works, step, y + LOW))
            for h in range(2):
                works[step, y, pl.ds(0, SUB), pl.ds(LANES * h, LANES)] = value[h]
        return carry

    lax.fori_loop(0, rows, compact, 0)

    def muscle(m, carry):
        total = [zero] * NB
        for y in range(rows):
            for h in range(2):
                mine = group_ref[y, :, pl.ds(LANES * h, LANES)] == m
                for step in range(NB):
                    total[step] = total[step] + jnp.where(
                        mine, works[step, y, pl.ds(0, SUB), pl.ds(LANES * h, LANES)], 0.0
                    )
        for step in range(NB):
            table[pl.ds(step * muscles + m, 1), :] = jnp.sum(total[step], axis=0, keepdims=True)
        return carry

    lax.fori_loop(0, muscles, muscle, 0)
    row = lax.dot_general(
        jnp.ones((SUB, LANES), jnp.float32),
        table[...],
        (((1,), (1,)), ((), ())),
        precision=lax.Precision.HIGHEST,
        preferred_element_type=jnp.float32,
    )
    for i in range(sums_ref.shape[0] // SUB):
        sums_ref[pl.ds(SUB * i, SUB), :] = row


def combine_kernel(muscles, scale, sums_ref, load_ref, basis_ref, x_ref, grad_ref):
    total = jnp.sum(sums_ref[...], axis=0, keepdims=True)
    at = NB * muscles
    pairs = [(i, j) for i in range(NB) for j in range(i, NB)]
    gram = {}
    for n, (i, j) in enumerate(pairs):
        gram[i, j] = gram[j, i] = total[:, at + n : at + n + 1]
    energy = total[:, at + len(pairs) : at + len(pairs) + 1]
    shifts = [MASS + s for s in SHIFTS]
    form = {}
    for j in range(NB - 1):
        for i in range(j + 1):
            form[i, j] = form[j, i] = SIGMA * gram[i, j + 1] + shifts[j] * gram[i, j]
    last = NB - 1
    for i in range(last):
        form[i, last] = form[last, i] = SIGMA * gram[i + 1, last] + shifts[i] * gram[i, last]
    form[last, last] = SIGMA * energy + MASS * gram[last, last]

    def quadratic(matrix, v):
        parts = []
        for i in range(NB):
            if v[i] is None:
                continue
            inner = [matrix[i, j] * v[j] for j in range(NB) if v[j] is not None]
            parts.append(v[i] * functools.reduce(lambda s, t: s + t, inner))
        return functools.reduce(lambda s, t: s + t, parts)

    one = jnp.ones((1, 1), jnp.float32)
    x = [None] * NB
    residual = [one] + [None] * (NB - 1)
    direction = list(residual)
    norm = gram[0, 0]

    def axpy(a, u, v):
        out = []
        for s, t in zip(u, v):
            if s is None:
                out.append(t)
            elif t is None:
                out.append(a * s)
            else:
                out.append(t + a * s)
        return out

    for step in range(NB):
        alpha = norm / quadratic(form, direction)
        x = axpy(alpha, direction, x)
        if step == NB - 1:
            break
        image = [None] * NB
        for i in range(NB - 1):
            if direction[i] is not None:
                up = SIGMA * direction[i]
                same = shifts[i] * direction[i]
                image[i] = same if image[i] is None else image[i] + same
                image[i + 1] = up if image[i + 1] is None else image[i + 1] + up
        residual = axpy(-alpha, image, residual)
        new = quadratic(gram, residual)
        direction = axpy(new / norm, direction, residual)
        norm = new

    grad = None
    for k in range(NB):
        part = x[k] * total[:, k * muscles : (k + 1) * muscles]
        grad = part if grad is None else grad + part
    grad_ref[...] = -scale * grad

    width = load_ref.shape[-1]
    coef = [jnp.broadcast_to(x[k], (SUB, width)) for k in range(NB)]

    def row(y, carry):
        for comp in range(3):
            value = coef[0] * load_ref[comp, y]
            for k in range(1, NB):
                value = value + coef[k] * basis_ref[k - 1, comp, y]
            x_ref[comp, y] = value
        return carry

    lax.fori_loop(0, load_ref.shape[1], row, 0)


def shift(shard, axis, by):
    length = lax.axis_size(axis)
    return lax.ppermute(
        shard, axis, [(i, i + by) for i in range(length) if 0 <= i + by < length]
    )


def per_device(displacement, load, occupancy, voxel_muscle_group, activation):
    rows, cols, depth = occupancy.shape
    muscles = activation.shape[0]
    levels = jnp.arange(muscles, dtype=jnp.int32)
    level = jnp.sum(
        jnp.where(
            voxel_muscle_group[None] == levels[:, None, None, None],
            activation[:, None, None, None],
            0.0,
        ),
        axis=0,
    )
    block = jnp.concatenate(
        [displacement, load, occupancy.astype(jnp.float32)[None], level[None]], axis=0
    )
    zlo = shift(block[:, :, cols - LOW :], "gz", 1)
    zhi = shift(block[:, :, :HIGH], "gz", -1)
    e = jnp.concatenate([zlo, block, zhi], axis=2)
    ylo = shift(e[:, rows - LOW :], "gy", 1)
    yhi = shift(e[:, :HIGH], "gy", -1)

    devices = lax.axis_size("gy") * lax.axis_size("gz")
    count = LOW + rows + HIGH
    vmem = pl.BlockSpec(memory_space=pltpu.VMEM)
    sums, basis = pl.pallas_call(
        functools.partial(krylov_kernel, ("gy", "gz")),
        out_shape=(
            jax.ShapeDtypeStruct((devices, 2 * NB * muscles), jnp.float32),
            jax.ShapeDtypeStruct((NB - 1, 3, rows, cols, depth), jnp.float32),
        ),
        in_specs=[vmem] * 5,
        out_specs=(vmem, vmem),
        scratch_shapes=[
            pltpu.VMEM((8, count, 2 * SUB, depth), jnp.float32),
            pltpu.VMEM((NB - 1, 3, count, 2 * SUB, depth), jnp.float32),
            pltpu.VMEM((TERMS, count - 1, 2 * SUB, depth), jnp.float32),
            pltpu.VMEM((9, 2 * SUB, depth), jnp.float32),
            pltpu.VMEM((NB, count - 1, 2 * SUB, depth), jnp.float32),
            pltpu.VMEM((2 * NB * muscles, LANES), jnp.float32),
        ],
        compiler_params=pltpu.CompilerParams(vmem_limit_bytes=48 << 20),
        name="krylov",
    )(e, ylo, yhi, load, voxel_muscle_group)

    every = lax.all_to_all(sums, ("gy", "gz"), 0, 0, tiled=True)

    cells = depth * rows * lax.axis_size("gy") * cols * lax.axis_size("gz")
    scale = 1.0 / math.sqrt(cells / muscles)
    adjoint, muscle_grad = pl.pallas_call(
        functools.partial(combine_kernel, muscles, scale),
        out_shape=(
            jax.ShapeDtypeStruct(load.shape, jnp.float32),
            jax.ShapeDtypeStruct((1, muscles), jnp.float32),
        ),
        in_specs=[vmem] * 3,
        out_specs=(vmem, vmem),
        compiler_params=pltpu.CompilerParams(vmem_limit_bytes=32 << 20),
        name="combine",
    )(every, load, basis)
    return adjoint, muscle_grad.reshape(muscles)


def solution(mesh):
    placed = (
        P(None, "gy", "gz", None),
        P(None, "gy", "gz", None),
        P("gy", "gz", None),
        P("gy", "gz", None),
        P(),
    )
    return jax.shard_map(
        per_device,
        mesh=mesh,
        in_specs=placed,
        out_specs=(P(None, "gy", "gz", None), P()),
        check_vma=False,
    )
```

```python
import functools
import math

import jax
import jax.numpy as jnp
from jax import lax
from jax.experimental import pallas as pl
from jax.experimental.pallas import tpu as pltpu
from jax.sharding import PartitionSpec as P

SHEAR = 1.0
LAME = 4.0
MASS = 0.05

LOW, HIGH = 3, 4
SIGMA = 16.0
SHIFTS = (0.0, 9.95, 1.95)
NB = 4
LANES = 128
SUB = 8
CHANNELS = 8
TERMS = 15
ALL = tuple((zt, h) for zt in range(2) for h in range(2))
OWN = ((0, 0), (0, 1))
VMEM = pl.BlockSpec(memory_space=pltpu.VMEM)
SMEM = pl.BlockSpec(memory_space=pltpu.SMEM)


class Shifts:
    def __init__(self):
        lane = lax.broadcasted_iota(jnp.int32, (SUB, LANES), 1)
        self.sub = lax.broadcasted_iota(jnp.int32, (SUB, LANES), 0)
        self.last_lane = lane == LANES - 1
        self.first_lane = lane == 0
        self.last_sub = self.sub == SUB - 1
        self.first_sub = self.sub == 0

    def xup(self, v):
        out = {}
        for zt in {zt for zt, _ in v}:
            r0 = pltpu.roll(v[zt, 0], LANES - 1, 1)
            r1 = pltpu.roll(v[zt, 1], LANES - 1, 1)
            out[zt, 0] = jnp.where(self.last_lane, r1, r0)
            out[zt, 1] = jnp.where(self.last_lane, 0.0, r1)
        return out

    def xdown(self, v):
        out = {}
        for zt in {zt for zt, _ in v}:
            r0 = pltpu.roll(v[zt, 0], 1, 1)
            r1 = pltpu.roll(v[zt, 1], 1, 1)
            out[zt, 0] = jnp.where(self.first_lane, 0.0, r0)
            out[zt, 1] = jnp.where(self.first_lane, r0, r1)
        return out

    def zup(self, v, keys):
        out = {}
        for h in range(2):
            r0 = pltpu.roll(v[0, h], SUB - 1, 0)
            r1 = pltpu.roll(v[1, h], SUB - 1, 0)
            out[0, h] = jnp.where(self.last_sub, r1, r0)
            if (1, h) in keys:
                out[1, h] = jnp.where(self.last_sub, r0, r1)
        return out

    def zdown(self, v):
        out = {}
        for h in range(2):
            r0 = pltpu.roll(v[0, h], 1, 0)
            r1 = pltpu.roll(v[1, h], 1, 0)
            out[0, h] = jnp.where(self.first_sub, r1, r0)
            out[1, h] = jnp.where(self.first_sub, r0, r1)
        return out


def part(k):
    return pl.ds(SUB * k[0], SUB), pl.ds(LANES * k[1], LANES)


def get(ref, *index):
    return {k: ref[(*index, *part(k))] for k in ALL}


def put(ref, value, *index):
    for k in value:
        ref[(*index, *part(k))] = value[k]


def add(a, b):
    return {k: a[k] + b[k] for k in a}


def sub(a, b):
    return {k: a[k] - b[k] for k in a}


def raw_gradient(sh, read, q, keys=ALL):
    result = []
    for comp in range(3):
        here, above = read(comp, q), read(comp, q + 1)
        both, step = add(here, above), sub(above, here)
        both_x, step_x = sh.xup(both), sh.xup(step)
        wide, slope, rise = add(both, both_x), sub(both_x, both), add(step, step_x)
        result.append(
            tuple(
                {k: up[k] + sign * v[k] if sign > 0 else up[k] - v[k] for k in keys}
                for v, up, sign in (
                    (slope, sh.zup(slope, keys), 1),
                    (rise, sh.zup(rise, keys), 1),
                    (wide, sh.zup(wide, keys), -1),
                )
            )
        )
    return result


def row_terms(sh, ext, terms, q):
    grad = raw_gradient(sh, lambda comp, at: get(ext, comp, at), q)
    for k in ALL:
        occ, level = ext[(6, q, *part(k))], ext[(7, q, *part(k))]
        deform = [
            [0.25 * grad[r][c][k] + (1.0 if r == c else 0.0) for c in range(3)] for r in range(3)
        ]
        cof = [
            [
                deform[(r + 1) % 3][(c + 1) % 3] * deform[(r + 2) % 3][(c + 2) % 3]
                - deform[(r + 1) % 3][(c + 2) % 3] * deform[(r + 2) % 3][(c + 1) % 3]
                for c in range(3)
            ]
            for r in range(3)
        ]
        volume = deform[0][0] * cof[0][0] + deform[0][1] * cof[0][1] + deform[0][2] * cof[0][2]
        inverse = 1.0 / volume
        scaled = occ * (1.0 / (16.0 * SIGMA))
        values = [cof[r][c] * inverse for r in range(3) for c in range(3)]
        values.append(scaled * (SHEAR - LAME * jnp.log(volume)))
        values.append(scaled)
        values.append(scaled * (SHEAR + level))
        quarter = 0.25 * occ
        values += [quarter * deform[r][0] for r in range(3)]
        for i, value in enumerate(values):
            terms[(i, q, *part(k))] = value


def row_rate(grad, terms, works, step, q, keys=ALL):
    rate = [[{} for _ in range(3)] for _ in range(3)]
    for k in keys:

        def term(i):
            return terms[(i, q, *part(k))]

        g = [[grad[r][c][k] for c in range(3)] for r in range(3)]
        inv_t = [[term(3 * r + c) for c in range(3)] for r in range(3)]
        shear, occ, fibre = term(9), term(10), term(11)
        pulled = [
            [
                inv_t[0][a] * g[0][b] + inv_t[1][a] * g[1][b] + inv_t[2][a] * g[2][b]
                for b in range(3)
            ]
            for a in range(3)
        ]
        spread = (LAME * occ) * (pulled[0][0] + pulled[1][1] + pulled[2][2])
        z = [
            [shear * pulled[c][m] + spread if c == m else shear * pulled[c][m] for c in range(3)]
            for m in range(3)
        ]
        for r in range(3):
            for c in range(3):
                rate[r][c][k] = (
                    (fibre if c == 0 else occ) * g[r][c]
                    + inv_t[r][0] * z[0][c]
                    + inv_t[r][1] * z[1][c]
                    + inv_t[r][2] * z[2][c]
                )
        if k in OWN:
            works[(step, q, *part(k))] = (
                term(12) * g[0][0] + term(13) * g[1][0] + term(14) * g[2][0]
            )
    return rate


def row_force(sh, before, rate, comp):
    p = add(before[comp][0], rate[comp][0])
    a = sub(before[comp][1], rate[comp][1])
    b = add(before[comp][2], rate[comp][2])
    along = add(p, sh.zdown(p))
    across = add(sh.zdown(add(a, b)), sub(a, b))
    return add(sh.xdown(add(along, across)), sub(across, along))


def load_rate(ref, *index):
    return [[get(ref, *index, 3 * r + c) for c in range(3)] for r in range(3)]


def save_rate(ref, rate, *index):
    for r in range(3):
        for c in range(3):
            put(ref, rate[r][c], *index, 3 * r + c)


class Sweep:
    def __init__(self, axes, rows, ext, fields, terms, works, last):
        self.sh = Shifts()
        self.ext, self.fields, self.terms, self.works, self.last = ext, fields, terms, works, last
        ends = [lax.axis_index(axis) == lax.axis_size(axis) - 1 for axis in axes]
        self.top_y = jnp.where(ends[0], LOW + rows, -1)
        top_z = jnp.where(ends[1], SUB, -1)
        self.keep_z = {k: jnp.where(self.sh.sub + SUB * k[0] == top_z, 0.0, 1.0) for k in ALL}

    def read(self, step):
        if step == 0:
            return lambda comp, q: get(self.ext, 3 + comp, q)
        return lambda comp, q: get(self.fields, step - 1, comp, q)

    def rate(self, step, q):
        if step == 0:
            row_terms(self.sh, self.ext, self.terms, q)
        grad = raw_gradient(self.sh, self.read(step), q)
        return row_rate(grad, self.terms, self.works, step, q)

    def node(self, step, q, rate):
        before = load_rate(self.last)
        keep_y = jnp.where(q == self.top_y, 0.0, 1.0)
        for comp in range(3):
            force = row_force(self.sh, before, rate, comp)
            if SHIFTS[step] != 0.0:
                here = self.read(step)(comp, q)
                force = {k: force[k] - (SHIFTS[step] / SIGMA) * here[k] for k in ALL}
            put(
                self.fields,
                {k: force[k] * (self.keep_z[k] * keep_y) for k in ALL},
                step,
                comp,
                q,
            )

    def rows(self, step, start, stop):
        def body(q, carry):
            rate = self.rate(step, q)
            self.node(step, q, rate)
            save_rate(self.last, rate)
            return carry

        lax.fori_loop(start, stop, body, 0)


def pack_kernel(
    disp_ref, load_ref, occ_ref, group_ref, act_ref, block_ref, zhi_ref, zlo_ref, yhi_ref, ylo_ref
):
    rows, cols, depth = occ_ref.shape
    muscles = act_ref.shape[0]

    def row(y, carry):
        group = group_ref[y]
        level = jnp.zeros((cols, depth), jnp.float32)
        for m in range(muscles):
            level = jnp.where(group == m, act_ref[m], level)
        values = [disp_ref[c, y] for c in range(3)] + [load_ref[c, y] for c in range(3)]
        values += [occ_ref[y].astype(jnp.float32), level]
        for c, value in enumerate(values):
            block_ref[c, y] = value
            zhi_ref[c, y] = value[:HIGH]
            zlo_ref[c, y] = value[cols - LOW :]
        return carry

    lax.fori_loop(0, rows, row, 0)

    def channel(c, carry):
        for y in range(HIGH):
            yhi_ref[c, y] = block_ref[c, y]
        for y in range(LOW):
            ylo_ref[c, y] = block_ref[c, rows - LOW + y]
        return carry

    lax.fori_loop(0, CHANNELS, channel, 0)


def inner_kernel(axes, block_ref, zlo_ref, zhi_ref, ext, fields, terms, works, edge, last):
    rows, depth = block_ref.shape[1], block_ref.shape[-1]
    blank = jnp.zeros((1, depth), jnp.float32)

    def assemble(c, carry):
        for y in range(rows):
            ext[c, LOW + y, pl.ds(0, SUB), :] = block_ref[c, y]
            ext[c, LOW + y, pl.ds(SUB, HIGH), :] = zhi_ref[c, y]
            ext[c, LOW + y, pl.ds(SUB + HIGH, 1), :] = blank
            ext[c, LOW + y, pl.ds(2 * SUB - LOW, LOW), :] = zlo_ref[c, y]
        return carry

    lax.fori_loop(0, CHANNELS, assemble, 0)
    sweep = Sweep(axes, rows, ext, fields, terms, works, last)
    for step in range(NB - 1):
        first, final = LOW + step, LOW + rows - 2 - step
        rate = sweep.rate(step, first)
        save_rate(last, rate)
        save_rate(edge, rate, step, 0)
        sweep.rows(step, first + 1, final + 1)
        save_rate(edge, load_rate(last), step, 1)


def outer_kernel(
    axes,
    group_ref,
    ylo_ref,
    yhi_ref,
    clo_ref,
    chi_ref,
    ext_in,
    fields_in,
    terms_in,
    works_in,
    edge,
    sums_ref,
    ext,
    fields,
    terms,
    works,
    last,
    table,
):
    del ext_in, fields_in, terms_in, works_in
    rows = group_ref.shape[0]

    def assemble(c, carry):
        for q in range(LOW):
            ext[c, q, pl.ds(0, SUB), :] = ylo_ref[c, q]
            ext[c, q, pl.ds(SUB, SUB), :] = clo_ref[c, q]
        for q in range(HIGH):
            ext[c, LOW + rows + q, pl.ds(0, SUB), :] = yhi_ref[c, q]
            ext[c, LOW + rows + q, pl.ds(SUB, SUB), :] = chi_ref[c, q]
        return carry

    lax.fori_loop(0, CHANNELS, assemble, 0)
    sweep = Sweep(axes, rows, ext, fields, terms, works, last)
    for step in range(NB - 1):
        save_rate(last, sweep.rate(step, step))
        sweep.rows(step, step + 1, LOW + step)
        sweep.node(step, LOW + step, load_rate(edge, step, 0))
        save_rate(last, load_rate(edge, step, 1))
        sweep.rows(step, LOW + rows - 1 - step, LOW + rows + HIGH - 1 - step)

    zero = jnp.zeros((SUB, LANES), jnp.float32)
    pairs = [(i, j) for i in range(NB) for j in range(i, NB)]

    def finish(q, acc):
        acc = list(acc)
        grad = raw_gradient(sweep.sh, sweep.read(NB - 1), q, OWN)
        rate = row_rate(grad, terms, works, NB - 1, q, OWN)
        for k in OWN:
            for r in range(3):
                for c in range(3):
                    acc[-1] = acc[-1] + rate[r][c][k] * grad[r][c][k]
            for comp in range(3):
                vectors = [ext[(3 + comp, q, *part(k))]]
                vectors += [fields[(s, comp, q, *part(k))] for s in range(NB - 1)]
                for n, (i, j) in enumerate(pairs):
                    acc[n] = acc[n] + vectors[i] * vectors[j]
        return tuple(acc)

    acc = lax.fori_loop(LOW, LOW + rows, finish, tuple(zero for _ in range(len(pairs) + 1)))
    table[...] = jnp.zeros_like(table)
    muscles = (table.shape[0] // 2) // NB
    for n, value in enumerate(acc):
        table[pl.ds(NB * muscles + n, 1), :] = jnp.sum(value, axis=0, keepdims=True)

    def muscle(m, carry):
        total = [zero] * NB
        for y in range(rows):
            for h in range(2):
                mine = group_ref[y, :, pl.ds(LANES * h, LANES)] == m
                for step in range(NB):
                    total[step] = total[step] + jnp.where(
                        mine, works[(step, LOW + y, *part((0, h)))], 0.0
                    )
        for step in range(NB):
            table[pl.ds(step * muscles + m, 1), :] = jnp.sum(total[step], axis=0, keepdims=True)
        return carry

    lax.fori_loop(0, muscles, muscle, 0)
    row = lax.dot_general(
        jnp.ones((SUB, LANES), jnp.float32),
        table[...],
        (((1,), (1,)), ((), ())),
        precision=lax.Precision.HIGHEST,
        preferred_element_type=jnp.float32,
    )
    for i in range(sums_ref.shape[0] // SUB):
        sums_ref[pl.ds(SUB * i, SUB), :] = row


def combine_kernel(muscles, scale, sums_ref, load_ref, fields, x_ref, grad_ref):
    total = jnp.sum(sums_ref[...], axis=0, keepdims=True)
    at = NB * muscles
    pairs = [(i, j) for i in range(NB) for j in range(i, NB)]
    gram = {}
    for n, (i, j) in enumerate(pairs):
        gram[i, j] = gram[j, i] = total[:, at + n : at + n + 1]
    energy = total[:, at + len(pairs) : at + len(pairs) + 1]
    shifts = [MASS + s for s in SHIFTS]
    form = {}
    for j in range(NB - 1):
        for i in range(j + 1):
            form[i, j] = form[j, i] = SIGMA * gram[i, j + 1] + shifts[j] * gram[i, j]
    last = NB - 1
    for i in range(last):
        form[i, last] = form[last, i] = SIGMA * gram[i + 1, last] + shifts[i] * gram[i, last]
    form[last, last] = SIGMA * energy + MASS * gram[last, last]

    def quadratic(matrix, v):
        parts = []
        for i in range(NB):
            if v[i] is None:
                continue
            inner = [matrix[i, j] * v[j] for j in range(NB) if v[j] is not None]
            parts.append(v[i] * functools.reduce(lambda s, t: s + t, inner))
        return functools.reduce(lambda s, t: s + t, parts)

    one = jnp.ones((1, 1), jnp.float32)
    x = [None] * NB
    residual = [one] + [None] * (NB - 1)
    direction = list(residual)
    norm = gram[0, 0]

    def axpy(a, u, v):
        out = []
        for s, t in zip(u, v):
            if s is None:
                out.append(t)
            elif t is None:
                out.append(a * s)
            else:
                out.append(t + a * s)
        return out

    for step in range(NB):
        alpha = norm / quadratic(form, direction)
        x = axpy(alpha, direction, x)
        if step == NB - 1:
            break
        image = [None] * NB
        for i in range(NB - 1):
            if direction[i] is not None:
                up = SIGMA * direction[i]
                same = shifts[i] * direction[i]
                image[i] = same if image[i] is None else image[i] + same
                image[i + 1] = up if image[i + 1] is None else image[i + 1] + up
        residual = axpy(-alpha, image, residual)
        new = quadratic(gram, residual)
        direction = axpy(new / norm, direction, residual)
        norm = new

    grad = None
    for k in range(NB):
        part = x[k] * total[:, k * muscles : (k + 1) * muscles]
        grad = part if grad is None else grad + part
    grad_ref[...] = -scale * grad

    width = load_ref.shape[-1]
    coef = [jnp.broadcast_to(x[k], (SUB, width)) for k in range(NB)]

    def row(y, carry):
        for comp in range(3):
            value = coef[0] * load_ref[comp, y]
            for k in range(1, NB):
                value = value + coef[k] * fields[k - 1, comp, LOW + y, pl.ds(0, SUB), :]
            x_ref[comp, y] = value
        return carry

    lax.fori_loop(0, load_ref.shape[1], row, 0)


def shift(shard, axis, by):
    length = lax.axis_size(axis)
    return lax.ppermute(
        shard, axis, [(i, i + by) for i in range(length) if 0 <= i + by < length]
    )


def per_device(displacement, load, occupancy, voxel_muscle_group, activation):
    rows, cols, depth = occupancy.shape
    muscles = activation.shape[0]
    axes = ("gy", "gz")
    count = LOW + rows + HIGH

    def arr(*shape):
        return jax.ShapeDtypeStruct(shape, jnp.float32)

    block, face_hi, face_lo, row_hi, row_lo = pl.pallas_call(
        pack_kernel,
        out_shape=(
            arr(CHANNELS, rows, cols, depth),
            arr(CHANNELS, rows, HIGH, depth),
            arr(CHANNELS, rows, LOW, depth),
            arr(CHANNELS, HIGH, cols, depth),
            arr(CHANNELS, LOW, cols, depth),
        ),
        in_specs=[VMEM] * 4 + [SMEM],
        out_specs=(VMEM,) * 5,
        compiler_params=pltpu.CompilerParams(vmem_limit_bytes=32 << 20),
        name="pack",
    )(displacement, load, occupancy, voxel_muscle_group, activation)

    zhi = shift(face_hi, "gz", -1)
    zlo = shift(face_lo, "gz", 1)
    yhi = shift(row_hi, "gy", -1)
    ylo = shift(row_lo, "gy", 1)
    gap = jnp.zeros((CHANNELS, rows, 1, depth), jnp.float32)
    around = jnp.concatenate([zhi, gap, zlo], axis=2)
    chi = shift(around[:, :HIGH], "gy", -1)
    clo = shift(around[:, rows - LOW :], "gy", 1)

    state = (
        arr(CHANNELS, count, 2 * SUB, depth),
        arr(NB - 1, 3, count, 2 * SUB, depth),
        arr(TERMS, count - 1, 2 * SUB, depth),
        arr(NB, count - 1, SUB, depth),
    )
    kept = pltpu.VMEM((9, 2 * SUB, depth), jnp.float32)
    inner = pl.pallas_call(
        functools.partial(inner_kernel, axes),
        out_shape=(*state, arr(NB - 1, 2, 9, 2 * SUB, depth)),
        in_specs=[VMEM] * 3,
        out_specs=(VMEM,) * 5,
        scratch_shapes=[kept],
        compiler_params=pltpu.CompilerParams(vmem_limit_bytes=32 << 20),
        name="inner",
    )(block, zlo, zhi)

    devices = lax.axis_size("gy") * lax.axis_size("gz")
    sums, _, fields, _, _ = pl.pallas_call(
        functools.partial(outer_kernel, axes),
        out_shape=(arr(devices, 2 * NB * muscles), *state),
        in_specs=[VMEM] * 10,
        out_specs=(VMEM,) * 5,
        scratch_shapes=[kept, pltpu.VMEM((2 * NB * muscles, LANES), jnp.float32)],
        input_output_aliases={5: 1, 6: 2, 7: 3, 8: 4},
        compiler_params=pltpu.CompilerParams(vmem_limit_bytes=32 << 20),
        name="outer",
    )(voxel_muscle_group, ylo, yhi, clo, chi, *inner)

    every = lax.all_to_all(sums, ("gy", "gz"), 0, 0, tiled=True)

    cells = depth * rows * lax.axis_size("gy") * cols * lax.axis_size("gz")
    scale = 1.0 / math.sqrt(cells / muscles)
    adjoint, muscle_grad = pl.pallas_call(
        functools.partial(combine_kernel, muscles, scale),
        out_shape=(
            jax.ShapeDtypeStruct(load.shape, jnp.float32),
            jax.ShapeDtypeStruct((1, muscles), jnp.float32),
        ),
        in_specs=[VMEM] * 3,
        out_specs=(VMEM, VMEM),
        compiler_params=pltpu.CompilerParams(vmem_limit_bytes=32 << 20),
        name="combine",
    )(every, load, fields)
    return adjoint, muscle_grad.reshape(muscles)


def solution(mesh):
    placed = (
        P(None, "gy", "gz", None),
        P(None, "gy", "gz", None),
        P("gy", "gz", None),
        P("gy", "gz", None),
        P(),
    )
    return jax.shard_map(
        per_device,
        mesh=mesh,
        in_specs=placed,
        out_specs=(P(None, "gy", "gz", None), P()),
        check_vma=False,
    )
```

```python
import functools
import math

import jax
import jax.numpy as jnp
from jax import lax
from jax.experimental import pallas as pl
from jax.experimental.pallas import tpu as pltpu
from jax.sharding import PartitionSpec as P

SHEAR = 1.0
LAME = 4.0
MASS = 0.05

LOW, HIGH = 3, 4
SIGMA = 16.0
SHIFTS = (0.0, 9.95, 1.95)
NB = 4
LANES = 128
SUB = 8
CHANNELS = 8
TERMS = 15
ALL = tuple((zt, h) for zt in range(2) for h in range(2))
OWN = ((0, 0), (0, 1))
VMEM = pl.BlockSpec(memory_space=pltpu.VMEM)


class Shifts:
    def __init__(self):
        lane = lax.broadcasted_iota(jnp.int32, (SUB, LANES), 1)
        self.sub = lax.broadcasted_iota(jnp.int32, (SUB, LANES), 0)
        self.last_lane = lane == LANES - 1
        self.first_lane = lane == 0
        self.last_sub = self.sub == SUB - 1
        self.first_sub = self.sub == 0

    def xup(self, v):
        out = {}
        for zt in {zt for zt, _ in v}:
            r0 = pltpu.roll(v[zt, 0], LANES - 1, 1)
            r1 = pltpu.roll(v[zt, 1], LANES - 1, 1)
            out[zt, 0] = jnp.where(self.last_lane, r1, r0)
            out[zt, 1] = jnp.where(self.last_lane, 0.0, r1)
        return out

    def xdown(self, v):
        out = {}
        for zt in {zt for zt, _ in v}:
            r0 = pltpu.roll(v[zt, 0], 1, 1)
            r1 = pltpu.roll(v[zt, 1], 1, 1)
            out[zt, 0] = jnp.where(self.first_lane, 0.0, r0)
            out[zt, 1] = jnp.where(self.first_lane, r0, r1)
        return out

    def zup(self, v, keys):
        out = {}
        for h in range(2):
            r0 = pltpu.roll(v[0, h], SUB - 1, 0)
            r1 = pltpu.roll(v[1, h], SUB - 1, 0)
            out[0, h] = jnp.where(self.last_sub, r1, r0)
            if (1, h) in keys:
                out[1, h] = jnp.where(self.last_sub, r0, r1)
        return out

    def zdown(self, v):
        out = {}
        for h in range(2):
            r0 = pltpu.roll(v[0, h], 1, 0)
            r1 = pltpu.roll(v[1, h], 1, 0)
            out[0, h] = jnp.where(self.first_sub, r1, r0)
            out[1, h] = jnp.where(self.first_sub, r0, r1)
        return out


def part(k):
    return pl.ds(SUB * k[0], SUB), pl.ds(LANES * k[1], LANES)


def get(ref, *index):
    return {k: ref[(*index, *part(k))] for k in ALL}


def put(ref, value, *index):
    for k in value:
        ref[(*index, *part(k))] = value[k]


def add(a, b):
    return {k: a[k] + b[k] for k in a}


def sub(a, b):
    return {k: a[k] - b[k] for k in a}


def raw_gradient(sh, read, q, keys=ALL):
    result = []
    for comp in range(3):
        here, above = read(comp, q), read(comp, q + 1)
        both, step = add(here, above), sub(above, here)
        both_x, step_x = sh.xup(both), sh.xup(step)
        wide, slope, rise = add(both, both_x), sub(both_x, both), add(step, step_x)
        result.append(
            tuple(
                {k: up[k] + sign * v[k] if sign > 0 else up[k] - v[k] for k in keys}
                for v, up, sign in (
                    (slope, sh.zup(slope, keys), 1),
                    (rise, sh.zup(rise, keys), 1),
                    (wide, sh.zup(wide, keys), -1),
                )
            )
        )
    return result


def row_terms(sh, ext, terms, q):
    grad = raw_gradient(sh, lambda comp, at: get(ext, comp, at), q)
    for k in ALL:
        occ, level = ext[(6, q, *part(k))], ext[(7, q, *part(k))]
        deform = [
            [0.25 * grad[r][c][k] + (1.0 if r == c else 0.0) for c in range(3)] for r in range(3)
        ]
        cof = [
            [
                deform[(r + 1) % 3][(c + 1) % 3] * deform[(r + 2) % 3][(c + 2) % 3]
                - deform[(r + 1) % 3][(c + 2) % 3] * deform[(r + 2) % 3][(c + 1) % 3]
                for c in range(3)
            ]
            for r in range(3)
        ]
        volume = deform[0][0] * cof[0][0] + deform[0][1] * cof[0][1] + deform[0][2] * cof[0][2]
        inverse = 1.0 / volume
        scaled = occ * (1.0 / (16.0 * SIGMA))
        values = [cof[r][c] * inverse for r in range(3) for c in range(3)]
        values.append(scaled * (SHEAR - LAME * jnp.log(volume)))
        values.append(scaled)
        values.append(scaled * (SHEAR + level))
        quarter = 0.25 * occ
        values += [quarter * deform[r][0] for r in range(3)]
        for i, value in enumerate(values):
            terms[(i, q, *part(k))] = value


def row_rate(grad, terms, works, step, q, keys=ALL):
    rate = [[{} for _ in range(3)] for _ in range(3)]
    for k in keys:

        def term(i):
            return terms[(i, q, *part(k))]

        g = [[grad[r][c][k] for c in range(3)] for r in range(3)]
        inv_t = [[term(3 * r + c) for c in range(3)] for r in range(3)]
        shear, occ, fibre = term(9), term(10), term(11)
        pulled = [
            [
                inv_t[0][a] * g[0][b] + inv_t[1][a] * g[1][b] + inv_t[2][a] * g[2][b]
                for b in range(3)
            ]
            for a in range(3)
        ]
        spread = (LAME * occ) * (pulled[0][0] + pulled[1][1] + pulled[2][2])
        z = [
            [shear * pulled[c][m] + spread if c == m else shear * pulled[c][m] for c in range(3)]
            for m in range(3)
        ]
        for r in range(3):
            for c in range(3):
                rate[r][c][k] = (
                    (fibre if c == 0 else occ) * g[r][c]
                    + inv_t[r][0] * z[0][c]
                    + inv_t[r][1] * z[1][c]
                    + inv_t[r][2] * z[2][c]
                )
        if k in OWN:
            works[(step, q, *part(k))] = (
                term(12) * g[0][0] + term(13) * g[1][0] + term(14) * g[2][0]
            )
    return rate


def row_force(sh, before, rate, comp):
    p = add(before[comp][0], rate[comp][0])
    a = sub(before[comp][1], rate[comp][1])
    b = add(before[comp][2], rate[comp][2])
    along = add(p, sh.zdown(p))
    across = add(sh.zdown(add(a, b)), sub(a, b))
    return add(sh.xdown(add(along, across)), sub(across, along))


def load_rate(ref, *index):
    return [[get(ref, *index, 3 * r + c) for c in range(3)] for r in range(3)]


def save_rate(ref, rate, *index):
    for r in range(3):
        for c in range(3):
            put(ref, rate[r][c], *index, 3 * r + c)


class Sweep:
    def __init__(self, axes, rows, ext, fields, terms, works, last):
        self.sh = Shifts()
        self.ext, self.fields, self.terms, self.works, self.last = ext, fields, terms, works, last
        ends = [lax.axis_index(axis) == lax.axis_size(axis) - 1 for axis in axes]
        self.top_y = jnp.where(ends[0], LOW + rows, -1)
        top_z = jnp.where(ends[1], SUB, -1)
        self.keep_z = {k: jnp.where(self.sh.sub + SUB * k[0] == top_z, 0.0, 1.0) for k in ALL}

    def read(self, step):
        if step == 0:
            return lambda comp, q: get(self.ext, 3 + comp, q)
        return lambda comp, q: get(self.fields, step - 1, comp, q)

    def rate(self, step, q):
        if step == 0:
            row_terms(self.sh, self.ext, self.terms, q)
        grad = raw_gradient(self.sh, self.read(step), q)
        return row_rate(grad, self.terms, self.works, step, q)

    def node(self, step, q, rate):
        before = load_rate(self.last)
        keep_y = jnp.where(q == self.top_y, 0.0, 1.0)
        for comp in range(3):
            force = row_force(self.sh, before, rate, comp)
            if SHIFTS[step] != 0.0:
                here = self.read(step)(comp, q)
                force = {k: force[k] - (SHIFTS[step] / SIGMA) * here[k] for k in ALL}
            put(
                self.fields,
                {k: force[k] * (self.keep_z[k] * keep_y) for k in ALL},
                step,
                comp,
                q,
            )

    def rows(self, step, start, stop):
        def body(q, carry):
            rate = self.rate(step, q)
            self.node(step, q, rate)
            save_rate(self.last, rate)
            return carry

        lax.fori_loop(start, stop, body, 0)


def even(axis):
    return lax.rem(lax.axis_index(axis), 2) == 0


def pack_kernel(
    axes,
    disp_hbm,
    load_hbm,
    occ_hbm,
    group_hbm,
    act_hbm,
    block_ref,
    zpair_ref,
    znext_ref,
    ypair_ref,
    ynext_ref,
    disp_ref,
    load_ref,
    occ_ref,
    group_ref,
    act_ref,
    sems,
):
    copies = [
        pltpu.make_async_copy(source, target, sems.at[i])
        for i, (source, target) in enumerate(
            (
                (act_hbm, act_ref),
                (group_hbm, group_ref),
                (occ_hbm, occ_ref),
                (disp_hbm, disp_ref),
                (load_hbm, load_ref),
            )
        )
    ]
    for copy in copies:
        copy.start()
    rows, cols, depth = occ_ref.shape
    muscles = act_ref.shape[0]
    even_y, even_z = even(axes[0]), even(axes[1])
    for copy in copies:
        copy.wait()

    def row(y, carry):
        group = group_ref[y]
        level = jnp.zeros((cols, depth), jnp.float32)
        for m in range(muscles):
            level = jnp.where(group == m, act_ref[m], level)
        values = [disp_ref[c, y] for c in range(3)] + [load_ref[c, y] for c in range(3)]
        values += [occ_ref[y].astype(jnp.float32), level]
        for c, value in enumerate(values):
            block_ref[c, y] = value
            bottom, top = value[:HIGH], value[cols - HIGH :]
            zpair_ref[c, y] = jnp.where(even_z, top, bottom)
            znext_ref[c, y] = jnp.where(even_z, bottom, top)
        return carry

    lax.fori_loop(0, rows, row, 0)
    send_rows(block_ref, ypair_ref, ynext_ref, even_y)


def send_rows(block_ref, pair_ref, next_ref, is_even):
    rows = block_ref.shape[1]
    pair_at = jnp.where(is_even, rows - HIGH, 0)

    def channel(c, carry):
        for y in range(HIGH):
            pair_ref[c, y] = block_ref[c, pair_at + y]
            next_ref[c, y] = block_ref[c, rows - HIGH - pair_at + y]
        return carry

    lax.fori_loop(0, CHANNELS, channel, 0)


def corner_kernel(axes, zpair_ref, znext_ref, around_ref, ypair_ref, ynext_ref):
    even_y, even_z = even(axes[0]), even(axes[1])

    def channel(c, carry):
        for y in range(around_ref.shape[1]):
            pair, far = zpair_ref[c, y], znext_ref[c, y]
            around_ref[c, y, pl.ds(0, HIGH), :] = jnp.where(even_z, pair, far)
            around_ref[c, y, pl.ds(HIGH, HIGH), :] = jnp.where(even_z, far, pair)
        return carry

    lax.fori_loop(0, CHANNELS, channel, 0)
    send_rows(around_ref, ypair_ref, ynext_ref, even_y)


def inner_kernel(axes, block_ref, around_ref, ext, fields, terms, works, edge, last):
    rows = block_ref.shape[1]

    def assemble(c, carry):
        for y in range(rows):
            ext[c, LOW + y, pl.ds(0, SUB), :] = block_ref[c, y]
            ext[c, LOW + y, pl.ds(SUB, SUB), :] = around_ref[c, y]
        return carry

    lax.fori_loop(0, CHANNELS, assemble, 0)
    sweep = Sweep(axes, rows, ext, fields, terms, works, last)
    for step in range(NB - 1):
        first, final = LOW + step, LOW + rows - 2 - step
        rate = sweep.rate(step, first)
        save_rate(last, rate)
        save_rate(edge, rate, step, 0)
        sweep.rows(step, first + 1, final + 1)
        save_rate(edge, load_rate(last), step, 1)


def outer_kernel(
    axes,
    group_ref,
    ypair_ref,
    ynext_ref,
    cpair_ref,
    cnext_ref,
    ext_in,
    fields_in,
    terms_in,
    works_in,
    edge,
    sums_ref,
    ext,
    fields,
    terms,
    works,
    last,
    table,
):
    del ext_in, fields_in, terms_in, works_in
    rows = group_ref.shape[0]
    even_y = even(axes[0])

    def assemble(c, carry):
        for zt, pair_ref, next_ref in ((0, ypair_ref, ynext_ref), (1, cpair_ref, cnext_ref)):
            for y in range(HIGH):
                pair, far = pair_ref[c, y], next_ref[c, y]
                ext[c, LOW + rows + y, pl.ds(SUB * zt, SUB), :] = jnp.where(even_y, pair, far)
                if y >= HIGH - LOW:
                    ext[c, y - HIGH + LOW, pl.ds(SUB * zt, SUB), :] = jnp.where(even_y, far, pair)
        return carry

    lax.fori_loop(0, CHANNELS, assemble, 0)
    sweep = Sweep(axes, rows, ext, fields, terms, works, last)
    for step in range(NB - 1):
        save_rate(last, sweep.rate(step, step))
        sweep.rows(step, step + 1, LOW + step)
        sweep.node(step, LOW + step, load_rate(edge, step, 0))
        save_rate(last, load_rate(edge, step, 1))
        sweep.rows(step, LOW + rows - 1 - step, LOW + rows + HIGH - 1 - step)

    zero = jnp.zeros((SUB, LANES), jnp.float32)
    pairs = [(i, j) for i in range(NB) for j in range(i, NB)]

    def finish(q, acc):
        acc = list(acc)
        grad = raw_gradient(sweep.sh, sweep.read(NB - 1), q, OWN)
        rate = row_rate(grad, terms, works, NB - 1, q, OWN)
        for k in OWN:
            for r in range(3):
                for c in range(3):
                    acc[-1] = acc[-1] + rate[r][c][k] * grad[r][c][k]
            for comp in range(3):
                vectors = [ext[(3 + comp, q, *part(k))]]
                vectors += [fields[(s, comp, q, *part(k))] for s in range(NB - 1)]
                for n, (i, j) in enumerate(pairs):
                    acc[n] = acc[n] + vectors[i] * vectors[j]
        return tuple(acc)

    acc = lax.fori_loop(LOW, LOW + rows, finish, tuple(zero for _ in range(len(pairs) + 1)))
    table[...] = jnp.zeros_like(table)
    muscles = (table.shape[0] // 2) // NB
    for n, value in enumerate(acc):
        table[pl.ds(NB * muscles + n, 1), :] = jnp.sum(value, axis=0, keepdims=True)

    def muscle(m, carry):
        total = [zero] * NB
        for y in range(rows):
            for h in range(2):
                mine = group_ref[y, :, pl.ds(LANES * h, LANES)] == m
                for step in range(NB):
                    total[step] = total[step] + jnp.where(
                        mine, works[(step, LOW + y, *part((0, h)))], 0.0
                    )
        for step in range(NB):
            table[pl.ds(step * muscles + m, 1), :] = jnp.sum(total[step], axis=0, keepdims=True)
        return carry

    lax.fori_loop(0, muscles, muscle, 0)
    row = lax.dot_general(
        jnp.ones((SUB, LANES), jnp.float32),
        table[...],
        (((1,), (1,)), ((), ())),
        precision=lax.Precision.HIGHEST,
        preferred_element_type=jnp.float32,
    )
    for i in range(sums_ref.shape[0] // SUB):
        sums_ref[pl.ds(SUB * i, SUB), :] = row


def combine_kernel(muscles, scale, sums_ref, block_ref, fields, x_ref, grad_ref):
    total = jnp.sum(sums_ref[...], axis=0, keepdims=True)
    at = NB * muscles
    pairs = [(i, j) for i in range(NB) for j in range(i, NB)]
    gram = {}
    for n, (i, j) in enumerate(pairs):
        gram[i, j] = gram[j, i] = total[:, at + n : at + n + 1]
    energy = total[:, at + len(pairs) : at + len(pairs) + 1]
    shifts = [MASS + s for s in SHIFTS]
    form = {}
    for j in range(NB - 1):
        for i in range(j + 1):
            form[i, j] = form[j, i] = SIGMA * gram[i, j + 1] + shifts[j] * gram[i, j]
    last = NB - 1
    for i in range(last):
        form[i, last] = form[last, i] = SIGMA * gram[i + 1, last] + shifts[i] * gram[i, last]
    form[last, last] = SIGMA * energy + MASS * gram[last, last]

    def quadratic(matrix, v):
        parts = []
        for i in range(NB):
            if v[i] is None:
                continue
            inner = [matrix[i, j] * v[j] for j in range(NB) if v[j] is not None]
            parts.append(v[i] * functools.reduce(lambda s, t: s + t, inner))
        return functools.reduce(lambda s, t: s + t, parts)

    one = jnp.ones((1, 1), jnp.float32)
    x = [None] * NB
    residual = [one] + [None] * (NB - 1)
    direction = list(residual)
    norm = gram[0, 0]

    def axpy(a, u, v):
        out = []
        for s, t in zip(u, v):
            if s is None:
                out.append(t)
            elif t is None:
                out.append(a * s)
            else:
                out.append(t + a * s)
        return out

    for step in range(NB):
        alpha = norm / quadratic(form, direction)
        x = axpy(alpha, direction, x)
        if step == NB - 1:
            break
        image = [None] * NB
        for i in range(NB - 1):
            if direction[i] is not None:
                up = SIGMA * direction[i]
                same = shifts[i] * direction[i]
                image[i] = same if image[i] is None else image[i] + same
                image[i + 1] = up if image[i + 1] is None else image[i + 1] + up
        residual = axpy(-alpha, image, residual)
        new = quadratic(gram, residual)
        direction = axpy(new / norm, direction, residual)
        norm = new

    grad = None
    for k in range(NB):
        part = x[k] * total[:, k * muscles : (k + 1) * muscles]
        grad = part if grad is None else grad + part
    grad_ref[...] = -scale * grad

    width = block_ref.shape[-1]
    coef = [jnp.broadcast_to(x[k], (SUB, width)) for k in range(NB)]

    def row(y, carry):
        for comp in range(3):
            value = coef[0] * block_ref[3 + comp, y]
            for k in range(1, NB):
                value = value + coef[k] * fields[k - 1, comp, LOW + y, pl.ds(0, SUB), :]
            x_ref[comp, y] = value
        return carry

    lax.fori_loop(0, block_ref.shape[1], row, 0)


def swap(shard, axis, first):
    length = lax.axis_size(axis)
    pairs = [(i, i + 1) for i in range(first, length - 1, 2)]
    return lax.ppermute(shard, axis, pairs + [(j, i) for i, j in pairs])


def per_device(displacement, load, occupancy, voxel_muscle_group, activation):
    rows, cols, depth = occupancy.shape
    muscles = activation.shape[0]
    axes = ("gy", "gz")
    count = LOW + rows + HIGH

    def arr(*shape):
        return jax.ShapeDtypeStruct(shape, jnp.float32)

    anywhere = pl.BlockSpec(memory_space=pltpu.HBM)
    faces = (arr(CHANNELS, rows, HIGH, depth),) * 2
    edges = (arr(CHANNELS, HIGH, cols, depth),) * 2
    block, zpair, znext, ypair, ynext = pl.pallas_call(
        functools.partial(pack_kernel, axes),
        out_shape=(arr(CHANNELS, rows, cols, depth), *faces, *edges),
        in_specs=[anywhere] * 5,
        out_specs=(VMEM,) * 5,
        scratch_shapes=[
            pltpu.VMEM(displacement.shape, jnp.float32),
            pltpu.VMEM(load.shape, jnp.float32),
            pltpu.VMEM(occupancy.shape, jnp.int32),
            pltpu.VMEM(occupancy.shape, jnp.int32),
            pltpu.SMEM((muscles,), jnp.float32),
            pltpu.SemaphoreType.DMA((5,)),
        ],
        compiler_params=pltpu.CompilerParams(vmem_limit_bytes=32 << 20),
        name="pack",
    )(
        *(
            pltpu.with_memory_space_constraint(value, pltpu.HBM)
            for value in (displacement, load, occupancy, voxel_muscle_group, activation)
        )
    )

    received = [
        swap(znext, "gz", 1),
        swap(zpair, "gz", 0),
        swap(ynext, "gy", 1),
        swap(ypair, "gy", 0),
    ]
    znext, zpair, ynext, ypair = lax.optimization_barrier(received)
    around, cpair, cnext = pl.pallas_call(
        functools.partial(corner_kernel, axes),
        out_shape=(arr(CHANNELS, rows, 2 * HIGH, depth), *edges),
        in_specs=[VMEM] * 2,
        out_specs=(VMEM,) * 3,
        compiler_params=pltpu.CompilerParams(vmem_limit_bytes=32 << 20),
        name="corner",
    )(zpair, znext)
    cnext = swap(cnext, "gy", 1)
    cpair = swap(cpair, "gy", 0)

    state = (
        arr(CHANNELS, count, 2 * SUB, depth),
        arr(NB - 1, 3, count, 2 * SUB, depth),
        arr(TERMS, count - 1, 2 * SUB, depth),
        arr(NB, count - 1, SUB, depth),
    )
    kept = pltpu.VMEM((9, 2 * SUB, depth), jnp.float32)
    inner = pl.pallas_call(
        functools.partial(inner_kernel, axes),
        out_shape=(*state, arr(NB - 1, 2, 9, 2 * SUB, depth)),
        in_specs=[VMEM] * 2,
        out_specs=(VMEM,) * 5,
        scratch_shapes=[kept],
        compiler_params=pltpu.CompilerParams(vmem_limit_bytes=32 << 20),
        name="inner",
    )(block, around)

    devices = lax.axis_size("gy") * lax.axis_size("gz")
    sums, _, fields, _, _ = pl.pallas_call(
        functools.partial(outer_kernel, axes),
        out_shape=(arr(devices, 2 * NB * muscles), *state),
        in_specs=[VMEM] * 10,
        out_specs=(VMEM,) * 5,
        scratch_shapes=[kept, pltpu.VMEM((2 * NB * muscles, LANES), jnp.float32)],
        input_output_aliases={5: 1, 6: 2, 7: 3, 8: 4},
        compiler_params=pltpu.CompilerParams(vmem_limit_bytes=32 << 20),
        name="outer",
    )(voxel_muscle_group, ypair, ynext, cpair, cnext, *inner)

    every = lax.all_to_all(sums, ("gy", "gz"), 0, 0, tiled=True)

    cells = depth * rows * lax.axis_size("gy") * cols * lax.axis_size("gz")
    scale = 1.0 / math.sqrt(cells / muscles)
    adjoint, muscle_grad = pl.pallas_call(
        functools.partial(combine_kernel, muscles, scale),
        out_shape=(
            jax.ShapeDtypeStruct(load.shape, jnp.float32),
            jax.ShapeDtypeStruct((1, muscles), jnp.float32),
        ),
        in_specs=[VMEM] * 3,
        out_specs=(VMEM, VMEM),
        compiler_params=pltpu.CompilerParams(vmem_limit_bytes=32 << 20),
        name="combine",
    )(every, block, fields)
    return adjoint, muscle_grad.reshape(muscles)


def solution(mesh):
    placed = (
        P(None, "gy", "gz", None),
        P(None, "gy", "gz", None),
        P("gy", "gz", None),
        P("gy", "gz", None),
        P(),
    )
    return jax.shard_map(
        per_device,
        mesh=mesh,
        in_specs=placed,
        out_specs=(P(None, "gy", "gz", None), P()),
        check_vma=False,
    )
```

```python
import functools
import math

import jax
import jax.numpy as jnp
from jax import lax
from jax.experimental import pallas as pl
from jax.experimental.pallas import tpu as pltpu
from jax.sharding import PartitionSpec as P

SHEAR = 1.0
LAME = 4.0
MASS = 0.05

LOW, HIGH = 3, 4
SIGMA = 16.0
SHIFTS = (0.0, 9.95, 1.95)
NB = 4
LANES = 128
SUB = 8
CHANNELS = 8
TERMS = 15
ALL = tuple((zt, h) for zt in range(2) for h in range(2))
OWN = ((0, 0), (0, 1))
VMEM = pl.BlockSpec(memory_space=pltpu.VMEM)


class Shifts:
    def __init__(self):
        lane = lax.broadcasted_iota(jnp.int32, (SUB, LANES), 1)
        self.sub = lax.broadcasted_iota(jnp.int32, (SUB, LANES), 0)
        self.last_lane = lane == LANES - 1
        self.first_lane = lane == 0
        self.last_sub = self.sub == SUB - 1
        self.first_sub = self.sub == 0

    def xup(self, v):
        out = {}
        for zt in {zt for zt, _ in v}:
            r0 = pltpu.roll(v[zt, 0], LANES - 1, 1)
            r1 = pltpu.roll(v[zt, 1], LANES - 1, 1)
            out[zt, 0] = jnp.where(self.last_lane, r1, r0)
            out[zt, 1] = jnp.where(self.last_lane, 0.0, r1)
        return out

    def xdown(self, v):
        out = {}
        for zt in {zt for zt, _ in v}:
            r0 = pltpu.roll(v[zt, 0], 1, 1)
            r1 = pltpu.roll(v[zt, 1], 1, 1)
            out[zt, 0] = jnp.where(self.first_lane, 0.0, r0)
            out[zt, 1] = jnp.where(self.first_lane, r0, r1)
        return out

    def zup(self, v, keys):
        out = {}
        for h in range(2):
            r0 = pltpu.roll(v[0, h], SUB - 1, 0)
            r1 = pltpu.roll(v[1, h], SUB - 1, 0)
            out[0, h] = jnp.where(self.last_sub, r1, r0)
            if (1, h) in keys:
                out[1, h] = jnp.where(self.last_sub, r0, r1)
        return out

    def zdown(self, v):
        out = {}
        for h in range(2):
            r0 = pltpu.roll(v[0, h], 1, 0)
            r1 = pltpu.roll(v[1, h], 1, 0)
            out[0, h] = jnp.where(self.first_sub, r1, r0)
            out[1, h] = jnp.where(self.first_sub, r0, r1)
        return out


def part(k):
    return pl.ds(SUB * k[0], SUB), pl.ds(LANES * k[1], LANES)


def get(ref, *index):
    return {k: ref[(*index, *part(k))] for k in ALL}


def put(ref, value, *index):
    for k in value:
        ref[(*index, *part(k))] = value[k]


def add(a, b):
    return {k: a[k] + b[k] for k in a}


def sub(a, b):
    return {k: a[k] - b[k] for k in a}


def raw_gradient(sh, read, q, keys=ALL):
    result = []
    for comp in range(3):
        here, above = read(comp, q), read(comp, q + 1)
        both, step = add(here, above), sub(above, here)
        both_x, step_x = sh.xup(both), sh.xup(step)
        wide, slope, rise = add(both, both_x), sub(both_x, both), add(step, step_x)
        result.append(
            tuple(
                {k: up[k] + sign * v[k] if sign > 0 else up[k] - v[k] for k in keys}
                for v, up, sign in (
                    (slope, sh.zup(slope, keys), 1),
                    (rise, sh.zup(rise, keys), 1),
                    (wide, sh.zup(wide, keys), -1),
                )
            )
        )
    return result


def row_terms(sh, ext, terms, q):
    grad = raw_gradient(sh, lambda comp, at: get(ext, comp, at), q)
    for k in ALL:
        occ, level = ext[(6, q, *part(k))], ext[(7, q, *part(k))]
        deform = [
            [0.25 * grad[r][c][k] + (1.0 if r == c else 0.0) for c in range(3)] for r in range(3)
        ]
        cof = [
            [
                deform[(r + 1) % 3][(c + 1) % 3] * deform[(r + 2) % 3][(c + 2) % 3]
                - deform[(r + 1) % 3][(c + 2) % 3] * deform[(r + 2) % 3][(c + 1) % 3]
                for c in range(3)
            ]
            for r in range(3)
        ]
        volume = deform[0][0] * cof[0][0] + deform[0][1] * cof[0][1] + deform[0][2] * cof[0][2]
        inverse = 1.0 / volume
        scaled = occ * (1.0 / (16.0 * SIGMA))
        values = [cof[r][c] * inverse for r in range(3) for c in range(3)]
        values.append(scaled * (SHEAR - LAME * jnp.log(volume)))
        values.append(scaled)
        values.append(scaled * (SHEAR + level))
        quarter = 0.25 * occ
        values += [quarter * deform[r][0] for r in range(3)]
        for i, value in enumerate(values):
            terms[(i, q, *part(k))] = value


def row_rate(grad, terms, works, step, q, keys=ALL):
    rate = [[{} for _ in range(3)] for _ in range(3)]
    for k in keys:

        def term(i):
            return terms[(i, q, *part(k))]

        g = [[grad[r][c][k] for c in range(3)] for r in range(3)]
        inv_t = [[term(3 * r + c) for c in range(3)] for r in range(3)]
        shear, occ, fibre = term(9), term(10), term(11)
        pulled = [
            [
                inv_t[0][a] * g[0][b] + inv_t[1][a] * g[1][b] + inv_t[2][a] * g[2][b]
                for b in range(3)
            ]
            for a in range(3)
        ]
        spread = (LAME * occ) * (pulled[0][0] + pulled[1][1] + pulled[2][2])
        z = [
            [shear * pulled[c][m] + spread if c == m else shear * pulled[c][m] for c in range(3)]
            for m in range(3)
        ]
        for r in range(3):
            for c in range(3):
                rate[r][c][k] = (
                    (fibre if c == 0 else occ) * g[r][c]
                    + inv_t[r][0] * z[0][c]
                    + inv_t[r][1] * z[1][c]
                    + inv_t[r][2] * z[2][c]
                )
        if k in OWN:
            works[(step, q, *part(k))] = (
                term(12) * g[0][0] + term(13) * g[1][0] + term(14) * g[2][0]
            )
    return rate


def row_force(sh, before, rate, comp):
    p = add(before[comp][0], rate[comp][0])
    a = sub(before[comp][1], rate[comp][1])
    b = add(before[comp][2], rate[comp][2])
    along = add(p, sh.zdown(p))
    across = add(sh.zdown(add(a, b)), sub(a, b))
    return add(sh.xdown(add(along, across)), sub(across, along))


def load_rate(ref, *index):
    return [[get(ref, *index, 3 * r + c) for c in range(3)] for r in range(3)]


def save_rate(ref, rate, *index):
    for r in range(3):
        for c in range(3):
            put(ref, rate[r][c], *index, 3 * r + c)


class Sweep:
    def __init__(self, axes, rows, ext, fields, terms, works, last):
        self.sh = Shifts()
        self.ext, self.fields, self.terms, self.works, self.last = ext, fields, terms, works, last
        ends = [lax.axis_index(axis) == lax.axis_size(axis) - 1 for axis in axes]
        self.top_y = jnp.where(ends[0], LOW + rows, -1)
        top_z = jnp.where(ends[1], SUB, -1)
        self.keep_z = {k: jnp.where(self.sh.sub + SUB * k[0] == top_z, 0.0, 1.0) for k in ALL}

    def read(self, step):
        if step == 0:
            return lambda comp, q: get(self.ext, 3 + comp, q)
        return lambda comp, q: get(self.fields, step - 1, comp, q)

    def rate(self, step, q):
        if step == 0:
            row_terms(self.sh, self.ext, self.terms, q)
        grad = raw_gradient(self.sh, self.read(step), q)
        return row_rate(grad, self.terms, self.works, step, q)

    def node(self, step, q, rate):
        before = load_rate(self.last)
        keep_y = jnp.where(q == self.top_y, 0.0, 1.0)
        for comp in range(3):
            force = row_force(self.sh, before, rate, comp)
            if SHIFTS[step] != 0.0:
                here = self.read(step)(comp, q)
                force = {k: force[k] - (SHIFTS[step] / SIGMA) * here[k] for k in ALL}
            put(
                self.fields,
                {k: force[k] * (self.keep_z[k] * keep_y) for k in ALL},
                step,
                comp,
                q,
            )

    def rows(self, step, start, stop):
        def body(q, carry):
            rate = self.rate(step, q)
            self.node(step, q, rate)
            save_rate(self.last, rate)
            return carry

        lax.fori_loop(start, stop, body, 0)


def even(axis):
    return lax.rem(lax.axis_index(axis), 2) == 0


def pack_kernel(
    axes,
    disp_hbm,
    load_hbm,
    occ_hbm,
    group_hbm,
    act_hbm,
    block_ref,
    zpair_ref,
    znext_ref,
    ypair_ref,
    ynext_ref,
    group_ref,
    disp_ref,
    load_ref,
    occ_ref,
    act_ref,
    sems,
):
    copies = [
        pltpu.make_async_copy(source, target, sems.at[i])
        for i, (source, target) in enumerate(
            (
                (act_hbm, act_ref),
                (group_hbm, group_ref),
                (occ_hbm, occ_ref),
                (disp_hbm, disp_ref),
                (load_hbm, load_ref),
            )
        )
    ]
    for copy in copies:
        copy.start()
    rows, cols, depth = occ_ref.shape
    muscles = act_ref.shape[0]
    even_y, even_z = even(axes[0]), even(axes[1])
    for copy in copies:
        copy.wait()

    def row(y, carry):
        group = group_ref[y]
        level = jnp.zeros((cols, depth), jnp.float32)
        for m in range(muscles):
            level = jnp.where(group == m, act_ref[m], level)
        values = [disp_ref[c, y] for c in range(3)] + [load_ref[c, y] for c in range(3)]
        values += [occ_ref[y].astype(jnp.float32), level]
        for c, value in enumerate(values):
            block_ref[c, y] = value
            bottom, top = value[:HIGH], value[cols - HIGH :]
            zpair_ref[c, y] = jnp.where(even_z, top, bottom)
            znext_ref[c, y] = jnp.where(even_z, bottom, top)
        return carry

    lax.fori_loop(0, rows, row, 0)
    send_rows(block_ref, ypair_ref, ynext_ref, even_y)


def send_rows(block_ref, pair_ref, next_ref, is_even):
    rows = block_ref.shape[1]
    pair_at = jnp.where(is_even, rows - HIGH, 0)

    def channel(c, carry):
        for y in range(HIGH):
            pair_ref[c, y] = block_ref[c, pair_at + y]
            next_ref[c, y] = block_ref[c, rows - HIGH - pair_at + y]
        return carry

    lax.fori_loop(0, CHANNELS, channel, 0)


def corner_kernel(axes, zpair_ref, znext_ref, around_ref, ypair_ref, ynext_ref):
    even_y, even_z = even(axes[0]), even(axes[1])

    def channel(c, carry):
        for y in range(around_ref.shape[1]):
            pair, far = zpair_ref[c, y], znext_ref[c, y]
            around_ref[c, y, pl.ds(0, HIGH), :] = jnp.where(even_z, pair, far)
            around_ref[c, y, pl.ds(HIGH, HIGH), :] = jnp.where(even_z, far, pair)
        return carry

    lax.fori_loop(0, CHANNELS, channel, 0)
    send_rows(around_ref, ypair_ref, ynext_ref, even_y)


def inner_kernel(axes, block_ref, around_ref, ext, fields, terms, works, edge, last):
    rows = block_ref.shape[1]

    def assemble(c, carry):
        for y in range(rows):
            ext[c, LOW + y, pl.ds(0, SUB), :] = block_ref[c, y]
            ext[c, LOW + y, pl.ds(SUB, SUB), :] = around_ref[c, y]
        return carry

    lax.fori_loop(0, CHANNELS, assemble, 0)
    sweep = Sweep(axes, rows, ext, fields, terms, works, last)
    for step in range(NB - 1):
        first, final = LOW + step, LOW + rows - 2 - step
        rate = sweep.rate(step, first)
        save_rate(last, rate)
        save_rate(edge, rate, step, 0)
        sweep.rows(step, first + 1, final + 1)
        save_rate(edge, load_rate(last), step, 1)


def outer_kernel(
    axes,
    group_ref,
    ynext_ref,
    ypair_ref,
    cnext_ref,
    cpair_ref,
    ext_in,
    fields_in,
    terms_in,
    works_in,
    edge,
    sums_ref,
    ext,
    fields,
    terms,
    works,
    last,
    table,
):
    del ext_in, fields_in, terms_in, works_in
    rows = group_ref.shape[0]
    even_y = even(axes[0])

    def assemble(c, carry):
        for zt, pair_ref, next_ref in ((0, ypair_ref, ynext_ref), (1, cpair_ref, cnext_ref)):
            for y in range(HIGH):
                pair, far = pair_ref[c, y], next_ref[c, y]
                ext[c, LOW + rows + y, pl.ds(SUB * zt, SUB), :] = jnp.where(even_y, pair, far)
                if y >= HIGH - LOW:
                    ext[c, y - HIGH + LOW, pl.ds(SUB * zt, SUB), :] = jnp.where(even_y, far, pair)
        return carry

    lax.fori_loop(0, CHANNELS, assemble, 0)
    sweep = Sweep(axes, rows, ext, fields, terms, works, last)
    for step in range(NB - 1):
        save_rate(last, sweep.rate(step, step))
        sweep.rows(step, step + 1, LOW + step)
        sweep.node(step, LOW + step, load_rate(edge, step, 0))
        save_rate(last, load_rate(edge, step, 1))
        sweep.rows(step, LOW + rows - 1 - step, LOW + rows + HIGH - 1 - step)

    zero = jnp.zeros((SUB, LANES), jnp.float32)
    pairs = [(i, j) for i in range(NB) for j in range(i, NB)]

    def finish(q, acc):
        acc = list(acc)
        grad = raw_gradient(sweep.sh, sweep.read(NB - 1), q, OWN)
        rate = row_rate(grad, terms, works, NB - 1, q, OWN)
        for k in OWN:
            for r in range(3):
                for c in range(3):
                    acc[-1] = acc[-1] + rate[r][c][k] * grad[r][c][k]
            for comp in range(3):
                vectors = [ext[(3 + comp, q, *part(k))]]
                vectors += [fields[(s, comp, q, *part(k))] for s in range(NB - 1)]
                for n, (i, j) in enumerate(pairs):
                    acc[n] = acc[n] + vectors[i] * vectors[j]
        return tuple(acc)

    acc = lax.fori_loop(LOW, LOW + rows, finish, tuple(zero for _ in range(len(pairs) + 1)))
    table[...] = jnp.zeros_like(table)
    muscles = (table.shape[0] // 2) // NB
    for n, value in enumerate(acc):
        table[pl.ds(NB * muscles + n, 1), :] = jnp.sum(value, axis=0, keepdims=True)

    def muscle(m, carry):
        total = [zero] * NB
        for y in range(rows):
            for h in range(2):
                mine = group_ref[y, :, pl.ds(LANES * h, LANES)] == m
                for step in range(NB):
                    total[step] = total[step] + jnp.where(
                        mine, works[(step, LOW + y, *part((0, h)))], 0.0
                    )
        for step in range(NB):
            table[pl.ds(step * muscles + m, 1), :] = jnp.sum(total[step], axis=0, keepdims=True)
        return carry

    lax.fori_loop(0, muscles, muscle, 0)
    row = lax.dot_general(
        jnp.ones((SUB, LANES), jnp.float32),
        table[...],
        (((1,), (1,)), ((), ())),
        precision=lax.Precision.HIGHEST,
        preferred_element_type=jnp.float32,
    )
    for i in range(sums_ref.shape[0] // SUB):
        sums_ref[pl.ds(SUB * i, SUB), :] = row


def combine_kernel(muscles, scale, sums_ref, block_ref, fields, x_hbm, grad_ref, x_ref, sems):
    total = jnp.sum(sums_ref[...], axis=0, keepdims=True)
    at = NB * muscles
    pairs = [(i, j) for i in range(NB) for j in range(i, NB)]
    gram = {}
    for n, (i, j) in enumerate(pairs):
        gram[i, j] = gram[j, i] = total[:, at + n : at + n + 1]
    energy = total[:, at + len(pairs) : at + len(pairs) + 1]
    shifts = [MASS + s for s in SHIFTS]
    form = {}
    for j in range(NB - 1):
        for i in range(j + 1):
            form[i, j] = form[j, i] = SIGMA * gram[i, j + 1] + shifts[j] * gram[i, j]
    last = NB - 1
    for i in range(last):
        form[i, last] = form[last, i] = SIGMA * gram[i + 1, last] + shifts[i] * gram[i, last]
    form[last, last] = SIGMA * energy + MASS * gram[last, last]

    rhs = [gram[0, i] for i in range(NB)]
    inverse = []
    for k in range(NB):
        inverse.append(1.0 / form[k, k])
        for i in range(k + 1, NB):
            factor = form[k, i] * inverse[k]
            rhs[i] = rhs[i] - factor * rhs[k]
            for j in range(i, NB):
                form[i, j] = form[i, j] - factor * form[k, j]
    x = [None] * NB
    for k in reversed(range(NB)):
        value = rhs[k]
        for j in range(k + 1, NB):
            value = value - form[k, j] * x[j]
        x[k] = value * inverse[k]

    grad = None
    for k in range(NB):
        part = x[k] * total[:, k * muscles : (k + 1) * muscles]
        grad = part if grad is None else grad + part
    grad_ref[...] = -scale * grad

    width = block_ref.shape[-1]
    coef = [jnp.broadcast_to(x[k], (SUB, width)) for k in range(NB)]
    copies = []
    for comp in range(3):
        for y in range(block_ref.shape[1]):
            value = coef[0] * block_ref[3 + comp, y]
            for k in range(1, NB):
                value = value + coef[k] * fields[k - 1, comp, LOW + y, pl.ds(0, SUB), :]
            x_ref[comp, y] = value
        copies.append(pltpu.make_async_copy(x_ref.at[comp], x_hbm.at[comp], sems.at[comp]))
        copies[-1].start()
    for copy in copies:
        copy.wait()


def swap(shard, axis, first):
    length = lax.axis_size(axis)
    pairs = [(i, i + 1) for i in range(first, length - 1, 2)]
    return lax.ppermute(shard, axis, pairs + [(j, i) for i, j in pairs])


def per_device(displacement, load, occupancy, voxel_muscle_group, activation):
    rows, cols, depth = occupancy.shape
    muscles = activation.shape[0]
    axes = ("gy", "gz")
    count = LOW + rows + HIGH

    def arr(*shape):
        return jax.ShapeDtypeStruct(shape, jnp.float32)

    anywhere = pl.BlockSpec(memory_space=pltpu.HBM)
    faces = (arr(CHANNELS, rows, HIGH, depth),) * 2
    edges = (arr(CHANNELS, HIGH, cols, depth),) * 2
    block, zpair, znext, ypair, ynext, group = pl.pallas_call(
        functools.partial(pack_kernel, axes),
        out_shape=(
            arr(CHANNELS, rows, cols, depth),
            *faces,
            *edges,
            jax.ShapeDtypeStruct(occupancy.shape, jnp.int32),
        ),
        in_specs=[anywhere] * 5,
        out_specs=(VMEM,) * 6,
        scratch_shapes=[
            pltpu.VMEM(displacement.shape, jnp.float32),
            pltpu.VMEM(load.shape, jnp.float32),
            pltpu.VMEM(occupancy.shape, jnp.int32),
            pltpu.SMEM((muscles,), jnp.float32),
            pltpu.SemaphoreType.DMA((5,)),
        ],
        compiler_params=pltpu.CompilerParams(vmem_limit_bytes=32 << 20),
        name="pack",
    )(
        *(
            pltpu.with_memory_space_constraint(value, pltpu.HBM)
            for value in (displacement, load, occupancy, voxel_muscle_group, activation)
        )
    )

    received = [
        swap(znext, "gz", 1),
        swap(zpair, "gz", 0),
        swap(ynext, "gy", 1),
        swap(ypair, "gy", 0),
    ]
    znext, zpair, ynext, ypair = lax.optimization_barrier(received)
    around, cpair, cnext = pl.pallas_call(
        functools.partial(corner_kernel, axes),
        out_shape=(arr(CHANNELS, rows, 2 * HIGH, depth), *edges),
        in_specs=[VMEM] * 2,
        out_specs=(VMEM,) * 3,
        compiler_params=pltpu.CompilerParams(vmem_limit_bytes=32 << 20),
        name="corner",
    )(zpair, znext)
    cnext = swap(cnext, "gy", 1)
    cpair = swap(cpair, "gy", 0)

    state = (
        arr(CHANNELS, count, 2 * SUB, depth),
        arr(NB - 1, 3, count, 2 * SUB, depth),
        arr(TERMS, count - 1, 2 * SUB, depth),
        arr(NB, count - 1, SUB, depth),
    )
    kept = pltpu.VMEM((9, 2 * SUB, depth), jnp.float32)
    inner = pl.pallas_call(
        functools.partial(inner_kernel, axes),
        out_shape=(*state, arr(NB - 1, 2, 9, 2 * SUB, depth)),
        in_specs=[VMEM] * 2,
        out_specs=(VMEM,) * 5,
        scratch_shapes=[kept],
        compiler_params=pltpu.CompilerParams(vmem_limit_bytes=32 << 20),
        name="inner",
    )(block, around)

    devices = lax.axis_size("gy") * lax.axis_size("gz")
    sums, _, fields, _, _ = pl.pallas_call(
        functools.partial(outer_kernel, axes),
        out_shape=(arr(devices, 2 * NB * muscles), *state),
        in_specs=[VMEM] * 10,
        out_specs=(VMEM,) * 5,
        scratch_shapes=[kept, pltpu.VMEM((2 * NB * muscles, LANES), jnp.float32)],
        input_output_aliases={5: 1, 6: 2, 7: 3, 8: 4},
        compiler_params=pltpu.CompilerParams(vmem_limit_bytes=32 << 20),
        name="outer",
    )(group, ynext, ypair, cnext, cpair, *inner)

    every = lax.all_to_all(sums, ("gy", "gz"), 0, 0, tiled=True)

    cells = depth * rows * lax.axis_size("gy") * cols * lax.axis_size("gz")
    scale = 1.0 / math.sqrt(cells / muscles)
    adjoint, muscle_grad = pl.pallas_call(
        functools.partial(combine_kernel, muscles, scale),
        out_shape=(
            jax.ShapeDtypeStruct(load.shape, jnp.float32),
            jax.ShapeDtypeStruct((1, muscles), jnp.float32),
        ),
        in_specs=[VMEM] * 3,
        out_specs=(anywhere, VMEM),
        scratch_shapes=[pltpu.VMEM(load.shape, jnp.float32), pltpu.SemaphoreType.DMA((3,))],
        compiler_params=pltpu.CompilerParams(vmem_limit_bytes=32 << 20),
        name="combine",
    )(every, block, fields)
    return adjoint, muscle_grad.reshape(muscles)


def solution(mesh):
    placed = (
        P(None, "gy", "gz", None),
        P(None, "gy", "gz", None),
        P("gy", "gz", None),
        P("gy", "gz", None),
        P(),
    )
    return jax.shard_map(
        per_device,
        mesh=mesh,
        in_specs=placed,
        out_specs=(P(None, "gy", "gz", None), P()),
        check_vma=False,
    )
```

```python
import functools
import math

import jax
import jax.numpy as jnp
from jax import lax
from jax.experimental import pallas as pl
from jax.experimental.pallas import tpu as pltpu
from jax.sharding import PartitionSpec as P

SHEAR = 1.0
LAME = 4.0
MASS = 0.05

LOW, HIGH = 3, 4
SIGMA = 16.0
SHIFTS = (0.0, 9.95, 1.95)
NB = 4
LANES = 128
SUB = 8
CHANNELS = 8
TERMS = 15
ALL = tuple((zt, h) for zt in range(2) for h in range(2))
OWN = ((0, 0), (0, 1))
VMEM = pl.BlockSpec(memory_space=pltpu.VMEM)


class Shifts:
    def __init__(self):
        lane = lax.broadcasted_iota(jnp.int32, (SUB, LANES), 1)
        self.sub = lax.broadcasted_iota(jnp.int32, (SUB, LANES), 0)
        self.last_lane = lane == LANES - 1
        self.first_lane = lane == 0
        self.last_sub = self.sub == SUB - 1
        self.first_sub = self.sub == 0

    def xup(self, v):
        out = {}
        for zt in {zt for zt, _ in v}:
            r0 = pltpu.roll(v[zt, 0], LANES - 1, 1)
            r1 = pltpu.roll(v[zt, 1], LANES - 1, 1)
            out[zt, 0] = jnp.where(self.last_lane, r1, r0)
            out[zt, 1] = jnp.where(self.last_lane, 0.0, r1)
        return out

    def xdown(self, v):
        out = {}
        for zt in {zt for zt, _ in v}:
            r0 = pltpu.roll(v[zt, 0], 1, 1)
            r1 = pltpu.roll(v[zt, 1], 1, 1)
            out[zt, 0] = jnp.where(self.first_lane, 0.0, r0)
            out[zt, 1] = jnp.where(self.first_lane, r0, r1)
        return out

    def zup(self, v, keys):
        out = {}
        for h in range(2):
            r0 = pltpu.roll(v[0, h], SUB - 1, 0)
            r1 = pltpu.roll(v[1, h], SUB - 1, 0)
            out[0, h] = jnp.where(self.last_sub, r1, r0)
            if (1, h) in keys:
                out[1, h] = jnp.where(self.last_sub, r0, r1)
        return out

    def zdown(self, v):
        out = {}
        for h in range(2):
            r0 = pltpu.roll(v[0, h], 1, 0)
            r1 = pltpu.roll(v[1, h], 1, 0)
            out[0, h] = jnp.where(self.first_sub, r1, r0)
            out[1, h] = jnp.where(self.first_sub, r0, r1)
        return out


def part(k):
    return pl.ds(SUB * k[0], SUB), pl.ds(LANES * k[1], LANES)


def get(ref, *index):
    return {k: ref[(*index, *part(k))] for k in ALL}


def put(ref, value, *index):
    for k in value:
        ref[(*index, *part(k))] = value[k]


def add(a, b):
    return {k: a[k] + b[k] for k in a}


def sub(a, b):
    return {k: a[k] - b[k] for k in a}


def raw_gradient(sh, read, q, keys=ALL):
    result = []
    for comp in range(3):
        here, above = read(comp, q), read(comp, q + 1)
        both, step = add(here, above), sub(above, here)
        both_x, step_x = sh.xup(both), sh.xup(step)
        wide, slope, rise = add(both, both_x), sub(both_x, both), add(step, step_x)
        result.append(
            tuple(
                {k: up[k] + sign * v[k] if sign > 0 else up[k] - v[k] for k in keys}
                for v, up, sign in (
                    (slope, sh.zup(slope, keys), 1),
                    (rise, sh.zup(rise, keys), 1),
                    (wide, sh.zup(wide, keys), -1),
                )
            )
        )
    return result


def row_terms(sh, ext, terms, q):
    grad = raw_gradient(sh, lambda comp, at: get(ext, comp, at), q)
    for k in ALL:
        occ, level = ext[(6, q, *part(k))], ext[(7, q, *part(k))]
        deform = [
            [0.25 * grad[r][c][k] + (1.0 if r == c else 0.0) for c in range(3)] for r in range(3)
        ]
        cof = [
            [
                deform[(r + 1) % 3][(c + 1) % 3] * deform[(r + 2) % 3][(c + 2) % 3]
                - deform[(r + 1) % 3][(c + 2) % 3] * deform[(r + 2) % 3][(c + 1) % 3]
                for c in range(3)
            ]
            for r in range(3)
        ]
        volume = deform[0][0] * cof[0][0] + deform[0][1] * cof[0][1] + deform[0][2] * cof[0][2]
        inverse = 1.0 / volume
        scaled = occ * (1.0 / (16.0 * SIGMA))
        values = [cof[r][c] * inverse for r in range(3) for c in range(3)]
        values.append(scaled * (SHEAR - LAME * jnp.log(volume)))
        values.append(scaled)
        values.append(scaled * (SHEAR + level))
        quarter = 0.25 * occ
        values += [quarter * deform[r][0] for r in range(3)]
        for i, value in enumerate(values):
            terms[(i, q, *part(k))] = value


def row_rate(grad, terms, works, step, q, keys=ALL):
    rate = [[{} for _ in range(3)] for _ in range(3)]
    for k in keys:

        def term(i):
            return terms[(i, q, *part(k))]

        g = [[grad[r][c][k] for c in range(3)] for r in range(3)]
        inv_t = [[term(3 * r + c) for c in range(3)] for r in range(3)]
        shear, occ, fibre = term(9), term(10), term(11)
        pulled = [
            [
                inv_t[0][a] * g[0][b] + inv_t[1][a] * g[1][b] + inv_t[2][a] * g[2][b]
                for b in range(3)
            ]
            for a in range(3)
        ]
        spread = (LAME * occ) * (pulled[0][0] + pulled[1][1] + pulled[2][2])
        z = [
            [shear * pulled[c][m] + spread if c == m else shear * pulled[c][m] for c in range(3)]
            for m in range(3)
        ]
        for r in range(3):
            for c in range(3):
                rate[r][c][k] = (
                    (fibre if c == 0 else occ) * g[r][c]
                    + inv_t[r][0] * z[0][c]
                    + inv_t[r][1] * z[1][c]
                    + inv_t[r][2] * z[2][c]
                )
        if k in OWN:
            works[(step, q, *part(k))] = (
                term(12) * g[0][0] + term(13) * g[1][0] + term(14) * g[2][0]
            )
    return rate


def row_force(sh, before, rate, comp):
    p = add(before[comp][0], rate[comp][0])
    a = sub(before[comp][1], rate[comp][1])
    b = add(before[comp][2], rate[comp][2])
    along = add(p, sh.zdown(p))
    across = add(sh.zdown(add(a, b)), sub(a, b))
    return add(sh.xdown(add(along, across)), sub(across, along))


def load_rate(ref, *index):
    return [[get(ref, *index, 3 * r + c) for c in range(3)] for r in range(3)]


def save_rate(ref, rate, *index):
    for r in range(3):
        for c in range(3):
            put(ref, rate[r][c], *index, 3 * r + c)


class Sweep:
    def __init__(self, axes, rows, ext, fields, terms, works, last):
        self.sh = Shifts()
        self.ext, self.fields, self.terms, self.works, self.last = ext, fields, terms, works, last
        ends = [lax.axis_index(axis) == lax.axis_size(axis) - 1 for axis in axes]
        self.top_y = jnp.where(ends[0], LOW + rows, -1)
        top_z = jnp.where(ends[1], SUB, -1)
        self.keep_z = {k: jnp.where(self.sh.sub + SUB * k[0] == top_z, 0.0, 1.0) for k in ALL}

    def read(self, step):
        if step == 0:
            return lambda comp, q: get(self.ext, 3 + comp, q)
        return lambda comp, q: get(self.fields, step - 1, comp, q)

    def rate(self, step, q):
        if step == 0:
            row_terms(self.sh, self.ext, self.terms, q)
        grad = raw_gradient(self.sh, self.read(step), q)
        return row_rate(grad, self.terms, self.works, step, q)

    def node(self, step, q, rate):
        before = load_rate(self.last)
        keep_y = jnp.where(q == self.top_y, 0.0, 1.0)
        for comp in range(3):
            force = row_force(self.sh, before, rate, comp)
            if SHIFTS[step] != 0.0:
                here = self.read(step)(comp, q)
                force = {k: force[k] - (SHIFTS[step] / SIGMA) * here[k] for k in ALL}
            put(
                self.fields,
                {k: force[k] * (self.keep_z[k] * keep_y) for k in ALL},
                step,
                comp,
                q,
            )

    def rows(self, step, start, stop):
        def body(q, carry):
            rate = self.rate(step, q)
            self.node(step, q, rate)
            save_rate(self.last, rate)
            return carry

        lax.fori_loop(start, stop, body, 0)


def even(axis):
    return lax.rem(lax.axis_index(axis), 2) == 0


def pack_kernel(
    axes,
    disp_hbm,
    load_hbm,
    occ_hbm,
    group_hbm,
    act_hbm,
    block_ref,
    zpair_ref,
    znext_ref,
    ypair_ref,
    ynext_ref,
    group_ref,
    disp_ref,
    load_ref,
    occ_ref,
    act_ref,
    sems,
):
    copies = [
        pltpu.make_async_copy(source, target, sems.at[i])
        for i, (source, target) in enumerate(
            (
                (act_hbm, act_ref),
                (group_hbm, group_ref),
                (occ_hbm, occ_ref),
                (disp_hbm, disp_ref),
                (load_hbm, load_ref),
            )
        )
    ]
    for copy in copies:
        copy.start()
    rows, cols, depth = occ_ref.shape
    muscles = act_ref.shape[0]
    even_y, even_z = even(axes[0]), even(axes[1])
    for copy in copies:
        copy.wait()

    def row(y, carry):
        group = group_ref[y]
        level = jnp.zeros((cols, depth), jnp.float32)
        for m in range(muscles):
            level = jnp.where(group == m, act_ref[m], level)
        values = [disp_ref[c, y] for c in range(3)] + [load_ref[c, y] for c in range(3)]
        values += [occ_ref[y].astype(jnp.float32), level]
        for c, value in enumerate(values):
            block_ref[c, y] = value
            bottom, top = value[:HIGH], value[cols - HIGH :]
            zpair_ref[c, y] = jnp.where(even_z, top, bottom)
            znext_ref[c, y] = jnp.where(even_z, bottom, top)
        return carry

    lax.fori_loop(0, rows, row, 0)
    send_rows(block_ref, ypair_ref, ynext_ref, even_y)


def send_rows(block_ref, pair_ref, next_ref, is_even):
    rows = block_ref.shape[1]
    pair_at = jnp.where(is_even, rows - HIGH, 0)

    def channel(c, carry):
        for y in range(HIGH):
            pair_ref[c, y] = block_ref[c, pair_at + y]
            next_ref[c, y] = block_ref[c, rows - HIGH - pair_at + y]
        return carry

    lax.fori_loop(0, CHANNELS, channel, 0)


def corner_kernel(axes, zpair_ref, znext_ref, around_ref, ypair_ref, ynext_ref):
    even_y, even_z = even(axes[0]), even(axes[1])

    def channel(c, carry):
        for y in range(around_ref.shape[1]):
            pair, far = zpair_ref[c, y], znext_ref[c, y]
            around_ref[c, y, pl.ds(0, HIGH), :] = jnp.where(even_z, pair, far)
            around_ref[c, y, pl.ds(HIGH, HIGH), :] = jnp.where(even_z, far, pair)
        return carry

    lax.fori_loop(0, CHANNELS, channel, 0)
    send_rows(around_ref, ypair_ref, ynext_ref, even_y)


def inner_kernel(axes, block_ref, around_ref, ext, fields, terms, works, edge, last):
    rows = block_ref.shape[1]

    def assemble(c, carry):
        for y in range(rows):
            ext[c, LOW + y, pl.ds(0, SUB), :] = block_ref[c, y]
            ext[c, LOW + y, pl.ds(SUB, SUB), :] = around_ref[c, y]
        return carry

    lax.fori_loop(0, CHANNELS, assemble, 0)
    sweep = Sweep(axes, rows, ext, fields, terms, works, last)
    for step in range(NB - 1):
        first, final = LOW + step, LOW + rows - 2 - step
        rate = sweep.rate(step, first)
        save_rate(last, rate)
        save_rate(edge, rate, step, 0)
        sweep.rows(step, first + 1, final + 1)
        save_rate(edge, load_rate(last), step, 1)


def outer_kernel(
    axes,
    group_ref,
    ynext_ref,
    ypair_ref,
    cnext_ref,
    cpair_ref,
    ext_in,
    fields_in,
    terms_in,
    works_in,
    edge,
    sums_ref,
    ext,
    fields,
    terms,
    works,
    last,
    table,
):
    del ext_in, fields_in, terms_in, works_in
    rows = group_ref.shape[0]
    even_y = even(axes[0])

    def assemble(c, carry):
        for zt, pair_ref, next_ref in ((0, ypair_ref, ynext_ref), (1, cpair_ref, cnext_ref)):
            for y in range(HIGH):
                pair, far = pair_ref[c, y], next_ref[c, y]
                ext[c, LOW + rows + y, pl.ds(SUB * zt, SUB), :] = jnp.where(even_y, pair, far)
                if y >= HIGH - LOW:
                    ext[c, y - HIGH + LOW, pl.ds(SUB * zt, SUB), :] = jnp.where(even_y, far, pair)
        return carry

    lax.fori_loop(0, CHANNELS, assemble, 0)
    sweep = Sweep(axes, rows, ext, fields, terms, works, last)
    for step in range(NB - 1):
        save_rate(last, sweep.rate(step, step))
        sweep.rows(step, step + 1, LOW + step)
        sweep.node(step, LOW + step, load_rate(edge, step, 0))
        save_rate(last, load_rate(edge, step, 1))
        sweep.rows(step, LOW + rows - 1 - step, LOW + rows + HIGH - 1 - step)

    zero = jnp.zeros((SUB, LANES), jnp.float32)
    pairs = [(i, j) for i in range(NB) for j in range(i, NB)]

    def finish(q, acc):
        acc = list(acc)
        grad = raw_gradient(sweep.sh, sweep.read(NB - 1), q, OWN)
        rate = row_rate(grad, terms, works, NB - 1, q, OWN)
        for k in OWN:
            for r in range(3):
                for c in range(3):
                    acc[-1] = acc[-1] + rate[r][c][k] * grad[r][c][k]
            for comp in range(3):
                vectors = [ext[(3 + comp, q, *part(k))]]
                vectors += [fields[(s, comp, q, *part(k))] for s in range(NB - 1)]
                for n, (i, j) in enumerate(pairs):
                    acc[n] = acc[n] + vectors[i] * vectors[j]
        return tuple(acc)

    acc = lax.fori_loop(LOW, LOW + rows, finish, tuple(zero for _ in range(len(pairs) + 1)))
    table[...] = jnp.zeros_like(table)
    muscles = (table.shape[0] // 2) // NB
    for n, value in enumerate(acc):
        table[pl.ds(NB * muscles + n, 1), :] = jnp.sum(value, axis=0, keepdims=True)

    def muscle(m, carry):
        total = [zero] * NB
        for y in range(rows):
            for h in range(2):
                mine = group_ref[y, :, pl.ds(LANES * h, LANES)] == m
                for step in range(NB):
                    total[step] = total[step] + jnp.where(
                        mine, works[(step, LOW + y, *part((0, h)))], 0.0
                    )
        for step in range(NB):
            table[pl.ds(step * muscles + m, 1), :] = jnp.sum(total[step], axis=0, keepdims=True)
        return carry

    lax.fori_loop(0, muscles, muscle, 0)
    row = lax.dot_general(
        jnp.ones((SUB, LANES), jnp.float32),
        table[...],
        (((1,), (1,)), ((), ())),
        precision=lax.Precision.HIGHEST,
        preferred_element_type=jnp.float32,
    )
    is_first = lax.rem(sweep.sh.sub, 2) == 0
    message = jnp.where(is_first, row[:, :LANES], row[:, LANES:])
    for i in range(sums_ref.shape[0] // SUB):
        sums_ref[pl.ds(SUB * i, SUB), :] = message


def combine_kernel(muscles, scale, sums_ref, block_ref, fields, x_hbm, grad_hbm, x_ref, grad_ref, sems):
    parts = [sums_ref[pl.ds(SUB * i, SUB), :] for i in range(sums_ref.shape[0] // SUB)]
    while len(parts) > 1:
        odd = parts[len(parts) // 2 * 2 :]
        parts = [a + b for a, b in zip(parts[0::2], parts[1::2])] + odd
    total = parts[0]
    is_first = lax.rem(lax.broadcasted_iota(jnp.int32, total.shape, 0), 2) == 0
    works = jnp.sum(jnp.where(is_first, total, 0.0), axis=0, keepdims=True)
    dots = jnp.sum(jnp.where(is_first, 0.0, total), axis=0, keepdims=True)
    pairs = [(i, j) for i in range(NB) for j in range(i, NB)]
    gram = {}
    for n, (i, j) in enumerate(pairs):
        gram[i, j] = gram[j, i] = dots[:, n : n + 1]
    energy = dots[:, len(pairs) : len(pairs) + 1]
    shifts = [MASS + s for s in SHIFTS]
    form = {}
    for j in range(NB - 1):
        for i in range(j + 1):
            form[i, j] = form[j, i] = SIGMA * gram[i, j + 1] + shifts[j] * gram[i, j]
    last = NB - 1
    for i in range(last):
        form[i, last] = form[last, i] = SIGMA * gram[i + 1, last] + shifts[i] * gram[i, last]
    form[last, last] = SIGMA * energy + MASS * gram[last, last]

    rhs = [gram[0, i] for i in range(NB)]
    inverse = []
    for k in range(NB):
        inverse.append(1.0 / form[k, k])
        for i in range(k + 1, NB):
            factor = form[k, i] * inverse[k]
            rhs[i] = rhs[i] - factor * rhs[k]
            for j in range(i, NB):
                form[i, j] = form[i, j] - factor * form[k, j]
    x = [None] * NB
    for k in reversed(range(NB)):
        value = rhs[k]
        for j in range(k + 1, NB):
            value = value - form[k, j] * x[j]
        x[k] = value * inverse[k]

    grad = None
    for k in range(NB):
        part = x[k] * works[:, k * muscles : (k + 1) * muscles]
        grad = part if grad is None else grad + part
    grad_ref[...] = -scale * grad
    copies = [pltpu.make_async_copy(grad_ref, grad_hbm, sems.at[3])]
    copies[0].start()

    width = block_ref.shape[-1]
    coef = [jnp.broadcast_to(x[k], (SUB, width)) for k in range(NB)]
    for comp in range(3):
        for y in range(block_ref.shape[1]):
            value = coef[0] * block_ref[3 + comp, y]
            for k in range(1, NB):
                value = value + coef[k] * fields[k - 1, comp, LOW + y, pl.ds(0, SUB), :]
            x_ref[comp, y] = value
        copies.append(pltpu.make_async_copy(x_ref.at[comp], x_hbm.at[comp], sems.at[comp]))
        copies[-1].start()
    for copy in copies:
        copy.wait()


def swap(shard, axis, first):
    length = lax.axis_size(axis)
    pairs = [(i, i + 1) for i in range(first, length - 1, 2)]
    return lax.ppermute(shard, axis, pairs + [(j, i) for i, j in pairs])


def per_device(displacement, load, occupancy, voxel_muscle_group, activation):
    rows, cols, depth = occupancy.shape
    muscles = activation.shape[0]
    axes = ("gy", "gz")
    count = LOW + rows + HIGH

    def arr(*shape):
        return jax.ShapeDtypeStruct(shape, jnp.float32)

    anywhere = pl.BlockSpec(memory_space=pltpu.HBM)
    faces = (arr(CHANNELS, rows, HIGH, depth),) * 2
    edges = (arr(CHANNELS, HIGH, cols, depth),) * 2
    block, zpair, znext, ypair, ynext, group = pl.pallas_call(
        functools.partial(pack_kernel, axes),
        out_shape=(
            arr(CHANNELS, rows, cols, depth),
            *faces,
            *edges,
            jax.ShapeDtypeStruct(occupancy.shape, jnp.int32),
        ),
        in_specs=[anywhere] * 5,
        out_specs=(VMEM,) * 6,
        scratch_shapes=[
            pltpu.VMEM(displacement.shape, jnp.float32),
            pltpu.VMEM(load.shape, jnp.float32),
            pltpu.VMEM(occupancy.shape, jnp.int32),
            pltpu.SMEM((muscles,), jnp.float32),
            pltpu.SemaphoreType.DMA((5,)),
        ],
        compiler_params=pltpu.CompilerParams(vmem_limit_bytes=32 << 20),
        name="pack",
    )(
        *(
            pltpu.with_memory_space_constraint(value, pltpu.HBM)
            for value in (displacement, load, occupancy, voxel_muscle_group, activation)
        )
    )

    received = [
        swap(znext, "gz", 1),
        swap(zpair, "gz", 0),
        swap(ynext, "gy", 1),
        swap(ypair, "gy", 0),
    ]
    znext, zpair, ynext, ypair = received
    znext, zpair = lax.optimization_barrier((znext, zpair))
    around, cpair, cnext = pl.pallas_call(
        functools.partial(corner_kernel, axes),
        out_shape=(arr(CHANNELS, rows, 2 * HIGH, depth), *edges),
        in_specs=[VMEM] * 2,
        out_specs=(VMEM,) * 3,
        compiler_params=pltpu.CompilerParams(vmem_limit_bytes=32 << 20),
        name="corner",
    )(zpair, znext)
    cnext = swap(cnext, "gy", 1)
    cpair = swap(cpair, "gy", 0)

    state = (
        arr(CHANNELS, count, 2 * SUB, depth),
        arr(NB - 1, 3, count, 2 * SUB, depth),
        arr(TERMS, count - 1, 2 * SUB, depth),
        arr(NB, count - 1, SUB, depth),
    )
    kept = pltpu.VMEM((9, 2 * SUB, depth), jnp.float32)
    inner = pl.pallas_call(
        functools.partial(inner_kernel, axes),
        out_shape=(*state, arr(NB - 1, 2, 9, 2 * SUB, depth)),
        in_specs=[VMEM] * 2,
        out_specs=(VMEM,) * 5,
        scratch_shapes=[kept],
        compiler_params=pltpu.CompilerParams(vmem_limit_bytes=32 << 20),
        name="inner",
    )(block, around)

    devices = lax.axis_size("gy") * lax.axis_size("gz")
    sums, _, fields, _, _ = pl.pallas_call(
        functools.partial(outer_kernel, axes),
        out_shape=(arr(2 * devices, LANES), *state),
        in_specs=[VMEM] * 10,
        out_specs=(VMEM,) * 5,
        scratch_shapes=[kept, pltpu.VMEM((2 * NB * muscles, LANES), jnp.float32)],
        input_output_aliases={5: 1, 6: 2, 7: 3, 8: 4},
        compiler_params=pltpu.CompilerParams(vmem_limit_bytes=32 << 20),
        name="outer",
    )(group, ynext, ypair, cnext, cpair, *inner)

    every = lax.all_to_all(sums, ("gy", "gz"), 0, 0, tiled=True)

    cells = depth * rows * lax.axis_size("gy") * cols * lax.axis_size("gz")
    scale = 1.0 / math.sqrt(cells / muscles)
    adjoint, muscle_grad = pl.pallas_call(
        functools.partial(combine_kernel, muscles, scale),
        out_shape=(
            jax.ShapeDtypeStruct(load.shape, jnp.float32),
            jax.ShapeDtypeStruct((1, muscles), jnp.float32),
        ),
        in_specs=[VMEM] * 3,
        out_specs=(anywhere, anywhere),
        scratch_shapes=[
            pltpu.VMEM(load.shape, jnp.float32),
            pltpu.VMEM((1, muscles), jnp.float32),
            pltpu.SemaphoreType.DMA((4,)),
        ],
        compiler_params=pltpu.CompilerParams(vmem_limit_bytes=32 << 20),
        name="combine",
    )(every, block, fields)
    return adjoint, muscle_grad.reshape(muscles)


def solution(mesh):
    placed = (
        P(None, "gy", "gz", None),
        P(None, "gy", "gz", None),
        P("gy", "gz", None),
        P("gy", "gz", None),
        P(),
    )
    return jax.shard_map(
        per_device,
        mesh=mesh,
        in_specs=placed,
        out_specs=(P(None, "gy", "gz", None), P()),
        check_vma=False,
    )
```

```python
import functools
import math

import jax
import jax.numpy as jnp
from jax import lax
from jax.experimental import pallas as pl
from jax.experimental.pallas import tpu as pltpu
from jax.sharding import PartitionSpec as P

SHEAR = 1.0
LAME = 4.0
MASS = 0.05

LOW, HIGH = 3, 4
SIGMA = 16.0
SHIFTS = (0.0, 9.95, 1.95)
NB = 4
LANES = 128
SUB = 8
CHANNELS = 8
TERMS = 15
ALL = tuple((zt, h) for zt in range(2) for h in range(2))
OWN = ((0, 0), (0, 1))
VMEM = pl.BlockSpec(memory_space=pltpu.VMEM)


class Shifts:
    def __init__(self):
        lane = lax.broadcasted_iota(jnp.int32, (SUB, LANES), 1)
        self.sub = lax.broadcasted_iota(jnp.int32, (SUB, LANES), 0)
        self.last_lane = lane == LANES - 1
        self.first_lane = lane == 0
        self.last_sub = self.sub == SUB - 1
        self.first_sub = self.sub == 0

    def xup(self, v):
        out = {}
        for zt in {zt for zt, _ in v}:
            r0 = pltpu.roll(v[zt, 0], LANES - 1, 1)
            r1 = pltpu.roll(v[zt, 1], LANES - 1, 1)
            out[zt, 0] = jnp.where(self.last_lane, r1, r0)
            out[zt, 1] = jnp.where(self.last_lane, 0.0, r1)
        return out

    def xdown(self, v):
        out = {}
        for zt in {zt for zt, _ in v}:
            r0 = pltpu.roll(v[zt, 0], 1, 1)
            r1 = pltpu.roll(v[zt, 1], 1, 1)
            out[zt, 0] = jnp.where(self.first_lane, 0.0, r0)
            out[zt, 1] = jnp.where(self.first_lane, r0, r1)
        return out

    def zup(self, v, keys):
        out = {}
        for h in range(2):
            r0 = pltpu.roll(v[0, h], SUB - 1, 0)
            r1 = pltpu.roll(v[1, h], SUB - 1, 0)
            out[0, h] = jnp.where(self.last_sub, r1, r0)
            if (1, h) in keys:
                out[1, h] = jnp.where(self.last_sub, r0, r1)
        return out

    def zdown(self, v):
        out = {}
        for h in range(2):
            r0 = pltpu.roll(v[0, h], 1, 0)
            r1 = pltpu.roll(v[1, h], 1, 0)
            out[0, h] = jnp.where(self.first_sub, r1, r0)
            out[1, h] = jnp.where(self.first_sub, r0, r1)
        return out


def part(k):
    return pl.ds(SUB * k[0], SUB), pl.ds(LANES * k[1], LANES)


def get(ref, *index):
    return {k: ref[(*index, *part(k))] for k in ALL}


def put(ref, value, *index):
    for k in value:
        ref[(*index, *part(k))] = value[k]


def add(a, b):
    return {k: a[k] + b[k] for k in a}


def sub(a, b):
    return {k: a[k] - b[k] for k in a}


def raw_gradient(sh, read, q, keys=ALL, cache=None):
    def level(comp, at):
        if cache is not None and (comp, at) in cache:
            return cache[comp, at]
        value = read(comp, at)
        value_x = sh.xup(value)
        wide, slope = add(value, value_x), sub(value_x, value)
        wide_z, slope_z = sh.zup(wide, keys), sh.zup(slope, keys)
        out = (
            {k: slope[k] + slope_z[k] for k in keys},
            {k: wide[k] + wide_z[k] for k in keys},
            {k: wide_z[k] - wide[k] for k in keys},
        )
        if cache is not None:
            cache[comp, at] = out
        return out

    result = []
    for comp in range(3):
        here, above = level(comp, q), level(comp, q + 1)
        result.append((add(here[0], above[0]), sub(above[1], here[1]), add(here[2], above[2])))
    return result


def row_terms(sh, ext, terms, q, cache):
    grad = raw_gradient(sh, lambda comp, at: get(ext, comp, at), q, ALL, cache)
    for k in ALL:
        occ, level = ext[(6, q, *part(k))], ext[(7, q, *part(k))]
        deform = [
            [0.25 * grad[r][c][k] + (1.0 if r == c else 0.0) for c in range(3)] for r in range(3)
        ]
        cof = [
            [
                deform[(r + 1) % 3][(c + 1) % 3] * deform[(r + 2) % 3][(c + 2) % 3]
                - deform[(r + 1) % 3][(c + 2) % 3] * deform[(r + 2) % 3][(c + 1) % 3]
                for c in range(3)
            ]
            for r in range(3)
        ]
        volume = deform[0][0] * cof[0][0] + deform[0][1] * cof[0][1] + deform[0][2] * cof[0][2]
        inverse = 1.0 / volume
        scaled = occ * (1.0 / (16.0 * SIGMA))
        values = [cof[r][c] * inverse for r in range(3) for c in range(3)]
        values.append(scaled * (SHEAR - LAME * jnp.log(volume)))
        values.append(scaled)
        values.append(scaled * (SHEAR + level))
        quarter = 0.25 * occ
        values += [quarter * deform[r][0] for r in range(3)]
        for i, value in enumerate(values):
            terms[(i, q, *part(k))] = value


def row_rate(grad, terms, works, step, q, keys=ALL):
    rate = [[{} for _ in range(3)] for _ in range(3)]
    for k in keys:

        def term(i):
            return terms[(i, q, *part(k))]

        g = [[grad[r][c][k] for c in range(3)] for r in range(3)]
        inv_t = [[term(3 * r + c) for c in range(3)] for r in range(3)]
        shear, occ, fibre = term(9), term(10), term(11)
        pulled = [
            [
                inv_t[0][a] * g[0][b] + inv_t[1][a] * g[1][b] + inv_t[2][a] * g[2][b]
                for b in range(3)
            ]
            for a in range(3)
        ]
        spread = (LAME * occ) * (pulled[0][0] + pulled[1][1] + pulled[2][2])
        z = [
            [shear * pulled[c][m] + spread if c == m else shear * pulled[c][m] for c in range(3)]
            for m in range(3)
        ]
        for r in range(3):
            for c in range(3):
                rate[r][c][k] = (
                    (fibre if c == 0 else occ) * g[r][c]
                    + inv_t[r][0] * z[0][c]
                    + inv_t[r][1] * z[1][c]
                    + inv_t[r][2] * z[2][c]
                )
        if k in OWN:
            works[(step, q, *part(k))] = (
                term(12) * g[0][0] + term(13) * g[1][0] + term(14) * g[2][0]
            )
    return rate


def row_force(sh, before, rate, comp):
    p = add(before[comp][0], rate[comp][0])
    a = sub(before[comp][1], rate[comp][1])
    b = add(before[comp][2], rate[comp][2])
    along = add(p, sh.zdown(p))
    across = add(sh.zdown(add(a, b)), sub(a, b))
    return add(sh.xdown(add(along, across)), sub(across, along))


def load_rate(ref, *index):
    return [[get(ref, *index, 3 * r + c) for c in range(3)] for r in range(3)]


def save_rate(ref, rate, *index):
    for r in range(3):
        for c in range(3):
            put(ref, rate[r][c], *index, 3 * r + c)


class Sweep:
    def __init__(self, axes, rows, ext, fields, terms, works):
        self.sh = Shifts()
        self.ext, self.fields, self.terms, self.works = ext, fields, terms, works
        ends = [lax.axis_index(axis) == lax.axis_size(axis) - 1 for axis in axes]
        self.top = LOW + rows
        self.cache = {i: {} for i in range(-1, NB)}
        self.keep_y = jnp.where(ends[0], 0.0, 1.0)
        top_z = jnp.where(ends[1], SUB, -1)
        self.keep_z = {k: jnp.where(self.sh.sub + SUB * k[0] == top_z, 0.0, 1.0) for k in ALL}

    def read(self, step):
        if step == 0:
            return lambda comp, q: get(self.ext, 3 + comp, q)
        return lambda comp, q: get(self.fields, step - 1, comp, q)

    def rate(self, step, q):
        if step == 0:
            row_terms(self.sh, self.ext, self.terms, q, self.cache[-1])
        grad = raw_gradient(self.sh, self.read(step), q, ALL, self.cache[step])
        return row_rate(grad, self.terms, self.works, step, q)

    def node(self, step, q, before, rate):
        for comp in range(3):
            force = row_force(self.sh, before, rate, comp)
            if SHIFTS[step] != 0.0:
                here = self.read(step)(comp, q)
                force = {k: force[k] - (SHIFTS[step] / SIGMA) * here[k] for k in ALL}
            if q == self.top:
                force = {k: force[k] * self.keep_y for k in ALL}
            force = {k: force[k] * self.keep_z[k] if k[0] else force[k] for k in ALL}
            put(self.fields, force, step, comp, q)

    def rows(self, step, start, stop, before):
        for q in range(start, stop):
            rate = self.rate(step, q)
            self.node(step, q, before, rate)
            before = rate
        return before


def even(axis):
    return lax.rem(lax.axis_index(axis), 2) == 0


def pack_kernel(
    axes,
    disp_hbm,
    load_hbm,
    occ_hbm,
    group_hbm,
    act_hbm,
    block_ref,
    zpair_ref,
    znext_ref,
    ypair_ref,
    ynext_ref,
    group_ref,
    disp_ref,
    load_ref,
    occ_ref,
    act_ref,
    sems,
):
    copies = [
        pltpu.make_async_copy(source, target, sems.at[i])
        for i, (source, target) in enumerate(
            (
                (act_hbm, act_ref),
                (group_hbm, group_ref),
                (occ_hbm, occ_ref),
                (disp_hbm, disp_ref),
                (load_hbm, load_ref),
            )
        )
    ]
    for copy in copies:
        copy.start()
    rows, cols, depth = occ_ref.shape
    muscles = act_ref.shape[0]
    even_y, even_z = even(axes[0]), even(axes[1])
    for copy in copies:
        copy.wait()

    def row(y, carry):
        group = group_ref[y]
        level = jnp.zeros((cols, depth), jnp.float32)
        for m in range(muscles):
            level = jnp.where(group == m, act_ref[m], level)
        values = [disp_ref[c, y] for c in range(3)] + [load_ref[c, y] for c in range(3)]
        values += [occ_ref[y].astype(jnp.float32), level]
        for c, value in enumerate(values):
            block_ref[c, y] = value
            bottom, top = value[:HIGH], value[cols - HIGH :]
            zpair_ref[c, y] = jnp.where(even_z, top, bottom)
            znext_ref[c, y] = jnp.where(even_z, bottom, top)
        return carry

    lax.fori_loop(0, rows, row, 0)
    send_rows(block_ref, ypair_ref, ynext_ref, even_y)


def send_rows(block_ref, pair_ref, next_ref, is_even):
    rows = block_ref.shape[1]
    pair_at = jnp.where(is_even, rows - HIGH, 0)

    def channel(c, carry):
        for y in range(HIGH):
            pair_ref[c, y] = block_ref[c, pair_at + y]
            next_ref[c, y] = block_ref[c, rows - HIGH - pair_at + y]
        return carry

    lax.fori_loop(0, CHANNELS, channel, 0)


def corner_kernel(axes, zpair_ref, znext_ref, around_ref, ypair_ref, ynext_ref):
    even_y, even_z = even(axes[0]), even(axes[1])

    def channel(c, carry):
        for y in range(around_ref.shape[1]):
            pair, far = zpair_ref[c, y], znext_ref[c, y]
            around_ref[c, y, pl.ds(0, HIGH), :] = jnp.where(even_z, pair, far)
            around_ref[c, y, pl.ds(HIGH, HIGH), :] = jnp.where(even_z, far, pair)
        return carry

    lax.fori_loop(0, CHANNELS, channel, 0)
    send_rows(around_ref, ypair_ref, ynext_ref, even_y)


def inner_kernel(axes, block_ref, around_ref, ext, fields, terms, works, edge):
    rows = block_ref.shape[1]

    def assemble(c, carry):
        for y in range(rows):
            ext[c, LOW + y, pl.ds(0, SUB), :] = block_ref[c, y]
            ext[c, LOW + y, pl.ds(SUB, SUB), :] = around_ref[c, y]
        return carry

    lax.fori_loop(0, CHANNELS, assemble, 0)
    sweep = Sweep(axes, rows, ext, fields, terms, works)
    for step in range(NB - 1):
        first, final = LOW + step, LOW + rows - 2 - step
        rate = sweep.rate(step, first)
        save_rate(edge, rate, step, 0)
        save_rate(edge, sweep.rows(step, first + 1, final + 1, rate), step, 1)


def outer_kernel(
    axes,
    group_ref,
    ynext_ref,
    ypair_ref,
    cnext_ref,
    cpair_ref,
    ext_in,
    fields_in,
    terms_in,
    works_in,
    edge,
    sums_ref,
    ext,
    fields,
    terms,
    works,
    table,
):
    del ext_in, fields_in, terms_in, works_in
    rows = group_ref.shape[0]
    even_y = even(axes[0])

    def assemble(c, carry):
        for zt, pair_ref, next_ref in ((0, ypair_ref, ynext_ref), (1, cpair_ref, cnext_ref)):
            for y in range(HIGH):
                pair, far = pair_ref[c, y], next_ref[c, y]
                ext[c, LOW + rows + y, pl.ds(SUB * zt, SUB), :] = jnp.where(even_y, pair, far)
                if y >= HIGH - LOW:
                    ext[c, y - HIGH + LOW, pl.ds(SUB * zt, SUB), :] = jnp.where(even_y, far, pair)
        return carry

    lax.fori_loop(0, CHANNELS, assemble, 0)
    sweep = Sweep(axes, rows, ext, fields, terms, works)
    for step in range(NB - 1):
        low = sweep.rows(step, step + 1, LOW + step, sweep.rate(step, step))
        sweep.node(step, LOW + step, low, load_rate(edge, step, 0))
        final = LOW + rows - 2 - step
        sweep.rows(step, final + 1, final + 1 + HIGH, load_rate(edge, step, 1))

    zero = jnp.zeros((SUB, LANES), jnp.float32)
    pairs = [(i, j) for i in range(NB) for j in range(i, NB)]

    def finish(q, acc):
        acc = list(acc)
        grad = raw_gradient(sweep.sh, sweep.read(NB - 1), q, OWN, sweep.cache[NB - 1])
        rate = row_rate(grad, terms, works, NB - 1, q, OWN)
        for k in OWN:
            for r in range(3):
                for c in range(3):
                    acc[-1] = acc[-1] + rate[r][c][k] * grad[r][c][k]
            for comp in range(3):
                vectors = [ext[(3 + comp, q, *part(k))]]
                vectors += [fields[(s, comp, q, *part(k))] for s in range(NB - 1)]
                for n, (i, j) in enumerate(pairs):
                    acc[n] = acc[n] + vectors[i] * vectors[j]
        return tuple(acc)

    acc = tuple(zero for _ in range(len(pairs) + 1))
    for q in range(LOW, LOW + rows):
        acc = finish(q, acc)
    table[...] = jnp.zeros_like(table)
    muscles = (table.shape[0] // 2) // NB
    for n, value in enumerate(acc):
        table[pl.ds(NB * muscles + n, 1), :] = jnp.sum(value, axis=0, keepdims=True)

    def muscle(m, carry):
        total = [zero] * NB
        for y in range(rows):
            for h in range(2):
                mine = group_ref[y, :, pl.ds(LANES * h, LANES)] == m
                for step in range(NB):
                    total[step] = total[step] + jnp.where(
                        mine, works[(step, LOW + y, *part((0, h)))], 0.0
                    )
        for step in range(NB):
            table[pl.ds(step * muscles + m, 1), :] = jnp.sum(total[step], axis=0, keepdims=True)
        return carry

    lax.fori_loop(0, muscles, muscle, 0, unroll=4)
    row = lax.dot_general(
        jnp.ones((SUB, LANES), jnp.float32),
        table[...],
        (((1,), (1,)), ((), ())),
        precision=lax.Precision.HIGHEST,
        preferred_element_type=jnp.float32,
    )
    is_first = lax.rem(sweep.sh.sub, 2) == 0
    message = jnp.where(is_first, row[:, :LANES], row[:, LANES:])
    for i in range(sums_ref.shape[0] // SUB):
        sums_ref[pl.ds(SUB * i, SUB), :] = message


def combine_kernel(muscles, scale, sums_ref, block_ref, fields, x_hbm, grad_hbm, x_ref, grad_ref, sems):
    parts = [sums_ref[pl.ds(SUB * i, SUB), :] for i in range(sums_ref.shape[0] // SUB)]
    while len(parts) > 1:
        odd = parts[len(parts) // 2 * 2 :]
        parts = [a + b for a, b in zip(parts[0::2], parts[1::2])] + odd
    total = parts[0]
    is_first = lax.rem(lax.broadcasted_iota(jnp.int32, total.shape, 0), 2) == 0
    works = jnp.sum(jnp.where(is_first, total, 0.0), axis=0, keepdims=True)
    dots = jnp.sum(jnp.where(is_first, 0.0, total), axis=0, keepdims=True)
    pairs = [(i, j) for i in range(NB) for j in range(i, NB)]
    gram = {}
    for n, (i, j) in enumerate(pairs):
        gram[i, j] = gram[j, i] = dots[:, n : n + 1]
    energy = dots[:, len(pairs) : len(pairs) + 1]
    shifts = [MASS + s for s in SHIFTS]
    form = {}
    for j in range(NB - 1):
        for i in range(j + 1):
            form[i, j] = form[j, i] = SIGMA * gram[i, j + 1] + shifts[j] * gram[i, j]
    last = NB - 1
    for i in range(last):
        form[i, last] = form[last, i] = SIGMA * gram[i + 1, last] + shifts[i] * gram[i, last]
    form[last, last] = SIGMA * energy + MASS * gram[last, last]

    rhs = [gram[0, i] for i in range(NB)]
    inverse = []
    for k in range(NB):
        inverse.append(1.0 / form[k, k])
        for i in range(k + 1, NB):
            factor = form[k, i] * inverse[k]
            rhs[i] = rhs[i] - factor * rhs[k]
            for j in range(i, NB):
                form[i, j] = form[i, j] - factor * form[k, j]
    x = [None] * NB
    for k in reversed(range(NB)):
        value = rhs[k]
        for j in range(k + 1, NB):
            value = value - form[k, j] * x[j]
        x[k] = value * inverse[k]

    grad = None
    for k in range(NB):
        part = x[k] * works[:, k * muscles : (k + 1) * muscles]
        grad = part if grad is None else grad + part
    grad_ref[...] = -scale * grad
    copies = [pltpu.make_async_copy(grad_ref, grad_hbm, sems.at[3])]
    copies[0].start()

    width = block_ref.shape[-1]
    coef = [jnp.broadcast_to(x[k], (SUB, width)) for k in range(NB)]
    for comp in range(3):
        for y in range(block_ref.shape[1]):
            value = coef[0] * block_ref[3 + comp, y]
            for k in range(1, NB):
                value = value + coef[k] * fields[k - 1, comp, LOW + y, pl.ds(0, SUB), :]
            x_ref[comp, y] = value
        copies.append(pltpu.make_async_copy(x_ref.at[comp], x_hbm.at[comp], sems.at[comp]))
        copies[-1].start()
    for copy in copies:
        copy.wait()


def swap(shard, axis, first):
    length = lax.axis_size(axis)
    pairs = [(i, i + 1) for i in range(first, length - 1, 2)]
    return lax.ppermute(shard, axis, pairs + [(j, i) for i, j in pairs])


def per_device(displacement, load, occupancy, voxel_muscle_group, activation):
    rows, cols, depth = occupancy.shape
    muscles = activation.shape[0]
    axes = ("gy", "gz")
    count = LOW + rows + HIGH

    def arr(*shape):
        return jax.ShapeDtypeStruct(shape, jnp.float32)

    anywhere = pl.BlockSpec(memory_space=pltpu.HBM)
    faces = (arr(CHANNELS, rows, HIGH, depth),) * 2
    edges = (arr(CHANNELS, HIGH, cols, depth),) * 2
    block, zpair, znext, ypair, ynext, group = pl.pallas_call(
        functools.partial(pack_kernel, axes),
        out_shape=(
            arr(CHANNELS, rows, cols, depth),
            *faces,
            *edges,
            jax.ShapeDtypeStruct(occupancy.shape, jnp.int32),
        ),
        in_specs=[anywhere] * 5,
        out_specs=(VMEM,) * 6,
        scratch_shapes=[
            pltpu.VMEM(displacement.shape, jnp.float32),
            pltpu.VMEM(load.shape, jnp.float32),
            pltpu.VMEM(occupancy.shape, jnp.int32),
            pltpu.SMEM((muscles,), jnp.float32),
            pltpu.SemaphoreType.DMA((5,)),
        ],
        compiler_params=pltpu.CompilerParams(vmem_limit_bytes=32 << 20),
        name="pack",
    )(
        *(
            pltpu.with_memory_space_constraint(value, pltpu.HBM)
            for value in (displacement, load, occupancy, voxel_muscle_group, activation)
        )
    )

    received = [
        swap(znext, "gz", 1),
        swap(zpair, "gz", 0),
        swap(ynext, "gy", 1),
        swap(ypair, "gy", 0),
    ]
    znext, zpair, ynext, ypair = received
    znext, zpair = lax.optimization_barrier((znext, zpair))
    around, cpair, cnext = pl.pallas_call(
        functools.partial(corner_kernel, axes),
        out_shape=(arr(CHANNELS, rows, 2 * HIGH, depth), *edges),
        in_specs=[VMEM] * 2,
        out_specs=(VMEM,) * 3,
        compiler_params=pltpu.CompilerParams(vmem_limit_bytes=32 << 20),
        name="corner",
    )(zpair, znext)
    cnext = swap(cnext, "gy", 1)
    cpair = swap(cpair, "gy", 0)

    state = (
        arr(CHANNELS, count, 2 * SUB, depth),
        arr(NB - 1, 3, count, 2 * SUB, depth),
        arr(TERMS, count - 1, 2 * SUB, depth),
        arr(NB, count - 1, SUB, depth),
    )
    inner = pl.pallas_call(
        functools.partial(inner_kernel, axes),
        out_shape=(*state, arr(NB - 1, 2, 9, 2 * SUB, depth)),
        in_specs=[VMEM] * 2,
        out_specs=(VMEM,) * 5,
        compiler_params=pltpu.CompilerParams(vmem_limit_bytes=32 << 20),
        name="inner",
    )(block, around)

    devices = lax.axis_size("gy") * lax.axis_size("gz")
    sums, _, fields, _, _ = pl.pallas_call(
        functools.partial(outer_kernel, axes),
        out_shape=(arr(2 * devices, LANES), *state),
        in_specs=[VMEM] * 10,
        out_specs=(VMEM,) * 5,
        scratch_shapes=[pltpu.VMEM((2 * NB * muscles, LANES), jnp.float32)],
        input_output_aliases={5: 1, 6: 2, 7: 3, 8: 4},
        compiler_params=pltpu.CompilerParams(vmem_limit_bytes=32 << 20),
        name="outer",
    )(group, ynext, ypair, cnext, cpair, *inner)

    every = lax.all_to_all(sums, ("gy", "gz"), 0, 0, tiled=True)

    cells = depth * rows * lax.axis_size("gy") * cols * lax.axis_size("gz")
    scale = 1.0 / math.sqrt(cells / muscles)
    adjoint, muscle_grad = pl.pallas_call(
        functools.partial(combine_kernel, muscles, scale),
        out_shape=(
            jax.ShapeDtypeStruct(load.shape, jnp.float32),
            jax.ShapeDtypeStruct((1, muscles), jnp.float32),
        ),
        in_specs=[VMEM] * 3,
        out_specs=(anywhere, anywhere),
        scratch_shapes=[
            pltpu.VMEM(load.shape, jnp.float32),
            pltpu.VMEM((1, muscles), jnp.float32),
            pltpu.SemaphoreType.DMA((4,)),
        ],
        compiler_params=pltpu.CompilerParams(vmem_limit_bytes=32 << 20),
        name="combine",
    )(every, block, fields)
    return adjoint, muscle_grad.reshape(muscles)


def solution(mesh):
    placed = (
        P(None, "gy", "gz", None),
        P(None, "gy", "gz", None),
        P("gy", "gz", None),
        P("gy", "gz", None),
        P(),
    )
    return jax.shard_map(
        per_device,
        mesh=mesh,
        in_specs=placed,
        out_specs=(P(None, "gy", "gz", None), P()),
        check_vma=False,
    )
```

```python
import functools
import math

import jax
import jax.numpy as jnp
from jax import lax
from jax.experimental import pallas as pl
from jax.experimental.pallas import tpu as pltpu
from jax.sharding import PartitionSpec as P

SHEAR = 1.0
LAME = 4.0
MASS = 0.05

LOW, HIGH = 3, 4
SIGMA = 16.0
SHIFTS = (0.0, 9.95, 1.95)
NB = 4
LANES = 128
SUB = 8
CHANNELS = 8
TERMS = 15
ALL = tuple((zt, h) for zt in range(2) for h in range(2))
OWN = ((0, 0), (0, 1))
VMEM = pl.BlockSpec(memory_space=pltpu.VMEM)


class Shifts:
    def __init__(self):
        lane = lax.broadcasted_iota(jnp.int32, (SUB, LANES), 1)
        self.sub = lax.broadcasted_iota(jnp.int32, (SUB, LANES), 0)
        self.last_lane = lane == LANES - 1
        self.first_lane = lane == 0
        self.last_sub = self.sub == SUB - 1
        self.first_sub = self.sub == 0

    def xup(self, v):
        out = {}
        for zt in {zt for zt, _ in v}:
            r0 = pltpu.roll(v[zt, 0], LANES - 1, 1)
            r1 = pltpu.roll(v[zt, 1], LANES - 1, 1)
            out[zt, 0] = jnp.where(self.last_lane, r1, r0)
            out[zt, 1] = jnp.where(self.last_lane, 0.0, r1)
        return out

    def xdown(self, v):
        out = {}
        for zt in {zt for zt, _ in v}:
            r0 = pltpu.roll(v[zt, 0], 1, 1)
            r1 = pltpu.roll(v[zt, 1], 1, 1)
            out[zt, 0] = jnp.where(self.first_lane, 0.0, r0)
            out[zt, 1] = jnp.where(self.first_lane, r0, r1)
        return out

    def zup(self, v, keys):
        out = {}
        for h in range(2):
            r0 = pltpu.roll(v[0, h], SUB - 1, 0)
            r1 = pltpu.roll(v[1, h], SUB - 1, 0)
            out[0, h] = jnp.where(self.last_sub, r1, r0)
            if (1, h) in keys:
                out[1, h] = jnp.where(self.last_sub, r0, r1)
        return out

    def zdown(self, v):
        out = {}
        for h in range(2):
            r0 = pltpu.roll(v[0, h], 1, 0)
            r1 = pltpu.roll(v[1, h], 1, 0)
            out[0, h] = jnp.where(self.first_sub, r1, r0)
            out[1, h] = jnp.where(self.first_sub, r0, r1)
        return out


def part(k):
    return pl.ds(SUB * k[0], SUB), pl.ds(LANES * k[1], LANES)


def get(ref, *index):
    return {k: ref[(*index, *part(k))] for k in ALL}


def put(ref, value, *index):
    for k in value:
        ref[(*index, *part(k))] = value[k]


def add(a, b):
    return {k: a[k] + b[k] for k in a}


def sub(a, b):
    return {k: a[k] - b[k] for k in a}


def raw_gradient(sh, read, q, keys=ALL, cache=None):
    def level(comp, at):
        if cache is not None and (comp, at) in cache:
            return cache[comp, at]
        value = read(comp, at)
        value_x = sh.xup(value)
        wide, slope = add(value, value_x), sub(value_x, value)
        wide_z, slope_z = sh.zup(wide, keys), sh.zup(slope, keys)
        out = (
            {k: slope[k] + slope_z[k] for k in keys},
            {k: wide[k] + wide_z[k] for k in keys},
            {k: wide_z[k] - wide[k] for k in keys},
        )
        if cache is not None:
            cache[comp, at] = out
        return out

    result = []
    for comp in range(3):
        here, above = level(comp, q), level(comp, q + 1)
        result.append((add(here[0], above[0]), sub(above[1], here[1]), add(here[2], above[2])))
    return result


def row_terms(sh, ext, terms, q, cache):
    grad = raw_gradient(sh, lambda comp, at: get(ext, comp, at), q, ALL, cache)
    for k in ALL:
        occ, level = ext[(6, q, *part(k))], ext[(7, q, *part(k))]
        deform = [
            [0.25 * grad[r][c][k] + (1.0 if r == c else 0.0) for c in range(3)] for r in range(3)
        ]
        cof = [
            [
                deform[(r + 1) % 3][(c + 1) % 3] * deform[(r + 2) % 3][(c + 2) % 3]
                - deform[(r + 1) % 3][(c + 2) % 3] * deform[(r + 2) % 3][(c + 1) % 3]
                for c in range(3)
            ]
            for r in range(3)
        ]
        volume = deform[0][0] * cof[0][0] + deform[0][1] * cof[0][1] + deform[0][2] * cof[0][2]
        inverse = 1.0 / volume
        scaled = occ * (1.0 / (16.0 * SIGMA))
        values = [cof[r][c] * inverse for r in range(3) for c in range(3)]
        values.append(scaled * (SHEAR - LAME * jnp.log(volume)))
        values.append(scaled)
        values.append(scaled * (SHEAR + level))
        quarter = 0.25 * occ
        values += [quarter * deform[r][0] for r in range(3)]
        for i, value in enumerate(values):
            terms[(i, q, *part(k))] = value


def row_rate(grad, terms, works, step, q, keys=ALL):
    rate = [[{} for _ in range(3)] for _ in range(3)]
    for k in keys:

        def term(i):
            return terms[(i, q, *part(k))]

        g = [[grad[r][c][k] for c in range(3)] for r in range(3)]
        inv_t = [[term(3 * r + c) for c in range(3)] for r in range(3)]
        shear, occ, fibre = term(9), term(10), term(11)
        pulled = [
            [
                inv_t[0][a] * g[0][b] + inv_t[1][a] * g[1][b] + inv_t[2][a] * g[2][b]
                for b in range(3)
            ]
            for a in range(3)
        ]
        spread = (LAME * occ) * (pulled[0][0] + pulled[1][1] + pulled[2][2])
        z = [
            [shear * pulled[c][m] + spread if c == m else shear * pulled[c][m] for c in range(3)]
            for m in range(3)
        ]
        for r in range(3):
            for c in range(3):
                rate[r][c][k] = (
                    (fibre if c == 0 else occ) * g[r][c]
                    + inv_t[r][0] * z[0][c]
                    + inv_t[r][1] * z[1][c]
                    + inv_t[r][2] * z[2][c]
                )
        if k in OWN:
            works[(step, q, *part(k))] = (
                term(12) * g[0][0] + term(13) * g[1][0] + term(14) * g[2][0]
            )
    return rate


def row_force(sh, before, rate, comp):
    p = add(before[comp][0], rate[comp][0])
    a = sub(before[comp][1], rate[comp][1])
    b = add(before[comp][2], rate[comp][2])
    along = add(p, sh.zdown(p))
    across = add(sh.zdown(add(a, b)), sub(a, b))
    return add(sh.xdown(add(along, across)), sub(across, along))


def load_rate(ref, *index):
    return [[get(ref, *index, 3 * r + c) for c in range(3)] for r in range(3)]


def save_rate(ref, rate, *index):
    for r in range(3):
        for c in range(3):
            put(ref, rate[r][c], *index, 3 * r + c)


class Sweep:
    def __init__(self, axes, rows, ext, fields, terms, works):
        self.sh = Shifts()
        self.ext, self.fields, self.terms, self.works = ext, fields, terms, works
        ends = [lax.axis_index(axis) == lax.axis_size(axis) - 1 for axis in axes]
        self.top = LOW + rows
        self.cache = {i: {} for i in range(-1, NB)}
        self.keep_y = jnp.where(ends[0], 0.0, 1.0)
        top_z = jnp.where(ends[1], SUB, -1)
        self.keep_z = {k: jnp.where(self.sh.sub + SUB * k[0] == top_z, 0.0, 1.0) for k in ALL}

    def read(self, step):
        if step == 0:
            return lambda comp, q: get(self.ext, 3 + comp, q)
        return lambda comp, q: get(self.fields, step - 1, comp, q)

    def rate(self, step, q):
        if step == 0:
            row_terms(self.sh, self.ext, self.terms, q, self.cache[-1])
        grad = raw_gradient(self.sh, self.read(step), q, ALL, self.cache[step])
        return row_rate(grad, self.terms, self.works, step, q)

    def node(self, step, q, before, rate):
        for comp in range(3):
            force = row_force(self.sh, before, rate, comp)
            if SHIFTS[step] != 0.0:
                here = self.read(step)(comp, q)
                force = {k: force[k] - (SHIFTS[step] / SIGMA) * here[k] for k in ALL}
            if q == self.top:
                force = {k: force[k] * self.keep_y for k in ALL}
            force = {k: force[k] * self.keep_z[k] if k[0] else force[k] for k in ALL}
            put(self.fields, force, step, comp, q)

    def rows(self, step, start, stop, before):
        for q in range(start, stop):
            rate = self.rate(step, q)
            self.node(step, q, before, rate)
            before = rate
        return before


def even(axis):
    return lax.rem(lax.axis_index(axis), 2) == 0


def pack_kernel(
    axes,
    disp_hbm,
    load_hbm,
    occ_hbm,
    group_hbm,
    act_hbm,
    block_ref,
    zpair_ref,
    znext_ref,
    ypair_ref,
    ynext_ref,
    group_ref,
    disp_ref,
    load_ref,
    occ_ref,
    act_ref,
    sems,
):
    copies = [
        pltpu.make_async_copy(source, target, sems.at[i])
        for i, (source, target) in enumerate(
            (
                (act_hbm, act_ref),
                (group_hbm, group_ref),
                (occ_hbm, occ_ref),
                (disp_hbm, disp_ref),
                (load_hbm, load_ref),
            )
        )
    ]
    for copy in copies:
        copy.start()
    rows, cols, depth = occ_ref.shape
    muscles = act_ref.shape[0]
    even_y, even_z = even(axes[0]), even(axes[1])
    for copy in copies:
        copy.wait()

    def row(y, carry):
        group = group_ref[y]
        level = jnp.zeros((cols, depth), jnp.float32)
        for m in range(muscles):
            level = jnp.where(group == m, act_ref[m], level)
        values = [disp_ref[c, y] for c in range(3)] + [load_ref[c, y] for c in range(3)]
        values += [occ_ref[y].astype(jnp.float32), level]
        for c, value in enumerate(values):
            block_ref[c, y] = value
            bottom, top = value[:HIGH], value[cols - HIGH :]
            zpair_ref[c, y] = jnp.where(even_z, top, bottom)
            znext_ref[c, y] = jnp.where(even_z, bottom, top)
        return carry

    lax.fori_loop(0, rows, row, 0)
    send_rows(block_ref, ypair_ref, ynext_ref, even_y)


def send_rows(block_ref, pair_ref, next_ref, is_even):
    rows = block_ref.shape[1]
    pair_at = jnp.where(is_even, rows - HIGH, 0)

    def channel(c, carry):
        for y in range(HIGH):
            pair_ref[c, y] = block_ref[c, pair_at + y]
            next_ref[c, y] = block_ref[c, rows - HIGH - pair_at + y]
        return carry

    lax.fori_loop(0, CHANNELS, channel, 0)


def corner_kernel(axes, zpair_ref, znext_ref, around_ref, ypair_ref, ynext_ref):
    even_y, even_z = even(axes[0]), even(axes[1])

    def channel(c, carry):
        for y in range(around_ref.shape[1]):
            pair, far = zpair_ref[c, y], znext_ref[c, y]
            around_ref[c, y, pl.ds(0, HIGH), :] = jnp.where(even_z, pair, far)
            around_ref[c, y, pl.ds(HIGH, HIGH), :] = jnp.where(even_z, far, pair)
        return carry

    lax.fori_loop(0, CHANNELS, channel, 0)
    send_rows(around_ref, ypair_ref, ynext_ref, even_y)


def table_row(step, m, muscles):
    half = muscles // 2
    return half * step + m + (LANES - half) * lax.div(m, half)


def muscle_sums(group_ref, works, muscles, spans, store):
    zero = jnp.zeros((SUB, LANES), jnp.float32)

    def muscle(m, carry):
        total = [zero for _ in spans]
        for q in sorted({q for span in spans for q in span}):
            for h in range(2):
                mine = group_ref[q - LOW, :, pl.ds(LANES * h, LANES)] == m
                for step, span in enumerate(spans):
                    if q in span:
                        work = works[(step, q, *part((0, h)))]
                        total[step] = total[step] + jnp.where(mine, work, 0.0)
        for step in range(len(spans)):
            store(step, table_row(step, m, muscles), jnp.sum(total[step], axis=0, keepdims=True))
        return carry

    lax.fori_loop(0, muscles, muscle, 0, unroll=4)


def inner_kernel(
    axes, muscles, block_ref, around_ref, group_ref, ext, fields, terms, works, edge, partial
):
    rows = block_ref.shape[1]

    def assemble(c, carry):
        for y in range(rows):
            ext[c, LOW + y, pl.ds(0, SUB), :] = block_ref[c, y]
            ext[c, LOW + y, pl.ds(SUB, SUB), :] = around_ref[c, y]
        return carry

    lax.fori_loop(0, CHANNELS, assemble, 0)
    sweep = Sweep(axes, rows, ext, fields, terms, works)
    for step in range(NB - 1):
        first, final = LOW + step, LOW + rows - 2 - step
        rate = sweep.rate(step, first)
        save_rate(edge, rate, step, 0)
        save_rate(edge, sweep.rows(step, first + 1, final + 1, rate), step, 1)

    def store(step, at, value):
        partial[pl.ds(at, 1), :] = value

    spans = [range(LOW + step, LOW + rows - 1 - step) for step in range(NB - 1)]
    muscle_sums(group_ref, works, muscles, spans, store)


def outer_kernel(
    axes,
    muscles,
    group_size,
    group_ref,
    partial,
    ynext_ref,
    ypair_ref,
    cnext_ref,
    cpair_ref,
    ext_in,
    fields_in,
    terms_in,
    works_in,
    edge,
    sums_ref,
    ext,
    fields,
    terms,
    works,
    table,
):
    del ext_in, fields_in, terms_in, works_in
    rows = group_ref.shape[0]
    even_y = even(axes[0])

    def assemble(c, carry):
        for zt, pair_ref, next_ref in ((0, ypair_ref, ynext_ref), (1, cpair_ref, cnext_ref)):
            for y in range(HIGH):
                pair, far = pair_ref[c, y], next_ref[c, y]
                ext[c, LOW + rows + y, pl.ds(SUB * zt, SUB), :] = jnp.where(even_y, pair, far)
                if y >= HIGH - LOW:
                    ext[c, y - HIGH + LOW, pl.ds(SUB * zt, SUB), :] = jnp.where(even_y, far, pair)
        return carry

    lax.fori_loop(0, CHANNELS, assemble, 0)
    sweep = Sweep(axes, rows, ext, fields, terms, works)
    for step in range(NB - 1):
        low = sweep.rows(step, step + 1, LOW + step, sweep.rate(step, step))
        sweep.node(step, LOW + step, low, load_rate(edge, step, 0))
        final = LOW + rows - 2 - step
        sweep.rows(step, final + 1, final + 1 + HIGH, load_rate(edge, step, 1))

    zero = jnp.zeros((SUB, LANES), jnp.float32)
    pairs = [(i, j) for i in range(NB) for j in range(i, NB)]

    def finish(q, acc):
        acc = list(acc)
        grad = raw_gradient(sweep.sh, sweep.read(NB - 1), q, OWN, sweep.cache[NB - 1])
        rate = row_rate(grad, terms, works, NB - 1, q, OWN)
        for k in OWN:
            for r in range(3):
                for c in range(3):
                    acc[-1] = acc[-1] + rate[r][c][k] * grad[r][c][k]
            for comp in range(3):
                vectors = [ext[(3 + comp, q, *part(k))]]
                vectors += [fields[(s, comp, q, *part(k))] for s in range(NB - 1)]
                for n, (i, j) in enumerate(pairs):
                    acc[n] = acc[n] + vectors[i] * vectors[j]
        return tuple(acc)

    acc = tuple(zero for _ in range(len(pairs) + 1))
    for q in range(LOW, LOW + rows):
        acc = finish(q, acc)
    table[...] = jnp.zeros_like(table)
    for n, value in enumerate(acc):
        total = jnp.sum(value, axis=0, keepdims=True)
        for core in range(2):
            table[pl.ds(LANES * core + NB * (muscles // 2) + n, 1), :] = total

    def store(step, at, value):
        if step < NB - 1:
            value = value + partial[pl.ds(at, 1), :]
        table[pl.ds(at, 1), :] = value

    own = range(LOW, LOW + rows)
    spans = [
        [q for q in own if not LOW + step <= q < LOW + rows - 1 - step or step == NB - 1]
        for step in range(NB)
    ]
    muscle_sums(group_ref, works, muscles, spans, store)
    row = lax.dot_general(
        jnp.ones((SUB, LANES), jnp.float32),
        table[...],
        (((1,), (1,)), ((), ())),
        precision=lax.Precision.HIGHEST,
        preferred_element_type=jnp.float32,
    )
    for i in range(sums_ref.shape[0] // SUB):
        core = i // (group_size // SUB) % 2
        sums_ref[pl.ds(SUB * i, SUB), :] = row[:, LANES * core : LANES * (core + 1)]


def solve_kernel(axes, muscles, scale, sums_ref, coef_ref, grad_ref):
    parts = [sums_ref[pl.ds(SUB * i, SUB), :] for i in range(sums_ref.shape[0] // SUB)]
    while len(parts) > 1:
        odd = parts[len(parts) // 2 * 2 :]
        parts = [a + b for a, b in zip(parts[0::2], parts[1::2])] + odd
    total = parts[0]
    total = jnp.sum(total, axis=0, keepdims=True)
    half = muscles // 2
    works, dots = total[:, : NB * half], total[:, NB * half :]
    pairs = [(i, j) for i in range(NB) for j in range(i, NB)]
    gram = {}
    for n, (i, j) in enumerate(pairs):
        gram[i, j] = gram[j, i] = dots[:, n : n + 1]
    energy = dots[:, len(pairs) : len(pairs) + 1]
    shifts = [MASS + s for s in SHIFTS]
    form = {}
    for j in range(NB - 1):
        for i in range(j + 1):
            form[i, j] = form[j, i] = SIGMA * gram[i, j + 1] + shifts[j] * gram[i, j]
    last = NB - 1
    for i in range(last):
        form[i, last] = form[last, i] = SIGMA * gram[i + 1, last] + shifts[i] * gram[i, last]
    form[last, last] = SIGMA * energy + MASS * gram[last, last]

    rhs = [gram[0, i] for i in range(NB)]
    inverse = []
    for k in range(NB):
        inverse.append(1.0 / form[k, k])
        for i in range(k + 1, NB):
            factor = form[k, i] * inverse[k]
            rhs[i] = rhs[i] - factor * rhs[k]
            for j in range(i, NB):
                form[i, j] = form[i, j] - factor * form[k, j]
    x = [None] * NB
    for k in reversed(range(NB)):
        value = rhs[k]
        for j in range(k + 1, NB):
            value = value - form[k, j] * x[j]
        x[k] = value * inverse[k]

    for k in range(NB):
        coef_ref[k] = jnp.broadcast_to(x[k], (SUB, LANES))
    grad = None
    for k in range(NB):
        piece = x[k] * works[:, k * half : (k + 1) * half]
        grad = piece if grad is None else grad + piece
    grad = -scale * grad
    nothing = jnp.zeros_like(grad)
    low = even(axes[0])
    grad_ref[:, pl.ds(0, half)] = jnp.where(low, grad, nothing)
    grad_ref[:, pl.ds(half, half)] = jnp.where(low, nothing, grad)


def update_kernel(coef_ref, block_ref, fields, x_hbm, x_ref, sems):
    coef = [coef_ref[k] for k in range(NB)]
    copies = []
    for comp in range(3):
        for y in range(block_ref.shape[1]):
            for h in range(2):
                at = pl.ds(LANES * h, LANES)
                value = coef[0] * block_ref[3 + comp, y, :, at]
                for k in range(1, NB):
                    value = value + coef[k] * fields[(k - 1, comp, LOW + y, *part((0, h)))]
                x_ref[comp, y, :, at] = value
        copies.append(pltpu.make_async_copy(x_ref.at[comp], x_hbm.at[comp], sems.at[comp]))
        copies[-1].start()
    for copy in copies:
        copy.wait()


def swap(shard, axis, first):
    length = lax.axis_size(axis)
    pairs = [(i, i + 1) for i in range(first, length - 1, 2)]
    return lax.ppermute(shard, axis, pairs + [(j, i) for i, j in pairs])


def per_device(displacement, load, occupancy, voxel_muscle_group, activation):
    rows, cols, depth = occupancy.shape
    muscles = activation.shape[0]
    axes = ("gy", "gz")
    count = LOW + rows + HIGH

    def arr(*shape):
        return jax.ShapeDtypeStruct(shape, jnp.float32)

    anywhere = pl.BlockSpec(memory_space=pltpu.HBM)
    faces = (arr(CHANNELS, rows, HIGH, depth),) * 2
    edges = (arr(CHANNELS, HIGH, cols, depth),) * 2
    block, zpair, znext, ypair, ynext, group = pl.pallas_call(
        functools.partial(pack_kernel, axes),
        out_shape=(
            arr(CHANNELS, rows, cols, depth),
            *faces,
            *edges,
            jax.ShapeDtypeStruct(occupancy.shape, jnp.int32),
        ),
        in_specs=[anywhere] * 5,
        out_specs=(VMEM,) * 6,
        scratch_shapes=[
            pltpu.VMEM(displacement.shape, jnp.float32),
            pltpu.VMEM(load.shape, jnp.float32),
            pltpu.VMEM(occupancy.shape, jnp.int32),
            pltpu.SMEM((muscles,), jnp.float32),
            pltpu.SemaphoreType.DMA((5,)),
        ],
        compiler_params=pltpu.CompilerParams(vmem_limit_bytes=32 << 20),
        name="pack",
    )(
        *(
            pltpu.with_memory_space_constraint(value, pltpu.HBM)
            for value in (displacement, load, occupancy, voxel_muscle_group, activation)
        )
    )

    received = [
        swap(znext, "gz", 1),
        swap(zpair, "gz", 0),
        swap(ynext, "gy", 1),
        swap(ypair, "gy", 0),
    ]
    znext, zpair, ynext, ypair = received
    znext, zpair = lax.optimization_barrier((znext, zpair))
    around, cpair, cnext = pl.pallas_call(
        functools.partial(corner_kernel, axes),
        out_shape=(arr(CHANNELS, rows, 2 * HIGH, depth), *edges),
        in_specs=[VMEM] * 2,
        out_specs=(VMEM,) * 3,
        compiler_params=pltpu.CompilerParams(vmem_limit_bytes=32 << 20),
        name="corner",
    )(zpair, znext)
    cnext = swap(cnext, "gy", 1)
    cpair = swap(cpair, "gy", 0)

    state = (
        arr(CHANNELS, count, 2 * SUB, depth),
        arr(NB - 1, 3, count, 2 * SUB, depth),
        arr(TERMS, count - 1, 2 * SUB, depth),
        arr(NB, count - 1, SUB, depth),
    )
    *inner, partial = pl.pallas_call(
        functools.partial(inner_kernel, axes, muscles),
        out_shape=(*state, arr(NB - 1, 2, 9, 2 * SUB, depth), arr(2 * LANES, LANES)),
        in_specs=[VMEM] * 3,
        out_specs=(VMEM,) * 6,
        compiler_params=pltpu.CompilerParams(vmem_limit_bytes=32 << 20),
        name="inner",
    )(block, around, group)

    devices = lax.axis_size("gy") * lax.axis_size("gz")
    sums, _, fields, _, _ = pl.pallas_call(
        functools.partial(outer_kernel, axes, muscles, lax.axis_size("gz")),
        out_shape=(arr(devices, LANES), *state),
        in_specs=[VMEM] * 11,
        out_specs=(VMEM,) * 5,
        scratch_shapes=[pltpu.VMEM((2 * LANES, LANES), jnp.float32)],
        input_output_aliases={6: 1, 7: 2, 8: 3, 9: 4},
        compiler_params=pltpu.CompilerParams(vmem_limit_bytes=32 << 20),
        name="outer",
    )(group, partial, ynext, ypair, cnext, cpair, *inner)

    every = lax.all_to_all(sums, ("gy", "gz"), 0, 0, tiled=True)

    cells = depth * rows * lax.axis_size("gy") * cols * lax.axis_size("gz")
    scale = 1.0 / math.sqrt(cells / muscles)
    coef, mine = pl.pallas_call(
        functools.partial(solve_kernel, axes, muscles, scale),
        out_shape=(arr(NB, SUB, LANES), arr(1, muscles)),
        in_specs=[VMEM],
        out_specs=(VMEM, VMEM),
        compiler_params=pltpu.CompilerParams(vmem_limit_bytes=32 << 20),
        name="solve",
    )(every)
    others = swap(mine, "gy", 0)
    adjoint = pl.pallas_call(
        update_kernel,
        out_shape=arr(*load.shape),
        in_specs=[VMEM] * 3,
        out_specs=anywhere,
        scratch_shapes=[pltpu.VMEM(load.shape, jnp.float32), pltpu.SemaphoreType.DMA((3,))],
        compiler_params=pltpu.CompilerParams(vmem_limit_bytes=32 << 20),
        name="update",
    )(coef, block, fields)
    return adjoint, (mine + others).reshape(muscles)


def solution(mesh):
    placed = (
        P(None, "gy", "gz", None),
        P(None, "gy", "gz", None),
        P("gy", "gz", None),
        P("gy", "gz", None),
        P(),
    )
    return jax.shard_map(
        per_device,
        mesh=mesh,
        in_specs=placed,
        out_specs=(P(None, "gy", "gz", None), P()),
        check_vma=False,
    )
```

```python
import functools
import math

import jax
import jax.numpy as jnp
from jax import lax
from jax.experimental import pallas as pl
from jax.experimental.pallas import tpu as pltpu
from jax.sharding import PartitionSpec as P

SHEAR = 1.0
LAME = 4.0
MASS = 0.05

LOW, HIGH = 3, 4
SIGMA = 16.0
SHIFTS = (0.0, 9.95, 1.95)
NB = 4
LANES = 128
SUB = 8
CHANNELS = 8
TERMS = 15
ALL = tuple((zt, h) for zt in range(2) for h in range(2))
OWN = ((0, 0), (0, 1))
VMEM = pl.BlockSpec(memory_space=pltpu.VMEM)


class Shifts:
    def __init__(self):
        lane = lax.broadcasted_iota(jnp.int32, (SUB, LANES), 1)
        self.sub = lax.broadcasted_iota(jnp.int32, (SUB, LANES), 0)
        self.last_lane = lane == LANES - 1
        self.first_lane = lane == 0
        self.last_sub = self.sub == SUB - 1
        self.first_sub = self.sub == 0

    def xup(self, v):
        out = {}
        for zt in {zt for zt, _ in v}:
            r0 = pltpu.roll(v[zt, 0], LANES - 1, 1)
            r1 = pltpu.roll(v[zt, 1], LANES - 1, 1)
            out[zt, 0] = jnp.where(self.last_lane, r1, r0)
            out[zt, 1] = jnp.where(self.last_lane, 0.0, r1)
        return out

    def xdown(self, v):
        out = {}
        for zt in {zt for zt, _ in v}:
            r0 = pltpu.roll(v[zt, 0], 1, 1)
            r1 = pltpu.roll(v[zt, 1], 1, 1)
            out[zt, 0] = jnp.where(self.first_lane, 0.0, r0)
            out[zt, 1] = jnp.where(self.first_lane, r0, r1)
        return out

    def zup(self, v, keys):
        out = {}
        for h in range(2):
            r0 = pltpu.roll(v[0, h], SUB - 1, 0)
            r1 = pltpu.roll(v[1, h], SUB - 1, 0)
            out[0, h] = jnp.where(self.last_sub, r1, r0)
            if (1, h) in keys:
                out[1, h] = jnp.where(self.last_sub, r0, r1)
        return out

    def zdown(self, v):
        out = {}
        for h in range(2):
            r0 = pltpu.roll(v[0, h], 1, 0)
            r1 = pltpu.roll(v[1, h], 1, 0)
            out[0, h] = jnp.where(self.first_sub, r1, r0)
            out[1, h] = jnp.where(self.first_sub, r0, r1)
        return out


def part(k):
    return pl.ds(SUB * k[0], SUB), pl.ds(LANES * k[1], LANES)


def get(ref, *index):
    return {k: ref[(*index, *part(k))] for k in ALL}


def put(ref, value, *index):
    for k in value:
        ref[(*index, *part(k))] = value[k]


def add(a, b):
    return {k: a[k] + b[k] for k in a}


def sub(a, b):
    return {k: a[k] - b[k] for k in a}


def raw_gradient(sh, read, q, keys=ALL, cache=None):
    def level(comp, at):
        if cache is not None and (comp, at) in cache:
            return cache[comp, at]
        value = read(comp, at)
        value_x = sh.xup(value)
        wide, slope = add(value, value_x), sub(value_x, value)
        wide_z, slope_z = sh.zup(wide, keys), sh.zup(slope, keys)
        out = (
            {k: slope[k] + slope_z[k] for k in keys},
            {k: wide[k] + wide_z[k] for k in keys},
            {k: wide_z[k] - wide[k] for k in keys},
        )
        if cache is not None:
            cache[comp, at] = out
        return out

    result = []
    for comp in range(3):
        here, above = level(comp, q), level(comp, q + 1)
        result.append((add(here[0], above[0]), sub(above[1], here[1]), add(here[2], above[2])))
    return result


def row_terms(sh, ext, terms, q, cache):
    grad = raw_gradient(sh, lambda comp, at: get(ext, comp, at), q, ALL, cache)
    for k in ALL:
        occ, level = ext[(6, q, *part(k))], ext[(7, q, *part(k))]
        deform = [
            [0.25 * grad[r][c][k] + (1.0 if r == c else 0.0) for c in range(3)] for r in range(3)
        ]
        cof = [
            [
                deform[(r + 1) % 3][(c + 1) % 3] * deform[(r + 2) % 3][(c + 2) % 3]
                - deform[(r + 1) % 3][(c + 2) % 3] * deform[(r + 2) % 3][(c + 1) % 3]
                for c in range(3)
            ]
            for r in range(3)
        ]
        volume = deform[0][0] * cof[0][0] + deform[0][1] * cof[0][1] + deform[0][2] * cof[0][2]
        inverse = 1.0 / volume
        scaled = occ * (1.0 / (16.0 * SIGMA))
        values = [cof[r][c] * inverse for r in range(3) for c in range(3)]
        values.append(scaled * (SHEAR - LAME * jnp.log(volume)))
        values.append(scaled)
        values.append(scaled * (SHEAR + level))
        quarter = 0.25 * occ
        values += [quarter * deform[r][0] for r in range(3)]
        for i, value in enumerate(values):
            terms[(i, q, *part(k))] = value


def row_rate(grad, terms, works, step, q, keys=ALL):
    rate = [[{} for _ in range(3)] for _ in range(3)]
    for k in keys:

        def term(i):
            return terms[(i, q, *part(k))]

        g = [[grad[r][c][k] for c in range(3)] for r in range(3)]
        inv_t = [[term(3 * r + c) for c in range(3)] for r in range(3)]
        shear, occ, fibre = term(9), term(10), term(11)
        pulled = [
            [
                inv_t[0][a] * g[0][b] + inv_t[1][a] * g[1][b] + inv_t[2][a] * g[2][b]
                for b in range(3)
            ]
            for a in range(3)
        ]
        spread = (LAME * occ) * (pulled[0][0] + pulled[1][1] + pulled[2][2])
        z = [
            [shear * pulled[c][m] + spread if c == m else shear * pulled[c][m] for c in range(3)]
            for m in range(3)
        ]
        for r in range(3):
            for c in range(3):
                rate[r][c][k] = (
                    (fibre if c == 0 else occ) * g[r][c]
                    + inv_t[r][0] * z[0][c]
                    + inv_t[r][1] * z[1][c]
                    + inv_t[r][2] * z[2][c]
                )
        if k in OWN:
            works[(step, q, *part(k))] = (
                term(12) * g[0][0] + term(13) * g[1][0] + term(14) * g[2][0]
            )
    return rate


def row_force(sh, before, rate, comp):
    p = add(before[comp][0], rate[comp][0])
    a = sub(before[comp][1], rate[comp][1])
    b = add(before[comp][2], rate[comp][2])
    along = add(p, sh.zdown(p))
    across = add(sh.zdown(add(a, b)), sub(a, b))
    return add(sh.xdown(add(along, across)), sub(across, along))


def load_rate(ref, *index):
    return [[get(ref, *index, 3 * r + c) for c in range(3)] for r in range(3)]


def save_rate(ref, rate, *index):
    for r in range(3):
        for c in range(3):
            put(ref, rate[r][c], *index, 3 * r + c)


class Sweep:
    def __init__(self, axes, rows, ext, fields, terms, works):
        self.sh = Shifts()
        self.ext, self.fields, self.terms, self.works = ext, fields, terms, works
        ends = [lax.axis_index(axis) == lax.axis_size(axis) - 1 for axis in axes]
        self.top = LOW + rows
        self.cache = {i: {} for i in range(-1, NB)}
        self.keep_y = jnp.where(ends[0], 0.0, 1.0)
        top_z = jnp.where(ends[1], SUB, -1)
        self.keep_z = {k: jnp.where(self.sh.sub + SUB * k[0] == top_z, 0.0, 1.0) for k in ALL}

    def read(self, step):
        if step == 0:
            return lambda comp, q: get(self.ext, 3 + comp, q)
        return lambda comp, q: get(self.fields, step - 1, comp, q)

    def rate(self, step, q):
        if step == 0:
            row_terms(self.sh, self.ext, self.terms, q, self.cache[-1])
        grad = raw_gradient(self.sh, self.read(step), q, ALL, self.cache[step])
        return row_rate(grad, self.terms, self.works, step, q)

    def node(self, step, q, before, rate):
        for comp in range(3):
            force = row_force(self.sh, before, rate, comp)
            if SHIFTS[step] != 0.0:
                here = self.read(step)(comp, q)
                force = {k: force[k] - (SHIFTS[step] / SIGMA) * here[k] for k in ALL}
            if q == self.top:
                force = {k: force[k] * self.keep_y for k in ALL}
            force = {k: force[k] * self.keep_z[k] if k[0] else force[k] for k in ALL}
            put(self.fields, force, step, comp, q)

    def rows(self, step, start, stop, before):
        for q in range(start, stop):
            rate = self.rate(step, q)
            self.node(step, q, before, rate)
            before = rate
        return before


def even(axis):
    return lax.rem(lax.axis_index(axis), 2) == 0


def pack_kernel(
    axes,
    disp_hbm,
    load_hbm,
    occ_hbm,
    group_hbm,
    act_hbm,
    block_ref,
    zpair_ref,
    znext_ref,
    ypair_ref,
    ynext_ref,
    group_ref,
    disp_ref,
    load_ref,
    occ_ref,
    act_ref,
    sems,
):
    copies = [
        pltpu.make_async_copy(source, target, sems.at[i])
        for i, (source, target) in enumerate(
            (
                (act_hbm, act_ref),
                (group_hbm, group_ref),
                (occ_hbm, occ_ref),
                (disp_hbm, disp_ref),
                (load_hbm, load_ref),
            )
        )
    ]
    for copy in copies:
        copy.start()
    rows, cols, depth = occ_ref.shape
    muscles = act_ref.shape[0]
    even_y, even_z = even(axes[0]), even(axes[1])
    for copy in copies:
        copy.wait()

    def row(y, carry):
        group = group_ref[y]
        level = jnp.zeros((cols, depth), jnp.float32)
        for m in range(muscles):
            level = jnp.where(group == m, act_ref[m], level)
        values = [disp_ref[c, y] for c in range(3)] + [load_ref[c, y] for c in range(3)]
        values += [occ_ref[y].astype(jnp.float32), level]
        for c, value in enumerate(values):
            block_ref[c, y] = value
            bottom, top = value[:HIGH], value[cols - HIGH :]
            zpair_ref[c, y] = jnp.where(even_z, top, bottom)
            znext_ref[c, y] = jnp.where(even_z, bottom, top)
        return carry

    lax.fori_loop(0, rows, row, 0, unroll=4)
    send_rows(block_ref, ypair_ref, ynext_ref, even_y)


def send_rows(block_ref, pair_ref, next_ref, is_even):
    rows = block_ref.shape[1]
    pair_at = jnp.where(is_even, rows - HIGH, 0)

    def channel(c, carry):
        for y in range(HIGH):
            pair_ref[c, y] = block_ref[c, pair_at + y]
            next_ref[c, y] = block_ref[c, rows - HIGH - pair_at + y]
        return carry

    lax.fori_loop(0, CHANNELS, channel, 0, unroll=4)


def corner_kernel(axes, zpair_ref, znext_ref, around_ref, ypair_ref, ynext_ref):
    even_y, even_z = even(axes[0]), even(axes[1])

    def channel(c, carry):
        for y in range(around_ref.shape[1]):
            pair, far = zpair_ref[c, y], znext_ref[c, y]
            around_ref[c, y, pl.ds(0, HIGH), :] = jnp.where(even_z, pair, far)
            around_ref[c, y, pl.ds(HIGH, HIGH), :] = jnp.where(even_z, far, pair)
        return carry

    lax.fori_loop(0, CHANNELS, channel, 0, unroll=4)
    send_rows(around_ref, ypair_ref, ynext_ref, even_y)


def table_row(step, m, muscles):
    half = muscles // 2
    return half * step + m + (LANES - half) * lax.div(m, half)


def muscle_sums(group_ref, works, muscles, spans, store):
    zero = jnp.zeros((SUB, LANES), jnp.float32)

    def muscle(m, carry):
        total = [zero for _ in spans]
        for q in sorted({q for span in spans for q in span}):
            for h in range(2):
                mine = group_ref[q - LOW, :, pl.ds(LANES * h, LANES)] == m
                for step, span in enumerate(spans):
                    if q in span:
                        work = works[(step, q, *part((0, h)))]
                        total[step] = total[step] + jnp.where(mine, work, 0.0)
        for step in range(len(spans)):
            store(step, table_row(step, m, muscles), jnp.sum(total[step], axis=0, keepdims=True))
        return carry

    lax.fori_loop(0, muscles, muscle, 0, unroll=8)


def inner_kernel(
    axes, muscles, block_ref, around_ref, group_ref, ext, fields, terms, works, edge, partial
):
    rows = block_ref.shape[1]

    def assemble(c, carry):
        for y in range(rows):
            ext[c, LOW + y, pl.ds(0, SUB), :] = block_ref[c, y]
            ext[c, LOW + y, pl.ds(SUB, SUB), :] = around_ref[c, y]
        return carry

    lax.fori_loop(0, CHANNELS, assemble, 0, unroll=4)
    sweep = Sweep(axes, rows, ext, fields, terms, works)
    for step in range(NB - 1):
        first, final = LOW + step, LOW + rows - 2 - step
        rate = sweep.rate(step, first)
        save_rate(edge, rate, step, 0)
        save_rate(edge, sweep.rows(step, first + 1, final + 1, rate), step, 1)

    def store(step, at, value):
        partial[pl.ds(at, 1), :] = value

    spans = [range(LOW + step, LOW + rows - 1 - step) for step in range(NB - 1)]
    muscle_sums(group_ref, works, muscles, spans, store)


def outer_kernel(
    axes,
    muscles,
    group_size,
    group_ref,
    partial,
    ynext_ref,
    ypair_ref,
    cnext_ref,
    cpair_ref,
    ext_in,
    fields_in,
    terms_in,
    works_in,
    edge,
    sums_ref,
    ext,
    fields,
    terms,
    works,
    table,
):
    del ext_in, fields_in, terms_in, works_in
    rows = group_ref.shape[0]
    even_y = even(axes[0])

    def assemble(c, carry):
        for zt, pair_ref, next_ref in ((0, ypair_ref, ynext_ref), (1, cpair_ref, cnext_ref)):
            for y in range(HIGH):
                pair, far = pair_ref[c, y], next_ref[c, y]
                ext[c, LOW + rows + y, pl.ds(SUB * zt, SUB), :] = jnp.where(even_y, pair, far)
                if y >= HIGH - LOW:
                    ext[c, y - HIGH + LOW, pl.ds(SUB * zt, SUB), :] = jnp.where(even_y, far, pair)
        return carry

    lax.fori_loop(0, CHANNELS, assemble, 0, unroll=4)
    sweep = Sweep(axes, rows, ext, fields, terms, works)
    for step in range(NB - 1):
        low = sweep.rows(step, step + 1, LOW + step, sweep.rate(step, step))
        sweep.node(step, LOW + step, low, load_rate(edge, step, 0))
        final = LOW + rows - 2 - step
        sweep.rows(step, final + 1, final + 1 + HIGH, load_rate(edge, step, 1))

    zero = jnp.zeros((SUB, LANES), jnp.float32)
    pairs = [(i, j) for i in range(NB) for j in range(i, NB)]

    def finish(q, acc):
        acc = list(acc)
        grad = raw_gradient(sweep.sh, sweep.read(NB - 1), q, OWN, sweep.cache[NB - 1])
        rate = row_rate(grad, terms, works, NB - 1, q, OWN)
        for k in OWN:
            for r in range(3):
                for c in range(3):
                    acc[-1] = acc[-1] + rate[r][c][k] * grad[r][c][k]
            for comp in range(3):
                vectors = [ext[(3 + comp, q, *part(k))]]
                vectors += [fields[(s, comp, q, *part(k))] for s in range(NB - 1)]
                for n, (i, j) in enumerate(pairs):
                    acc[n] = acc[n] + vectors[i] * vectors[j]
        return tuple(acc)

    acc = tuple(zero for _ in range(len(pairs) + 1))
    for q in range(LOW, LOW + rows):
        acc = finish(q, acc)
    table[...] = jnp.zeros_like(table)
    for n, value in enumerate(acc):
        total = jnp.sum(value, axis=0, keepdims=True)
        for core in range(2):
            table[pl.ds(LANES * core + NB * (muscles // 2) + n, 1), :] = total

    def store(step, at, value):
        if step < NB - 1:
            value = value + partial[pl.ds(at, 1), :]
        table[pl.ds(at, 1), :] = value

    own = range(LOW, LOW + rows)
    spans = [
        [q for q in own if not LOW + step <= q < LOW + rows - 1 - step or step == NB - 1]
        for step in range(NB)
    ]
    muscle_sums(group_ref, works, muscles, spans, store)
    row = lax.dot_general(
        jnp.ones((SUB, LANES), jnp.float32),
        table[...],
        (((1,), (1,)), ((), ())),
        precision=lax.Precision.HIGHEST,
        preferred_element_type=jnp.float32,
    )
    for i in range(sums_ref.shape[0] // SUB):
        core = i // (group_size // SUB) % 2
        sums_ref[pl.ds(SUB * i, SUB), :] = row[:, LANES * core : LANES * (core + 1)]


def solve_kernel(axes, muscles, scale, sums_ref, coef_ref, grad_ref):
    parts = [sums_ref[pl.ds(SUB * i, SUB), :] for i in range(sums_ref.shape[0] // SUB)]
    while len(parts) > 1:
        odd = parts[len(parts) // 2 * 2 :]
        parts = [a + b for a, b in zip(parts[0::2], parts[1::2])] + odd
    total = parts[0]
    total = jnp.broadcast_to(jnp.sum(total, axis=0, keepdims=True), (SUB, LANES))
    half = muscles // 2

    def everywhere(lane):
        return jnp.broadcast_to(total[:, lane : lane + 1], (SUB, LANES))

    pairs = [(i, j) for i in range(NB) for j in range(i, NB)]
    gram = {}
    for n, (i, j) in enumerate(pairs):
        gram[i, j] = gram[j, i] = everywhere(NB * half + n)
    energy = everywhere(NB * half + len(pairs))
    shifts = [MASS + s for s in SHIFTS]
    form = {}
    for j in range(NB - 1):
        for i in range(j + 1):
            form[i, j] = form[j, i] = SIGMA * gram[i, j + 1] + shifts[j] * gram[i, j]
    last = NB - 1
    for i in range(last):
        form[i, last] = form[last, i] = SIGMA * gram[i + 1, last] + shifts[i] * gram[i, last]
    form[last, last] = SIGMA * energy + MASS * gram[last, last]

    rhs = [gram[0, i] for i in range(NB)]
    inverse = []
    for k in range(NB):
        inverse.append(1.0 / form[k, k])
        for i in range(k + 1, NB):
            factor = form[k, i] * inverse[k]
            rhs[i] = rhs[i] - factor * rhs[k]
            for j in range(i, NB):
                form[i, j] = form[i, j] - factor * form[k, j]
    x = [None] * NB
    for k in reversed(range(NB)):
        value = rhs[k]
        for j in range(k + 1, NB):
            value = value - form[k, j] * x[j]
        x[k] = value * inverse[k]

    for k in range(NB):
        coef_ref[k] = x[k]
    lane = lax.broadcasted_iota(jnp.int32, (SUB, LANES), 1)
    weight = jnp.zeros((SUB, LANES), jnp.float32)
    for k in range(NB):
        weight = jnp.where((lane >= k * half) & (lane < (k + 1) * half), x[k], weight)
    grad = total * weight
    grad = grad + pltpu.roll(grad, LANES - 2 * half, 1)
    grad = -scale * (grad + pltpu.roll(grad, LANES - half, 1))
    low = jnp.where(lane < half, grad, 0.0)
    high = jnp.where((lane >= half) & (lane < 2 * half), pltpu.roll(grad, half, 1), 0.0)
    grad_ref[...] = jnp.where(even(axes[0]), low, high)[:1, :muscles]


def update_kernel(coef_ref, block_ref, fields, x_hbm, x_ref, sems):
    coef = [coef_ref[k] for k in range(NB)]
    copies = []
    for comp in range(3):
        for y in range(block_ref.shape[1]):
            for h in range(2):
                at = pl.ds(LANES * h, LANES)
                value = coef[0] * block_ref[3 + comp, y, :, at]
                for k in range(1, NB):
                    value = value + coef[k] * fields[(k - 1, comp, LOW + y, *part((0, h)))]
                x_ref[comp, y, :, at] = value
        copies.append(pltpu.make_async_copy(x_ref.at[comp], x_hbm.at[comp], sems.at[comp]))
        copies[-1].start()
    for copy in copies:
        copy.wait()


def swap(shard, axis, first):
    length = lax.axis_size(axis)
    pairs = [(i, i + 1) for i in range(first, length - 1, 2)]
    return lax.ppermute(shard, axis, pairs + [(j, i) for i, j in pairs])


def per_device(displacement, load, occupancy, voxel_muscle_group, activation):
    rows, cols, depth = occupancy.shape
    muscles = activation.shape[0]
    axes = ("gy", "gz")
    count = LOW + rows + HIGH

    def arr(*shape):
        return jax.ShapeDtypeStruct(shape, jnp.float32)

    anywhere = pl.BlockSpec(memory_space=pltpu.HBM)
    faces = (arr(CHANNELS, rows, HIGH, depth),) * 2
    edges = (arr(CHANNELS, HIGH, cols, depth),) * 2
    block, zpair, znext, ypair, ynext, group = pl.pallas_call(
        functools.partial(pack_kernel, axes),
        out_shape=(
            arr(CHANNELS, rows, cols, depth),
            *faces,
            *edges,
            jax.ShapeDtypeStruct(occupancy.shape, jnp.int32),
        ),
        in_specs=[anywhere] * 5,
        out_specs=(VMEM,) * 6,
        scratch_shapes=[
            pltpu.VMEM(displacement.shape, jnp.float32),
            pltpu.VMEM(load.shape, jnp.float32),
            pltpu.VMEM(occupancy.shape, jnp.int32),
            pltpu.SMEM((muscles,), jnp.float32),
            pltpu.SemaphoreType.DMA((5,)),
        ],
        compiler_params=pltpu.CompilerParams(vmem_limit_bytes=32 << 20),
        name="pack",
    )(
        *(
            pltpu.with_memory_space_constraint(value, pltpu.HBM)
            for value in (displacement, load, occupancy, voxel_muscle_group, activation)
        )
    )

    received = [
        swap(znext, "gz", 1),
        swap(zpair, "gz", 0),
        swap(ynext, "gy", 1),
        swap(ypair, "gy", 0),
    ]
    znext, zpair, ynext, ypair = received
    znext, zpair = lax.optimization_barrier((znext, zpair))
    around, cpair, cnext = pl.pallas_call(
        functools.partial(corner_kernel, axes),
        out_shape=(arr(CHANNELS, rows, 2 * HIGH, depth), *edges),
        in_specs=[VMEM] * 2,
        out_specs=(VMEM,) * 3,
        compiler_params=pltpu.CompilerParams(vmem_limit_bytes=32 << 20),
        name="corner",
    )(zpair, znext)
    cnext = swap(cnext, "gy", 1)
    cpair = swap(cpair, "gy", 0)

    state = (
        arr(CHANNELS, count, 2 * SUB, depth),
        arr(NB - 1, 3, count, 2 * SUB, depth),
        arr(TERMS, count - 1, 2 * SUB, depth),
        arr(NB, count - 1, SUB, depth),
    )
    *inner, partial = pl.pallas_call(
        functools.partial(inner_kernel, axes, muscles),
        out_shape=(*state, arr(NB - 1, 2, 9, 2 * SUB, depth), arr(2 * LANES, LANES)),
        in_specs=[VMEM] * 3,
        out_specs=(VMEM,) * 6,
        compiler_params=pltpu.CompilerParams(vmem_limit_bytes=32 << 20),
        name="inner",
    )(block, around, group)

    devices = lax.axis_size("gy") * lax.axis_size("gz")
    sums, _, fields, _, _ = pl.pallas_call(
        functools.partial(outer_kernel, axes, muscles, lax.axis_size("gz")),
        out_shape=(arr(devices, LANES), *state),
        in_specs=[VMEM] * 11,
        out_specs=(VMEM,) * 5,
        scratch_shapes=[pltpu.VMEM((2 * LANES, LANES), jnp.float32)],
        input_output_aliases={6: 1, 7: 2, 8: 3, 9: 4},
        compiler_params=pltpu.CompilerParams(vmem_limit_bytes=32 << 20),
        name="outer",
    )(group, partial, ynext, ypair, cnext, cpair, *inner)

    every = lax.all_to_all(sums, ("gy", "gz"), 0, 0, tiled=True)

    cells = depth * rows * lax.axis_size("gy") * cols * lax.axis_size("gz")
    scale = 1.0 / math.sqrt(cells / muscles)
    coef, mine = pl.pallas_call(
        functools.partial(solve_kernel, axes, muscles, scale),
        out_shape=(arr(NB, SUB, LANES), arr(1, muscles)),
        in_specs=[VMEM],
        out_specs=(VMEM, VMEM),
        compiler_params=pltpu.CompilerParams(vmem_limit_bytes=32 << 20),
        name="solve",
    )(every)
    others = swap(mine, "gy", 0)
    adjoint = pl.pallas_call(
        update_kernel,
        out_shape=arr(*load.shape),
        in_specs=[VMEM] * 3,
        out_specs=anywhere,
        scratch_shapes=[pltpu.VMEM(load.shape, jnp.float32), pltpu.SemaphoreType.DMA((3,))],
        compiler_params=pltpu.CompilerParams(vmem_limit_bytes=32 << 20),
        name="update",
    )(coef, block, fields)
    return adjoint, (mine + others).reshape(muscles)


def solution(mesh):
    placed = (
        P(None, "gy", "gz", None),
        P(None, "gy", "gz", None),
        P("gy", "gz", None),
        P("gy", "gz", None),
        P(),
    )
    return jax.shard_map(
        per_device,
        mesh=mesh,
        in_specs=placed,
        out_specs=(P(None, "gy", "gz", None), P()),
        check_vma=False,
    )
```

```python
import functools
import math

import jax
import jax.numpy as jnp
from jax import lax
from jax.experimental import pallas as pl
from jax.experimental.pallas import tpu as pltpu
from jax.sharding import PartitionSpec as P

SHEAR = 1.0
LAME = 4.0
MASS = 0.05

LOW, HIGH = 3, 4
SIGMA = 16.0
SHIFTS = (0.0, 9.95, 1.95)
NB = 4
LANES = 128
SUB = 8
CHANNELS = 8
TERMS = 15
ALL = tuple((zt, h) for zt in range(2) for h in range(2))
OWN = ((0, 0), (0, 1))
VMEM = pl.BlockSpec(memory_space=pltpu.VMEM)


class Shifts:
    def __init__(self):
        lane = lax.broadcasted_iota(jnp.int32, (SUB, LANES), 1)
        self.sub = lax.broadcasted_iota(jnp.int32, (SUB, LANES), 0)
        self.last_lane = lane == LANES - 1
        self.first_lane = lane == 0
        self.last_sub = self.sub == SUB - 1
        self.first_sub = self.sub == 0

    def xup(self, v):
        out = {}
        for zt in {zt for zt, _ in v}:
            r0 = pltpu.roll(v[zt, 0], LANES - 1, 1)
            r1 = pltpu.roll(v[zt, 1], LANES - 1, 1)
            out[zt, 0] = jnp.where(self.last_lane, r1, r0)
            out[zt, 1] = jnp.where(self.last_lane, 0.0, r1)
        return out

    def xdown(self, v):
        out = {}
        for zt in {zt for zt, _ in v}:
            r0 = pltpu.roll(v[zt, 0], 1, 1)
            r1 = pltpu.roll(v[zt, 1], 1, 1)
            out[zt, 0] = jnp.where(self.first_lane, 0.0, r0)
            out[zt, 1] = jnp.where(self.first_lane, r0, r1)
        return out

    def zup(self, v, keys):
        out = {}
        for h in range(2):
            r0 = pltpu.roll(v[0, h], SUB - 1, 0)
            r1 = pltpu.roll(v[1, h], SUB - 1, 0)
            out[0, h] = jnp.where(self.last_sub, r1, r0)
            if (1, h) in keys:
                out[1, h] = jnp.where(self.last_sub, r0, r1)
        return out

    def zdown(self, v):
        out = {}
        for h in range(2):
            r0 = pltpu.roll(v[0, h], 1, 0)
            r1 = pltpu.roll(v[1, h], 1, 0)
            out[0, h] = jnp.where(self.first_sub, r1, r0)
            out[1, h] = jnp.where(self.first_sub, r0, r1)
        return out


def part(k):
    return pl.ds(SUB * k[0], SUB), pl.ds(LANES * k[1], LANES)


def get(ref, *index):
    return {k: ref[(*index, *part(k))] for k in ALL}


def put(ref, value, *index):
    for k in value:
        ref[(*index, *part(k))] = value[k]


def add(a, b):
    return {k: a[k] + b[k] for k in a}


def sub(a, b):
    return {k: a[k] - b[k] for k in a}


def raw_gradient(sh, read, q, keys=ALL, cache=None):
    def level(comp, at):
        if cache is not None and (comp, at) in cache:
            return cache[comp, at]
        value = read(comp, at)
        value_x = sh.xup(value)
        wide, slope = add(value, value_x), sub(value_x, value)
        wide_z, slope_z = sh.zup(wide, keys), sh.zup(slope, keys)
        out = (
            {k: slope[k] + slope_z[k] for k in keys},
            {k: wide[k] + wide_z[k] for k in keys},
            {k: wide_z[k] - wide[k] for k in keys},
        )
        if cache is not None:
            cache[comp, at] = out
        return out

    result = []
    for comp in range(3):
        here, above = level(comp, q), level(comp, q + 1)
        result.append((add(here[0], above[0]), sub(above[1], here[1]), add(here[2], above[2])))
    return result


def row_terms(sh, ext, terms, q, cache):
    grad = raw_gradient(sh, lambda comp, at: get(ext, comp, at), q, ALL, cache)
    for k in ALL:
        occ, level = ext[(6, q, *part(k))], ext[(7, q, *part(k))]
        deform = [
            [0.25 * grad[r][c][k] + (1.0 if r == c else 0.0) for c in range(3)] for r in range(3)
        ]
        cof = [
            [
                deform[(r + 1) % 3][(c + 1) % 3] * deform[(r + 2) % 3][(c + 2) % 3]
                - deform[(r + 1) % 3][(c + 2) % 3] * deform[(r + 2) % 3][(c + 1) % 3]
                for c in range(3)
            ]
            for r in range(3)
        ]
        volume = deform[0][0] * cof[0][0] + deform[0][1] * cof[0][1] + deform[0][2] * cof[0][2]
        inverse = 1.0 / volume
        scaled = occ * (1.0 / (16.0 * SIGMA))
        values = [cof[r][c] * inverse for r in range(3) for c in range(3)]
        values.append(scaled * (SHEAR - LAME * jnp.log(volume)))
        values.append(scaled)
        values.append(scaled * (SHEAR + level))
        quarter = 0.25 * occ
        values += [quarter * deform[r][0] for r in range(3)]
        for i, value in enumerate(values):
            terms[(i, q, *part(k))] = value


def row_rate(grad, terms, works, step, q, keys=ALL):
    rate = [[{} for _ in range(3)] for _ in range(3)]
    for k in keys:

        def term(i):
            return terms[(i, q, *part(k))]

        g = [[grad[r][c][k] for c in range(3)] for r in range(3)]
        inv_t = [[term(3 * r + c) for c in range(3)] for r in range(3)]
        shear, occ, fibre = term(9), term(10), term(11)
        pulled = [
            [
                inv_t[0][a] * g[0][b] + inv_t[1][a] * g[1][b] + inv_t[2][a] * g[2][b]
                for b in range(3)
            ]
            for a in range(3)
        ]
        spread = (LAME * occ) * (pulled[0][0] + pulled[1][1] + pulled[2][2])
        z = [
            [shear * pulled[c][m] + spread if c == m else shear * pulled[c][m] for c in range(3)]
            for m in range(3)
        ]
        for r in range(3):
            for c in range(3):
                rate[r][c][k] = (
                    (fibre if c == 0 else occ) * g[r][c]
                    + inv_t[r][0] * z[0][c]
                    + inv_t[r][1] * z[1][c]
                    + inv_t[r][2] * z[2][c]
                )
        if k in OWN:
            works[(step, q, *part(k))] = (
                term(12) * g[0][0] + term(13) * g[1][0] + term(14) * g[2][0]
            )
    return rate


def row_force(sh, before, rate, comp):
    p = add(before[comp][0], rate[comp][0])
    a = sub(before[comp][1], rate[comp][1])
    b = add(before[comp][2], rate[comp][2])
    along = add(p, sh.zdown(p))
    across = add(sh.zdown(add(a, b)), sub(a, b))
    return add(sh.xdown(add(along, across)), sub(across, along))


def load_rate(ref, *index):
    return [[get(ref, *index, 3 * r + c) for c in range(3)] for r in range(3)]


def save_rate(ref, rate, *index):
    for r in range(3):
        for c in range(3):
            put(ref, rate[r][c], *index, 3 * r + c)


class Sweep:
    def __init__(self, axes, rows, ext, fields, terms, works):
        self.sh = Shifts()
        self.ext, self.fields, self.terms, self.works = ext, fields, terms, works
        ends = [lax.axis_index(axis) == lax.axis_size(axis) - 1 for axis in axes]
        self.top = LOW + rows
        self.cache = {i: {} for i in range(-1, NB)}
        self.keep_y = jnp.where(ends[0], 0.0, 1.0)
        top_z = jnp.where(ends[1], SUB, -1)
        self.keep_z = {k: jnp.where(self.sh.sub + SUB * k[0] == top_z, 0.0, 1.0) for k in ALL}

    def read(self, step):
        if step == 0:
            return lambda comp, q: get(self.ext, 3 + comp, q)
        return lambda comp, q: get(self.fields, step - 1, comp, q)

    def rate(self, step, q):
        if step == 0:
            row_terms(self.sh, self.ext, self.terms, q, self.cache[-1])
        grad = raw_gradient(self.sh, self.read(step), q, ALL, self.cache[step])
        return row_rate(grad, self.terms, self.works, step, q)

    def node(self, step, q, before, rate):
        for comp in range(3):
            force = row_force(self.sh, before, rate, comp)
            if SHIFTS[step] != 0.0:
                here = self.read(step)(comp, q)
                force = {k: force[k] - (SHIFTS[step] / SIGMA) * here[k] for k in ALL}
            if q == self.top:
                force = {k: force[k] * self.keep_y for k in ALL}
            force = {k: force[k] * self.keep_z[k] if k[0] else force[k] for k in ALL}
            put(self.fields, force, step, comp, q)

    def rows(self, step, start, stop, before):
        for q in range(start, stop):
            rate = self.rate(step, q)
            self.node(step, q, before, rate)
            before = rate
        return before


def even(axis):
    return lax.rem(lax.axis_index(axis), 2) == 0


def pack_kernel(
    axes,
    disp_hbm,
    load_hbm,
    occ_hbm,
    group_hbm,
    act_hbm,
    block_ref,
    zpair_ref,
    znext_ref,
    ypair_ref,
    ynext_ref,
    group_ref,
    disp_ref,
    load_ref,
    occ_ref,
    act_ref,
    sems,
):
    copies = [
        pltpu.make_async_copy(source, target, sems.at[i])
        for i, (source, target) in enumerate(
            (
                (act_hbm, act_ref),
                (group_hbm, group_ref),
                (occ_hbm, occ_ref),
                (disp_hbm, disp_ref),
                (load_hbm, load_ref),
            )
        )
    ]
    for copy in copies:
        copy.start()
    rows, cols, depth = occ_ref.shape
    muscles = act_ref.shape[0]
    even_y, even_z = even(axes[0]), even(axes[1])
    for copy in copies[:2]:
        copy.wait()
    for y in range(rows):
        group = group_ref[y]
        level = jnp.zeros((cols, depth), jnp.float32)
        for m in range(muscles):
            level = jnp.where(group == m, act_ref[m], level)
        block_ref[CHANNELS - 1, y] = level
    for copy in copies[2:]:
        copy.wait()
    for y in range(rows):
        values = [disp_ref[c, y] for c in range(3)] + [load_ref[c, y] for c in range(3)]
        values.append(occ_ref[y].astype(jnp.float32))
        for c, value in enumerate(values):
            block_ref[c, y] = value
        values.append(block_ref[CHANNELS - 1, y])
        for c, value in enumerate(values):
            bottom, top = value[:HIGH], value[cols - HIGH :]
            zpair_ref[c, y] = jnp.where(even_z, top, bottom)
            znext_ref[c, y] = jnp.where(even_z, bottom, top)
    send_rows(block_ref, ypair_ref, ynext_ref, even_y)


def send_rows(block_ref, pair_ref, next_ref, is_even):
    rows = block_ref.shape[1]
    pair_at = jnp.where(is_even, rows - HIGH, 0)

    def channel(c, carry):
        for y in range(HIGH):
            pair_ref[c, y] = block_ref[c, pair_at + y]
            next_ref[c, y] = block_ref[c, rows - HIGH - pair_at + y]
        return carry

    lax.fori_loop(0, CHANNELS, channel, 0, unroll=4)


def corner_kernel(axes, zpair_ref, znext_ref, around_ref, ypair_ref, ynext_ref):
    even_y, even_z = even(axes[0]), even(axes[1])

    def channel(c, carry):
        for y in range(around_ref.shape[1]):
            pair, far = zpair_ref[c, y], znext_ref[c, y]
            around_ref[c, y, pl.ds(0, HIGH), :] = jnp.where(even_z, pair, far)
            around_ref[c, y, pl.ds(HIGH, HIGH), :] = jnp.where(even_z, far, pair)
        return carry

    lax.fori_loop(0, CHANNELS, channel, 0, unroll=4)
    send_rows(around_ref, ypair_ref, ynext_ref, even_y)


def table_row(step, m, muscles):
    half = muscles // 2
    return half * step + m + (LANES - half) * lax.div(m, half)


def muscle_sums(group_ref, works, muscles, spans, store):
    zero = jnp.zeros((SUB, LANES), jnp.float32)

    def muscle(m, carry):
        total = [zero for _ in spans]
        for q in sorted({q for span in spans for q in span}):
            for h in range(2):
                mine = group_ref[q - LOW, :, pl.ds(LANES * h, LANES)] == m
                for step, span in enumerate(spans):
                    if q in span:
                        work = works[(step, q, *part((0, h)))]
                        total[step] = total[step] + jnp.where(mine, work, 0.0)
        for step in range(len(spans)):
            store(step, table_row(step, m, muscles), jnp.sum(total[step], axis=0, keepdims=True))
        return carry

    lax.fori_loop(0, muscles, muscle, 0, unroll=16)


def inner_kernel(
    axes, muscles, block_ref, around_ref, group_ref, ext, fields, terms, works, edge, partial
):
    rows = block_ref.shape[1]

    def assemble(c, carry):
        for y in range(rows):
            ext[c, LOW + y, pl.ds(0, SUB), :] = block_ref[c, y]
            ext[c, LOW + y, pl.ds(SUB, SUB), :] = around_ref[c, y]
        return carry

    lax.fori_loop(0, CHANNELS, assemble, 0, unroll=4)
    sweep = Sweep(axes, rows, ext, fields, terms, works)
    for step in range(NB - 1):
        first, final = LOW + step, LOW + rows - 2 - step
        rate = sweep.rate(step, first)
        save_rate(edge, rate, step, 0)
        save_rate(edge, sweep.rows(step, first + 1, final + 1, rate), step, 1)

    def store(step, at, value):
        partial[pl.ds(at, 1), :] = value

    spans = [range(LOW + step, LOW + rows - 1 - step) for step in range(NB - 1)]
    muscle_sums(group_ref, works, muscles, spans, store)


def outer_kernel(
    axes,
    muscles,
    group_size,
    group_ref,
    partial,
    ynext_ref,
    ypair_ref,
    cnext_ref,
    cpair_ref,
    ext_in,
    fields_in,
    terms_in,
    works_in,
    edge,
    sums_ref,
    ext,
    fields,
    terms,
    works,
    table,
):
    del ext_in, fields_in, terms_in, works_in
    rows = group_ref.shape[0]
    even_y = even(axes[0])

    def assemble(c, carry):
        for zt, pair_ref, next_ref in ((0, ypair_ref, ynext_ref), (1, cpair_ref, cnext_ref)):
            for y in range(HIGH):
                pair, far = pair_ref[c, y], next_ref[c, y]
                ext[c, LOW + rows + y, pl.ds(SUB * zt, SUB), :] = jnp.where(even_y, pair, far)
                if y >= HIGH - LOW:
                    ext[c, y - HIGH + LOW, pl.ds(SUB * zt, SUB), :] = jnp.where(even_y, far, pair)
        return carry

    lax.fori_loop(0, CHANNELS, assemble, 0, unroll=4)
    sweep = Sweep(axes, rows, ext, fields, terms, works)
    for step in range(NB - 1):
        low = sweep.rows(step, step + 1, LOW + step, sweep.rate(step, step))
        sweep.node(step, LOW + step, low, load_rate(edge, step, 0))
        final = LOW + rows - 2 - step
        sweep.rows(step, final + 1, final + 1 + HIGH, load_rate(edge, step, 1))

    zero = jnp.zeros((SUB, LANES), jnp.float32)
    pairs = [(i, j) for i in range(NB) for j in range(i, NB)]

    def finish(q, acc):
        acc = list(acc)
        grad = raw_gradient(sweep.sh, sweep.read(NB - 1), q, OWN, sweep.cache[NB - 1])
        rate = row_rate(grad, terms, works, NB - 1, q, OWN)
        for k in OWN:
            for r in range(3):
                for c in range(3):
                    acc[-1] = acc[-1] + rate[r][c][k] * grad[r][c][k]
            for comp in range(3):
                vectors = [ext[(3 + comp, q, *part(k))]]
                vectors += [fields[(s, comp, q, *part(k))] for s in range(NB - 1)]
                for n, (i, j) in enumerate(pairs):
                    acc[n] = acc[n] + vectors[i] * vectors[j]
        return tuple(acc)

    acc = tuple(zero for _ in range(len(pairs) + 1))
    for q in range(LOW, LOW + rows):
        acc = finish(q, acc)
    table[...] = jnp.zeros_like(table)
    for n, value in enumerate(acc):
        total = jnp.sum(value, axis=0, keepdims=True)
        for core in range(2):
            table[pl.ds(LANES * core + NB * (muscles // 2) + n, 1), :] = total

    def store(step, at, value):
        if step < NB - 1:
            value = value + partial[pl.ds(at, 1), :]
        table[pl.ds(at, 1), :] = value

    own = range(LOW, LOW + rows)
    spans = [
        [q for q in own if not LOW + step <= q < LOW + rows - 1 - step or step == NB - 1]
        for step in range(NB)
    ]
    muscle_sums(group_ref, works, muscles, spans, store)
    row = lax.dot_general(
        jnp.ones((SUB, LANES), jnp.float32),
        table[...],
        (((1,), (1,)), ((), ())),
        precision=lax.Precision.HIGHEST,
        preferred_element_type=jnp.float32,
    )
    for i in range(sums_ref.shape[0] // SUB):
        core = i // (group_size // SUB) % 2
        sums_ref[pl.ds(SUB * i, SUB), :] = row[:, LANES * core : LANES * (core + 1)]


def solve_kernel(axes, muscles, scale, sums_ref, coef_ref, grad_ref):
    parts = [sums_ref[pl.ds(SUB * i, SUB), :] for i in range(sums_ref.shape[0] // SUB)]
    while len(parts) > 1:
        odd = parts[len(parts) // 2 * 2 :]
        parts = [a + b for a, b in zip(parts[0::2], parts[1::2])] + odd
    total = parts[0]
    total = jnp.broadcast_to(jnp.sum(total, axis=0, keepdims=True), (SUB, LANES))
    half = muscles // 2

    def everywhere(lane):
        return jnp.broadcast_to(total[:, lane : lane + 1], (SUB, LANES))

    pairs = [(i, j) for i in range(NB) for j in range(i, NB)]
    gram = {}
    for n, (i, j) in enumerate(pairs):
        gram[i, j] = gram[j, i] = everywhere(NB * half + n)
    energy = everywhere(NB * half + len(pairs))
    shifts = [MASS + s for s in SHIFTS]
    form = {}
    for j in range(NB - 1):
        for i in range(j + 1):
            form[i, j] = form[j, i] = SIGMA * gram[i, j + 1] + shifts[j] * gram[i, j]
    last = NB - 1
    for i in range(last):
        form[i, last] = form[last, i] = SIGMA * gram[i + 1, last] + shifts[i] * gram[i, last]
    form[last, last] = SIGMA * energy + MASS * gram[last, last]

    rhs = [gram[0, i] for i in range(NB)]
    inverse = []
    for k in range(NB):
        inverse.append(1.0 / form[k, k])
        for i in range(k + 1, NB):
            factor = form[k, i] * inverse[k]
            rhs[i] = rhs[i] - factor * rhs[k]
            for j in range(i, NB):
                form[i, j] = form[i, j] - factor * form[k, j]
    x = [None] * NB
    for k in reversed(range(NB)):
        value = rhs[k]
        for j in range(k + 1, NB):
            value = value - form[k, j] * x[j]
        x[k] = value * inverse[k]

    for k in range(NB):
        coef_ref[k] = x[k]
    lane = lax.broadcasted_iota(jnp.int32, (SUB, LANES), 1)
    weight = jnp.zeros((SUB, LANES), jnp.float32)
    for k in range(NB):
        weight = jnp.where((lane >= k * half) & (lane < (k + 1) * half), x[k], weight)
    grad = total * weight
    grad = grad + pltpu.roll(grad, LANES - 2 * half, 1)
    grad = -scale * (grad + pltpu.roll(grad, LANES - half, 1))
    low = jnp.where(lane < half, grad, 0.0)
    high = jnp.where((lane >= half) & (lane < 2 * half), pltpu.roll(grad, half, 1), 0.0)
    grad_ref[...] = jnp.where(even(axes[0]), low, high)[:1, :muscles]


def update_kernel(coef_ref, block_ref, fields, x_hbm, x_ref, sems):
    coef = [coef_ref[k] for k in range(NB)]
    copies = []
    for comp in range(3):
        for y in range(block_ref.shape[1]):
            for h in range(2):
                at = pl.ds(LANES * h, LANES)
                value = coef[0] * block_ref[3 + comp, y, :, at]
                for k in range(1, NB):
                    value = value + coef[k] * fields[(k - 1, comp, LOW + y, *part((0, h)))]
                x_ref[comp, y, :, at] = value
        copies.append(pltpu.make_async_copy(x_ref.at[comp], x_hbm.at[comp], sems.at[comp]))
        copies[-1].start()
    for copy in copies:
        copy.wait()


def swap(shard, axis, first):
    length = lax.axis_size(axis)
    pairs = [(i, i + 1) for i in range(first, length - 1, 2)]
    return lax.ppermute(shard, axis, pairs + [(j, i) for i, j in pairs])


def per_device(displacement, load, occupancy, voxel_muscle_group, activation):
    rows, cols, depth = occupancy.shape
    muscles = activation.shape[0]
    axes = ("gy", "gz")
    count = LOW + rows + HIGH

    def arr(*shape):
        return jax.ShapeDtypeStruct(shape, jnp.float32)

    anywhere = pl.BlockSpec(memory_space=pltpu.HBM)
    faces = (arr(CHANNELS, rows, HIGH, depth),) * 2
    edges = (arr(CHANNELS, HIGH, cols, depth),) * 2
    block, zpair, znext, ypair, ynext, group = pl.pallas_call(
        functools.partial(pack_kernel, axes),
        out_shape=(
            arr(CHANNELS, rows, cols, depth),
            *faces,
            *edges,
            jax.ShapeDtypeStruct(occupancy.shape, jnp.int32),
        ),
        in_specs=[anywhere] * 5,
        out_specs=(VMEM,) * 6,
        scratch_shapes=[
            pltpu.VMEM(displacement.shape, jnp.float32),
            pltpu.VMEM(load.shape, jnp.float32),
            pltpu.VMEM(occupancy.shape, jnp.int32),
            pltpu.SMEM((muscles,), jnp.float32),
            pltpu.SemaphoreType.DMA((5,)),
        ],
        compiler_params=pltpu.CompilerParams(vmem_limit_bytes=32 << 20),
        name="pack",
    )(
        *(
            pltpu.with_memory_space_constraint(value, pltpu.HBM)
            for value in (displacement, load, occupancy, voxel_muscle_group, activation)
        )
    )

    received = [
        swap(znext, "gz", 1),
        swap(zpair, "gz", 0),
        swap(ynext, "gy", 1),
        swap(ypair, "gy", 0),
    ]
    znext, zpair, ynext, ypair = received
    znext, zpair = lax.optimization_barrier((znext, zpair))
    around, cpair, cnext = pl.pallas_call(
        functools.partial(corner_kernel, axes),
        out_shape=(arr(CHANNELS, rows, 2 * HIGH, depth), *edges),
        in_specs=[VMEM] * 2,
        out_specs=(VMEM,) * 3,
        compiler_params=pltpu.CompilerParams(vmem_limit_bytes=32 << 20),
        name="corner",
    )(zpair, znext)
    cnext = swap(cnext, "gy", 1)
    cpair = swap(cpair, "gy", 0)

    state = (
        arr(CHANNELS, count, 2 * SUB, depth),
        arr(NB - 1, 3, count, 2 * SUB, depth),
        arr(TERMS, count - 1, 2 * SUB, depth),
        arr(NB, count - 1, SUB, depth),
    )
    *inner, partial = pl.pallas_call(
        functools.partial(inner_kernel, axes, muscles),
        out_shape=(*state, arr(NB - 1, 2, 9, 2 * SUB, depth), arr(2 * LANES, LANES)),
        in_specs=[VMEM] * 3,
        out_specs=(VMEM,) * 6,
        compiler_params=pltpu.CompilerParams(vmem_limit_bytes=32 << 20),
        name="inner",
    )(block, around, group)

    devices = lax.axis_size("gy") * lax.axis_size("gz")
    sums, _, fields, _, _ = pl.pallas_call(
        functools.partial(outer_kernel, axes, muscles, lax.axis_size("gz")),
        out_shape=(arr(devices, LANES), *state),
        in_specs=[VMEM] * 11,
        out_specs=(VMEM,) * 5,
        scratch_shapes=[pltpu.VMEM((2 * LANES, LANES), jnp.float32)],
        input_output_aliases={6: 1, 7: 2, 8: 3, 9: 4},
        compiler_params=pltpu.CompilerParams(vmem_limit_bytes=32 << 20),
        name="outer",
    )(group, partial, ynext, ypair, cnext, cpair, *inner)

    every = lax.all_to_all(sums, ("gy", "gz"), 0, 0, tiled=True)

    cells = depth * rows * lax.axis_size("gy") * cols * lax.axis_size("gz")
    scale = 1.0 / math.sqrt(cells / muscles)
    coef, mine = pl.pallas_call(
        functools.partial(solve_kernel, axes, muscles, scale),
        out_shape=(arr(NB, SUB, LANES), arr(1, muscles)),
        in_specs=[VMEM],
        out_specs=(VMEM, VMEM),
        compiler_params=pltpu.CompilerParams(vmem_limit_bytes=32 << 20),
        name="solve",
    )(every)
    others = swap(mine, "gy", 0)
    adjoint = pl.pallas_call(
        update_kernel,
        out_shape=arr(*load.shape),
        in_specs=[VMEM] * 3,
        out_specs=anywhere,
        scratch_shapes=[pltpu.VMEM(load.shape, jnp.float32), pltpu.SemaphoreType.DMA((3,))],
        compiler_params=pltpu.CompilerParams(vmem_limit_bytes=32 << 20),
        name="update",
    )(coef, block, fields)
    return adjoint, (mine + others).reshape(muscles)


def solution(mesh):
    placed = (
        P(None, "gy", "gz", None),
        P(None, "gy", "gz", None),
        P("gy", "gz", None),
        P("gy", "gz", None),
        P(),
    )
    return jax.shard_map(
        per_device,
        mesh=mesh,
        in_specs=placed,
        out_specs=(P(None, "gy", "gz", None), P()),
        check_vma=False,
    )
```

```python
import functools
import math

import jax
import jax.numpy as jnp
from jax import lax
from jax.experimental import pallas as pl
from jax.experimental.pallas import tpu as pltpu
from jax.sharding import PartitionSpec as P

SHEAR = 1.0
LAME = 4.0
MASS = 0.05

LOW, HIGH = 3, 4
SIGMA = 16.0
SHIFTS = (0.0, 9.95, 1.95)
NB = 4
LANES = 128
SUB = 8
CHANNELS = 8
TERMS = 15
ALL = tuple((zt, h) for zt in range(2) for h in range(2))
OWN = ((0, 0), (0, 1))
VMEM = pl.BlockSpec(memory_space=pltpu.VMEM)


class Shifts:
    def __init__(self):
        lane = lax.broadcasted_iota(jnp.int32, (SUB, LANES), 1)
        self.sub = lax.broadcasted_iota(jnp.int32, (SUB, LANES), 0)
        self.last_lane = lane == LANES - 1
        self.first_lane = lane == 0
        self.last_sub = self.sub == SUB - 1
        self.first_sub = self.sub == 0

    def xup(self, v):
        out = {}
        for zt in {zt for zt, _ in v}:
            r0 = pltpu.roll(v[zt, 0], LANES - 1, 1)
            r1 = pltpu.roll(v[zt, 1], LANES - 1, 1)
            out[zt, 0] = jnp.where(self.last_lane, r1, r0)
            out[zt, 1] = jnp.where(self.last_lane, 0.0, r1)
        return out

    def xdown(self, v):
        out = {}
        for zt in {zt for zt, _ in v}:
            r0 = pltpu.roll(v[zt, 0], 1, 1)
            r1 = pltpu.roll(v[zt, 1], 1, 1)
            out[zt, 0] = jnp.where(self.first_lane, 0.0, r0)
            out[zt, 1] = jnp.where(self.first_lane, r0, r1)
        return out

    def zup(self, v, keys):
        out = {}
        for h in range(2):
            r0 = pltpu.roll(v[0, h], SUB - 1, 0)
            r1 = pltpu.roll(v[1, h], SUB - 1, 0)
            out[0, h] = jnp.where(self.last_sub, r1, r0)
            if (1, h) in keys:
                out[1, h] = jnp.where(self.last_sub, r0, r1)
        return out

    def zdown(self, v):
        out = {}
        for h in range(2):
            r0 = pltpu.roll(v[0, h], 1, 0)
            r1 = pltpu.roll(v[1, h], 1, 0)
            out[0, h] = jnp.where(self.first_sub, r1, r0)
            out[1, h] = jnp.where(self.first_sub, r0, r1)
        return out


def part(k):
    return pl.ds(SUB * k[0], SUB), pl.ds(LANES * k[1], LANES)


def get(ref, *index):
    return {k: ref[(*index, *part(k))] for k in ALL}


def put(ref, value, *index):
    for k in value:
        ref[(*index, *part(k))] = value[k]


def add(a, b):
    return {k: a[k] + b[k] for k in a}


def sub(a, b):
    return {k: a[k] - b[k] for k in a}


def raw_gradient(sh, read, q, keys=ALL, cache=None):
    def level(comp, at):
        if cache is not None and (comp, at) in cache:
            return cache[comp, at]
        value = read(comp, at)
        value_x = sh.xup(value)
        wide, slope = add(value, value_x), sub(value_x, value)
        wide_z, slope_z = sh.zup(wide, keys), sh.zup(slope, keys)
        out = (
            {k: slope[k] + slope_z[k] for k in keys},
            {k: wide[k] + wide_z[k] for k in keys},
            {k: wide_z[k] - wide[k] for k in keys},
        )
        if cache is not None:
            cache[comp, at] = out
        return out

    result = []
    for comp in range(3):
        here, above = level(comp, q), level(comp, q + 1)
        result.append((add(here[0], above[0]), sub(above[1], here[1]), add(here[2], above[2])))
    return result


def row_terms(sh, ext, terms, q, cache):
    grad = raw_gradient(sh, lambda comp, at: get(ext, comp, at), q, ALL, cache)
    for k in ALL:
        occ, level = ext[(6, q, *part(k))], ext[(7, q, *part(k))]
        deform = [
            [0.25 * grad[r][c][k] + (1.0 if r == c else 0.0) for c in range(3)] for r in range(3)
        ]
        cof = [
            [
                deform[(r + 1) % 3][(c + 1) % 3] * deform[(r + 2) % 3][(c + 2) % 3]
                - deform[(r + 1) % 3][(c + 2) % 3] * deform[(r + 2) % 3][(c + 1) % 3]
                for c in range(3)
            ]
            for r in range(3)
        ]
        volume = deform[0][0] * cof[0][0] + deform[0][1] * cof[0][1] + deform[0][2] * cof[0][2]
        inverse = 1.0 / volume
        scaled = occ * (1.0 / (16.0 * SIGMA))
        values = [cof[r][c] * inverse for r in range(3) for c in range(3)]
        values.append(scaled * (SHEAR - LAME * jnp.log(volume)))
        values.append(scaled)
        values.append(scaled * (SHEAR + level))
        quarter = 0.25 * occ
        values += [quarter * deform[r][0] for r in range(3)]
        for i, value in enumerate(values):
            terms[(i, q, *part(k))] = value


def row_rate(grad, terms, works, step, q, keys=ALL):
    rate = [[{} for _ in range(3)] for _ in range(3)]
    for k in keys:

        def term(i):
            return terms[(i, q, *part(k))]

        g = [[grad[r][c][k] for c in range(3)] for r in range(3)]
        inv_t = [[term(3 * r + c) for c in range(3)] for r in range(3)]
        shear, occ, fibre = term(9), term(10), term(11)
        pulled = [
            [
                inv_t[0][a] * g[0][b] + inv_t[1][a] * g[1][b] + inv_t[2][a] * g[2][b]
                for b in range(3)
            ]
            for a in range(3)
        ]
        spread = (LAME * occ) * (pulled[0][0] + pulled[1][1] + pulled[2][2])
        z = [
            [shear * pulled[c][m] + spread if c == m else shear * pulled[c][m] for c in range(3)]
            for m in range(3)
        ]
        for r in range(3):
            for c in range(3):
                rate[r][c][k] = (
                    (fibre if c == 0 else occ) * g[r][c]
                    + inv_t[r][0] * z[0][c]
                    + inv_t[r][1] * z[1][c]
                    + inv_t[r][2] * z[2][c]
                )
        if k in OWN:
            works[(step, q, *part(k))] = (
                term(12) * g[0][0] + term(13) * g[1][0] + term(14) * g[2][0]
            )
    return rate


def row_force(sh, before, rate, comp):
    p = add(before[comp][0], rate[comp][0])
    a = sub(before[comp][1], rate[comp][1])
    b = add(before[comp][2], rate[comp][2])
    along = add(p, sh.zdown(p))
    across = add(sh.zdown(add(a, b)), sub(a, b))
    return add(sh.xdown(add(along, across)), sub(across, along))


def load_rate(ref, *index):
    return [[get(ref, *index, 3 * r + c) for c in range(3)] for r in range(3)]


def save_rate(ref, rate, *index):
    for r in range(3):
        for c in range(3):
            put(ref, rate[r][c], *index, 3 * r + c)


class Sweep:
    def __init__(self, axes, rows, ext, fields, terms, works):
        self.sh = Shifts()
        self.ext, self.fields, self.terms, self.works = ext, fields, terms, works
        ends = [lax.axis_index(axis) == lax.axis_size(axis) - 1 for axis in axes]
        self.top = LOW + rows
        self.cache = {i: {} for i in range(-1, NB)}
        self.keep_y = jnp.where(ends[0], 0.0, 1.0)
        top_z = jnp.where(ends[1], SUB, -1)
        self.keep_z = {k: jnp.where(self.sh.sub + SUB * k[0] == top_z, 0.0, 1.0) for k in ALL}

    def read(self, step):
        if step == 0:
            return lambda comp, q: get(self.ext, 3 + comp, q)
        return lambda comp, q: get(self.fields, step - 1, comp, q)

    def rate(self, step, q):
        if step == 0:
            row_terms(self.sh, self.ext, self.terms, q, self.cache[-1])
        grad = raw_gradient(self.sh, self.read(step), q, ALL, self.cache[step])
        return row_rate(grad, self.terms, self.works, step, q)

    def node(self, step, q, before, rate):
        for comp in range(3):
            force = row_force(self.sh, before, rate, comp)
            if SHIFTS[step] != 0.0:
                here = self.read(step)(comp, q)
                force = {k: force[k] - (SHIFTS[step] / SIGMA) * here[k] for k in ALL}
            if q == self.top:
                force = {k: force[k] * self.keep_y for k in ALL}
            force = {k: force[k] * self.keep_z[k] if k[0] else force[k] for k in ALL}
            put(self.fields, force, step, comp, q)

    def rows(self, step, start, stop, before):
        for q in range(start, stop):
            rate = self.rate(step, q)
            self.node(step, q, before, rate)
            before = rate
        return before


def even(axis):
    return lax.rem(lax.axis_index(axis), 2) == 0


def pack_kernel(
    axes,
    disp_hbm,
    load_hbm,
    occ_hbm,
    group_hbm,
    act_hbm,
    block_ref,
    zpair_ref,
    znext_ref,
    ypair_ref,
    ynext_ref,
    group_ref,
    disp_ref,
    load_ref,
    occ_ref,
    act_ref,
    sems,
):
    copies = [
        pltpu.make_async_copy(source, target, sems.at[i])
        for i, (source, target) in enumerate(
            (
                (act_hbm, act_ref),
                (group_hbm, group_ref),
                (occ_hbm, occ_ref),
                (disp_hbm, disp_ref),
                (load_hbm, load_ref),
            )
        )
    ]
    for copy in copies:
        copy.start()
    rows, cols, depth = occ_ref.shape
    muscles = act_ref.shape[0]
    even_y, even_z = even(axes[0]), even(axes[1])
    for copy in copies[:2]:
        copy.wait()
    for y in range(rows):
        group = group_ref[y]
        level = jnp.zeros((cols, depth), jnp.float32)
        for m in range(muscles):
            level = jnp.where(group == m, act_ref[m], level)
        block_ref[CHANNELS - 1, y] = level
    for copy in copies[2:]:
        copy.wait()
    for y in range(rows):
        values = [disp_ref[c, y] for c in range(3)] + [load_ref[c, y] for c in range(3)]
        values.append(occ_ref[y].astype(jnp.float32))
        for c, value in enumerate(values):
            block_ref[c, y] = value
        values.append(block_ref[CHANNELS - 1, y])
        for c, value in enumerate(values):
            bottom, top = value[:HIGH], value[cols - HIGH :]
            zpair_ref[c, y] = jnp.where(even_z, top, bottom)
            znext_ref[c, y] = jnp.where(even_z, bottom, top)
    send_rows(block_ref, ypair_ref, ynext_ref, even_y)


def send_rows(block_ref, pair_ref, next_ref, is_even):
    rows = block_ref.shape[1]
    pair_at = jnp.where(is_even, rows - HIGH, 0)

    def channel(c, carry):
        for y in range(HIGH):
            pair_ref[c, y] = block_ref[c, pair_at + y]
            next_ref[c, y] = block_ref[c, rows - HIGH - pair_at + y]
        return carry

    lax.fori_loop(0, CHANNELS, channel, 0, unroll=4)


def corner_kernel(axes, zpair_ref, znext_ref, around_ref, ypair_ref, ynext_ref):
    even_y, even_z = even(axes[0]), even(axes[1])

    def channel(c, carry):
        for y in range(around_ref.shape[1]):
            pair, far = zpair_ref[c, y], znext_ref[c, y]
            around_ref[c, y, pl.ds(0, HIGH), :] = jnp.where(even_z, pair, far)
            around_ref[c, y, pl.ds(HIGH, HIGH), :] = jnp.where(even_z, far, pair)
        return carry

    lax.fori_loop(0, CHANNELS, channel, 0, unroll=4)
    send_rows(around_ref, ypair_ref, ynext_ref, even_y)


def table_row(step, m, muscles):
    half = muscles // 2
    return half * step + m + (LANES - half) * lax.div(m, half)


def muscle_sums(group_ref, works, muscles, spans, store):
    zero = jnp.zeros((SUB, LANES), jnp.float32)

    def muscle(m, carry):
        total = [zero for _ in spans]
        for q in sorted({q for span in spans for q in span}):
            for h in range(2):
                mine = group_ref[q - LOW, :, pl.ds(LANES * h, LANES)] == m
                for step, span in enumerate(spans):
                    if q in span:
                        work = works[(step, q, *part((0, h)))]
                        total[step] = total[step] + jnp.where(mine, work, 0.0)
        for step in range(len(spans)):
            store(step, table_row(step, m, muscles), jnp.sum(total[step], axis=0, keepdims=True))
        return carry

    lax.fori_loop(0, muscles, muscle, 0, unroll=32)


def inner_kernel(
    axes, muscles, block_ref, around_ref, group_ref, ext, fields, terms, works, edge, partial
):
    rows = block_ref.shape[1]

    def assemble(c, carry):
        for y in range(rows):
            ext[c, LOW + y, pl.ds(0, SUB), :] = block_ref[c, y]
            ext[c, LOW + y, pl.ds(SUB, SUB), :] = around_ref[c, y]
        return carry

    lax.fori_loop(0, CHANNELS, assemble, 0, unroll=8)
    sweep = Sweep(axes, rows, ext, fields, terms, works)
    for step in range(NB - 1):
        first, final = LOW + step, LOW + rows - 2 - step
        rate = sweep.rate(step, first)
        save_rate(edge, rate, step, 0)
        save_rate(edge, sweep.rows(step, first + 1, final + 1, rate), step, 1)

    def store(step, at, value):
        partial[pl.ds(at, 1), :] = value

    spans = [range(LOW + step, LOW + rows - 1 - step) for step in range(NB - 1)]
    muscle_sums(group_ref, works, muscles, spans, store)


def outer_kernel(
    axes,
    muscles,
    group_size,
    group_ref,
    partial,
    ynext_ref,
    ypair_ref,
    cnext_ref,
    cpair_ref,
    ext_in,
    fields_in,
    terms_in,
    works_in,
    edge,
    sums_ref,
    ext,
    fields,
    terms,
    works,
    table,
):
    del ext_in, fields_in, terms_in, works_in
    rows = group_ref.shape[0]
    even_y = even(axes[0])

    def assemble(c, carry):
        for zt, pair_ref, next_ref in ((0, ypair_ref, ynext_ref), (1, cpair_ref, cnext_ref)):
            for y in range(HIGH):
                pair, far = pair_ref[c, y], next_ref[c, y]
                ext[c, LOW + rows + y, pl.ds(SUB * zt, SUB), :] = jnp.where(even_y, pair, far)
                if y >= HIGH - LOW:
                    ext[c, y - HIGH + LOW, pl.ds(SUB * zt, SUB), :] = jnp.where(even_y, far, pair)
        return carry

    lax.fori_loop(0, CHANNELS, assemble, 0, unroll=8)
    sweep = Sweep(axes, rows, ext, fields, terms, works)
    for step in range(NB - 1):
        low = sweep.rows(step, step + 1, LOW + step, sweep.rate(step, step))
        sweep.node(step, LOW + step, low, load_rate(edge, step, 0))
        final = LOW + rows - 2 - step
        sweep.rows(step, final + 1, final + 1 + HIGH, load_rate(edge, step, 1))

    zero = jnp.zeros((SUB, LANES), jnp.float32)
    pairs = [(i, j) for i in range(NB) for j in range(i, NB)]

    def finish(q, acc):
        acc = list(acc)
        grad = raw_gradient(sweep.sh, sweep.read(NB - 1), q, OWN, sweep.cache[NB - 1])
        rate = row_rate(grad, terms, works, NB - 1, q, OWN)
        for k in OWN:
            for r in range(3):
                for c in range(3):
                    acc[-1] = acc[-1] + rate[r][c][k] * grad[r][c][k]
            for comp in range(3):
                vectors = [ext[(3 + comp, q, *part(k))]]
                vectors += [fields[(s, comp, q, *part(k))] for s in range(NB - 1)]
                for n, (i, j) in enumerate(pairs):
                    acc[n] = acc[n] + vectors[i] * vectors[j]
        return tuple(acc)

    acc = tuple(zero for _ in range(len(pairs) + 1))
    for q in range(LOW, LOW + rows):
        acc = finish(q, acc)
    table[...] = jnp.zeros_like(table)
    for n, value in enumerate(acc):
        total = jnp.sum(value, axis=0, keepdims=True)
        for core in range(2):
            table[pl.ds(LANES * core + NB * (muscles // 2) + n, 1), :] = total

    def store(step, at, value):
        if step < NB - 1:
            value = value + partial[pl.ds(at, 1), :]
        table[pl.ds(at, 1), :] = value

    own = range(LOW, LOW + rows)
    spans = [
        [q for q in own if not LOW + step <= q < LOW + rows - 1 - step or step == NB - 1]
        for step in range(NB)
    ]
    muscle_sums(group_ref, works, muscles, spans, store)
    row = lax.dot_general(
        jnp.ones((SUB, LANES), jnp.float32),
        table[...],
        (((1,), (1,)), ((), ())),
        precision=lax.Precision.HIGHEST,
        preferred_element_type=jnp.float32,
    )
    for i in range(sums_ref.shape[0] // SUB):
        core = i // (group_size // SUB) % 2
        sums_ref[pl.ds(SUB * i, SUB), :] = row[:, LANES * core : LANES * (core + 1)]


def solve_kernel(axes, muscles, scale, sums_ref, coef_ref, grad_ref):
    parts = [sums_ref[pl.ds(SUB * i, SUB), :] for i in range(sums_ref.shape[0] // SUB)]
    while len(parts) > 1:
        odd = parts[len(parts) // 2 * 2 :]
        parts = [a + b for a, b in zip(parts[0::2], parts[1::2])] + odd
    total = parts[0]
    total = jnp.broadcast_to(jnp.sum(total, axis=0, keepdims=True), (SUB, LANES))
    half = muscles // 2

    def everywhere(lane):
        return jnp.broadcast_to(total[:, lane : lane + 1], (SUB, LANES))

    pairs = [(i, j) for i in range(NB) for j in range(i, NB)]
    gram = {}
    for n, (i, j) in enumerate(pairs):
        gram[i, j] = gram[j, i] = everywhere(NB * half + n)
    energy = everywhere(NB * half + len(pairs))
    shifts = [MASS + s for s in SHIFTS]
    form = {}
    for j in range(NB - 1):
        for i in range(j + 1):
            form[i, j] = form[j, i] = SIGMA * gram[i, j + 1] + shifts[j] * gram[i, j]
    last = NB - 1
    for i in range(last):
        form[i, last] = form[last, i] = SIGMA * gram[i + 1, last] + shifts[i] * gram[i, last]
    form[last, last] = SIGMA * energy + MASS * gram[last, last]

    rhs = [gram[0, i] for i in range(NB)]
    inverse = []
    for k in range(NB):
        inverse.append(1.0 / form[k, k])
        for i in range(k + 1, NB):
            factor = form[k, i] * inverse[k]
            rhs[i] = rhs[i] - factor * rhs[k]
            for j in range(i, NB):
                form[i, j] = form[i, j] - factor * form[k, j]
    x = [None] * NB
    for k in reversed(range(NB)):
        value = rhs[k]
        for j in range(k + 1, NB):
            value = value - form[k, j] * x[j]
        x[k] = value * inverse[k]

    for k in range(NB):
        coef_ref[k] = x[k]
    lane = lax.broadcasted_iota(jnp.int32, (SUB, LANES), 1)
    weight = jnp.zeros((SUB, LANES), jnp.float32)
    for k in range(NB):
        weight = jnp.where((lane >= k * half) & (lane < (k + 1) * half), x[k], weight)
    grad = total * weight
    grad = grad + pltpu.roll(grad, LANES - 2 * half, 1)
    grad = -scale * (grad + pltpu.roll(grad, LANES - half, 1))
    low = jnp.where(lane < half, grad, 0.0)
    high = jnp.where((lane >= half) & (lane < 2 * half), pltpu.roll(grad, half, 1), 0.0)
    grad_ref[...] = jnp.where(even(axes[0]), low, high)[:1, :muscles]


def update_kernel(coef_ref, block_ref, fields, x_hbm, x_ref, sems):
    coef = [coef_ref[k] for k in range(NB)]
    copies = []
    for comp in range(3):
        for y in range(block_ref.shape[1]):
            for h in range(2):
                at = pl.ds(LANES * h, LANES)
                value = coef[0] * block_ref[3 + comp, y, :, at]
                for k in range(1, NB):
                    value = value + coef[k] * fields[(k - 1, comp, LOW + y, *part((0, h)))]
                x_ref[comp, y, :, at] = value
        copies.append(pltpu.make_async_copy(x_ref.at[comp], x_hbm.at[comp], sems.at[comp]))
        copies[-1].start()
    for copy in copies:
        copy.wait()


def swap(shard, axis, first):
    length = lax.axis_size(axis)
    pairs = [(i, i + 1) for i in range(first, length - 1, 2)]
    return lax.ppermute(shard, axis, pairs + [(j, i) for i, j in pairs])


def per_device(displacement, load, occupancy, voxel_muscle_group, activation):
    rows, cols, depth = occupancy.shape
    muscles = activation.shape[0]
    axes = ("gy", "gz")
    count = LOW + rows + HIGH

    def arr(*shape):
        return jax.ShapeDtypeStruct(shape, jnp.float32)

    anywhere = pl.BlockSpec(memory_space=pltpu.HBM)
    faces = (arr(CHANNELS, rows, HIGH, depth),) * 2
    edges = (arr(CHANNELS, HIGH, cols, depth),) * 2
    block, zpair, znext, ypair, ynext, group = pl.pallas_call(
        functools.partial(pack_kernel, axes),
        out_shape=(
            arr(CHANNELS, rows, cols, depth),
            *faces,
            *edges,
            jax.ShapeDtypeStruct(occupancy.shape, jnp.int32),
        ),
        in_specs=[anywhere] * 5,
        out_specs=(VMEM,) * 6,
        scratch_shapes=[
            pltpu.VMEM(displacement.shape, jnp.float32),
            pltpu.VMEM(load.shape, jnp.float32),
            pltpu.VMEM(occupancy.shape, jnp.int32),
            pltpu.SMEM((muscles,), jnp.float32),
            pltpu.SemaphoreType.DMA((5,)),
        ],
        compiler_params=pltpu.CompilerParams(vmem_limit_bytes=32 << 20),
        name="pack",
    )(
        *(
            pltpu.with_memory_space_constraint(value, pltpu.HBM)
            for value in (displacement, load, occupancy, voxel_muscle_group, activation)
        )
    )

    received = [
        swap(znext, "gz", 1),
        swap(zpair, "gz", 0),
        swap(ynext, "gy", 1),
        swap(ypair, "gy", 0),
    ]
    znext, zpair, ynext, ypair = received
    znext, zpair = lax.optimization_barrier((znext, zpair))
    around, cpair, cnext = pl.pallas_call(
        functools.partial(corner_kernel, axes),
        out_shape=(arr(CHANNELS, rows, 2 * HIGH, depth), *edges),
        in_specs=[VMEM] * 2,
        out_specs=(VMEM,) * 3,
        compiler_params=pltpu.CompilerParams(vmem_limit_bytes=32 << 20),
        name="corner",
    )(zpair, znext)
    cnext = swap(cnext, "gy", 1)
    cpair = swap(cpair, "gy", 0)

    state = (
        arr(CHANNELS, count, 2 * SUB, depth),
        arr(NB - 1, 3, count, 2 * SUB, depth),
        arr(TERMS, count - 1, 2 * SUB, depth),
        arr(NB, count - 1, SUB, depth),
    )
    *inner, partial = pl.pallas_call(
        functools.partial(inner_kernel, axes, muscles),
        out_shape=(*state, arr(NB - 1, 2, 9, 2 * SUB, depth), arr(2 * LANES, LANES)),
        in_specs=[VMEM] * 3,
        out_specs=(VMEM,) * 6,
        compiler_params=pltpu.CompilerParams(vmem_limit_bytes=32 << 20),
        name="inner",
    )(block, around, group)

    devices = lax.axis_size("gy") * lax.axis_size("gz")
    sums, _, fields, _, _ = pl.pallas_call(
        functools.partial(outer_kernel, axes, muscles, lax.axis_size("gz")),
        out_shape=(arr(devices, LANES), *state),
        in_specs=[VMEM] * 11,
        out_specs=(VMEM,) * 5,
        scratch_shapes=[pltpu.VMEM((2 * LANES, LANES), jnp.float32)],
        input_output_aliases={6: 1, 7: 2, 8: 3, 9: 4},
        compiler_params=pltpu.CompilerParams(vmem_limit_bytes=32 << 20),
        name="outer",
    )(group, partial, ynext, ypair, cnext, cpair, *inner)

    every = lax.all_to_all(sums, ("gy", "gz"), 0, 0, tiled=True)

    cells = depth * rows * lax.axis_size("gy") * cols * lax.axis_size("gz")
    scale = 1.0 / math.sqrt(cells / muscles)
    coef, mine = pl.pallas_call(
        functools.partial(solve_kernel, axes, muscles, scale),
        out_shape=(arr(NB, SUB, LANES), arr(1, muscles)),
        in_specs=[VMEM],
        out_specs=(VMEM, VMEM),
        compiler_params=pltpu.CompilerParams(vmem_limit_bytes=32 << 20),
        name="solve",
    )(every)
    others = swap(mine, "gy", 0)
    adjoint = pl.pallas_call(
        update_kernel,
        out_shape=arr(*load.shape),
        in_specs=[VMEM] * 3,
        out_specs=anywhere,
        scratch_shapes=[pltpu.VMEM(load.shape, jnp.float32), pltpu.SemaphoreType.DMA((3,))],
        compiler_params=pltpu.CompilerParams(vmem_limit_bytes=32 << 20),
        name="update",
    )(coef, block, fields)
    return adjoint, (mine + others).reshape(muscles)


def solution(mesh):
    placed = (
        P(None, "gy", "gz", None),
        P(None, "gy", "gz", None),
        P("gy", "gz", None),
        P("gy", "gz", None),
        P(),
    )
    return jax.shard_map(
        per_device,
        mesh=mesh,
        in_specs=placed,
        out_specs=(P(None, "gy", "gz", None), P()),
        check_vma=False,
    )
```
